256 devices in a mesh: px: 16 (over z, core), py: 16 (over x, y).
Axes of the slice: x: 4, y: 4, z: 8, core: 2. Of those that a mesh axis runs over, the one named last changes fastest.
Arguments:
- right_side: float32 [64, 128, 1024], P('px', 'py'), may hold values from -40 to 40
- diagonal: float32 [64, 128, 1024], P('px', 'py'), may hold values from 0.05 to 3
- aggregate_id: int32 [64, 128, 1024], P('px', 'py'), may hold values from 0 to 511, as said below
- coarse_diag: float32 [32, 32, 128], P('px', 'py'), may hold values from 150 to 230
- coarse_link: float32 [3, 32, 32, 128], P(None, 'px', 'py'), may hold values from 0.75 to 1.25
Outputs:
- solution_field: float32 [64, 128, 1024], P('px', 'py')
- residual: float32 [64, 128, 1024], P('px', 'py')
The draws below stay inside these ranges and needn't reach their ends.
Inputs may be any that keep to these rules, and one draw needn't show every extreme that they name: `aggregate_id`: the cell (x, y, z) names the aggregate ((x % 4) // 2) * 2 * 128 + ((y % 8) // 4) * 128 + k of its own partition, where k differs from z // 8 by at most one; every aggregate of every partition holds cells.
All inputs are finite; a program needn't handle non-finite values.
Results may differ from the reference program's by a relative error of at most 0.0003.
Values sent between devices are 32-bit elements; how exact they have to be, the bound alone decides.
No kernel may reach another device: no remote copies, remote signals or barrier semaphores. Data moves between devices by JAX's collectives and lax.ppermute only.
A program may use at most 64 MiB of HBM per device.

```python
import math
import jax
import jax.numpy as jnp

CX = 4
CY = 8
ITERS = 4
CXA = 2
CYA = 2
CZA = 128
AGG = 512
PGX = 16
PGY = 16
NX = 64
NY = 128
NZ = 1024
NXA = 32
NYA = 32
NZA = 128


def draw_right_side(key, part):
    along_x = jnp.arange(NX, dtype=jnp.float32) / max(NX - 1, 1)
    along_y = jnp.arange(NY, dtype=jnp.float32) / max(NY - 1, 1)
    ramp = 0.25 * jnp.exp(math.log(10.0) * along_x)[:, None, None] * jnp.exp(math.log(3.0) * along_y)[None, :, None]
    values = ramp * jnp.clip(jax.random.normal(key, (NX, NY, NZ), jnp.float32), -5.0, 5.0)
    return values


def draw_aggregate_id(key, part):
    jitter = jax.random.randint(key, (NX, NY, NZ), -2, 3)
    across_x = jnp.arange(NX, dtype=jnp.int32) % CX // 2
    across_y = jnp.arange(NY, dtype=jnp.int32) % CY // 4
    depth = jnp.clip(jnp.arange(NZ, dtype=jnp.int32)[None, None, :] + jitter, 0, NZ - 1) // 8
    labels = across_x[:, None, None] * (CYA * CZA) + across_y[None, :, None] * CZA + depth
    return labels.astype(jnp.int32)


def steps_of(own_key, dims, split, least, largest):
    def one(position, blocks):
        steps = jax.random.uniform(jax.random.fold_in(jax.random.fold_in(own_key, 6), position), (blocks,), jnp.float32, least / len(split), largest / len(split))
        return jnp.repeat(jnp.exp(steps), dims[position] // blocks).reshape((-1,) + (1,) * (len(dims) - position - 1))

    loudness = one(*split[0])
    for cut in split[1:]:
        loudness = loudness * one(*cut)
    return loudness


def setup_inputs(seed: int = 0) -> dict:
    streams_of = jax.random.split(jax.random.key(seed), 6)
    right_side = draw_right_side(jax.random.fold_in(streams_of[5], 71), 0)
    diagonal = jnp.clip(jnp.exp(math.log(3.0) - 4.0943445 * jax.random.uniform(streams_of[1], (NX, NY, NZ), jnp.float32) ** steps_of(streams_of[1], (NX, NY, NZ), ((0, 16), (1, 16)), -0.2, 0.2)), 0.05, 3.0)
    aggregate_id = draw_aggregate_id(jax.random.fold_in(streams_of[5], 71), 0)
    coarse_diag = jnp.clip(150.0 + 80.0 * jax.random.uniform(streams_of[3], (NXA, NYA, NZA), jnp.float32) ** steps_of(streams_of[3], (NXA, NYA, NZA), ((0, 16), (1, 16)), -0.2, 0.2), 150.0, 230.0)
    coarse_link = jnp.clip(0.75 + 0.5 * jax.random.uniform(streams_of[4], (3, NXA, NYA, NZA), jnp.float32) ** steps_of(streams_of[4], (3, NXA, NYA, NZA), ((1, 16), (2, 16)), -0.2, 0.2), 0.75, 1.25)
    return {"right_side": right_side, "diagonal": diagonal, "aggregate_id": aggregate_id, "coarse_diag": coarse_diag, "coarse_link": coarse_link}


OMEGA = 2.0 / 3.0
FACES = (32.0, 16.0, 8.0)


def stencil(values, diagonal):
    padded = jnp.pad(values, 1)
    beside = padded[2:, 1:-1, 1:-1] + padded[:-2, 1:-1, 1:-1]
    beside = beside + padded[1:-1, 2:, 1:-1] + padded[1:-1, :-2, 1:-1]
    beside = beside + padded[1:-1, 1:-1, 2:] + padded[1:-1, 1:-1, :-2]
    return (6.0 + diagonal) * values - beside


def to_blocks(array):
    shaped = array.reshape(PGX, CX, PGY, CY, NZ).transpose(0, 2, 1, 3, 4)
    return shaped.reshape(PGX * PGY, CX * CY * NZ)


def from_blocks(blocks):
    shaped = blocks.reshape(PGX, PGY, CX, CY, NZ).transpose(0, 2, 1, 3, 4)
    return shaped.reshape(PGX * CX, PGY * CY, NZ)


def restrict(values, id_blocks):
    def one_block(piece, labels):
        return jax.ops.segment_sum(piece, labels, num_segments=AGG)
    sums = jax.vmap(one_block)(to_blocks(values), id_blocks)
    shaped = sums.reshape(PGX, PGY, CXA, CYA, CZA).transpose(0, 2, 1, 3, 4)
    return shaped.reshape(NXA, NYA, NZA)


def lift(coarse, id_blocks):
    table = coarse.reshape(PGX, CXA, PGY, CYA, CZA).transpose(0, 2, 1, 3, 4).reshape(PGX * PGY, AGG)
    return from_blocks(jnp.take_along_axis(table, id_blocks, axis=1))


def coarse_apply(coarse, coarse_diag, weights):
    padded = jnp.pad(coarse, 1)
    padded_w = jnp.pad(weights * coarse[None], ((0, 0), (1, 1), (1, 1), (1, 1)))
    near = weights[0] * padded[2:, 1:-1, 1:-1] + padded_w[0, :-2, 1:-1, 1:-1]
    near = near + weights[1] * padded[1:-1, 2:, 1:-1] + padded_w[1, 1:-1, :-2, 1:-1]
    near = near + weights[2] * padded[1:-1, 1:-1, 2:] + padded_w[2, 1:-1, 1:-1, :-2]
    return coarse_diag * coarse - near


def precondition(vector, diagonal, id_blocks, coarse_diag, weights):
    scaling = 6.0 + diagonal
    smoothed = OMEGA * vector / scaling
    remainder = vector - stencil(smoothed, diagonal)
    reduced = remainder - OMEGA * stencil(remainder / scaling, diagonal)
    coarse_rhs = restrict(reduced, id_blocks)
    estimate = coarse_rhs / coarse_diag
    for sweep_index in range(2):
        estimate = estimate + (coarse_rhs - coarse_apply(estimate, coarse_diag, weights)) / coarse_diag
    lifted = lift(estimate, id_blocks)
    spread = lifted - OMEGA * stencil(lifted, diagonal) / scaling
    leftover = remainder - stencil(spread, diagonal)
    return smoothed + spread + OMEGA * leftover / scaling


def reference(right_side, diagonal, aggregate_id, coarse_diag, coarse_link):
    id_blocks = to_blocks(aggregate_id).astype(jnp.int32)
    faces = jnp.array(FACES, dtype=jnp.float32)
    weights = coarse_link * faces[:, None, None, None]
    solution = jnp.zeros_like(right_side)
    residual = right_side
    shaped = precondition(residual, diagonal, id_blocks, coarse_diag, weights)
    direction = shaped
    gamma_now = jnp.sum(residual * shaped)
    for iteration in range(ITERS):
        applied_dir = stencil(direction, diagonal)
        alpha_now = gamma_now / jnp.sum(direction * applied_dir)
        solution = solution + alpha_now * direction
        residual = residual - alpha_now * applied_dir
        if iteration + 1 < ITERS:
            shaped = precondition(residual, diagonal, id_blocks, coarse_diag, weights)
            fresh = jnp.sum(residual * shaped)
            direction = shaped + (fresh / gamma_now) * direction
            gamma_now = fresh
    return solution, residual
```

```python
import jax
import jax.numpy as jnp
from jax import lax
from jax.experimental import pallas as pl
from jax.experimental.pallas import tpu as pltpu
from jax.sharding import PartitionSpec as P

ITERS = 4
OMEGA = 2.0 / 3.0
REST = 1.0 - OMEGA
FACES = (32.0, 16.0, 8.0)
F32 = jnp.float32


def call(body, outs, *args, scalars=1, scratch=(), flops=2_000_000):
    smem = pl.BlockSpec(memory_space=pltpu.SMEM)
    vmem = pl.BlockSpec(memory_space=pltpu.VMEM)
    specs = [smem] * scalars + [vmem] * (len(args) - scalars)
    return pl.pallas_call(
        body,
        out_shape=[jax.ShapeDtypeStruct(shape, F32) for shape in outs],
        in_specs=specs,
        out_specs=[vmem] * len(outs),
        scratch_shapes=list(scratch),
        compiler_params=pltpu.CompilerParams(vmem_limit_bytes=20 * 1024 * 1024),
        cost_estimate=pl.CostEstimate(flops=flops, bytes_accessed=1_000_000, transcendentals=0),
    )(*args)


def along_z(value):
    lane = lax.broadcasted_iota(jnp.int32, value.shape, value.ndim - 1)
    sub = lax.broadcasted_iota(jnp.int32, value.shape, value.ndim - 2)
    after = pltpu.roll(value, 127, value.ndim - 1)
    before = pltpu.roll(value, 1, value.ndim - 1)
    after_row = jnp.where(sub == 7, 0.0, pltpu.roll(after, 7, value.ndim - 2))
    before_row = jnp.where(sub == 0, 0.0, pltpu.roll(before, 1, value.ndim - 2))
    return jnp.where(lane == 127, after_row, after) + jnp.where(lane == 0, before_row, before)


def by_eight(value, ahead):
    lane = lax.broadcasted_iota(jnp.int32, value.shape, value.ndim - 1)
    if ahead:
        moved = pltpu.roll(value, 120, value.ndim - 1)
        return jnp.where(lane >= 120, pltpu.roll(moved, 7, value.ndim - 2), moved)
    moved = pltpu.roll(value, 8, value.ndim - 1)
    return jnp.where(lane < 8, pltpu.roll(moved, 1, value.ndim - 2), moved)


def beside(below, here, above):
    count = here.shape[0]
    inner = here[1 : count - 1]
    return below + above + here[0 : count - 2] + here[2:count] + along_z(inner)


def enter_body(b_ref, d_ref, a_ref, low_ref, high_ref, olow_ref, ohigh_ref):
    lane = lax.broadcasted_iota(jnp.int32, (8, 128), 1)
    for x in range(4):
        for s in range(8):
            part = slice(s * 128, (s + 1) * 128)
            b = b_ref[x, :, part]
            d = d_ref[x, :, part]
            home = (lane + s * 128) // 8
            o = ((a_ref[x, :, part] & 127) - home).astype(F32)
            ref = low_ref if x < 2 else high_ref
            at = (x % 2) * 64 + s
            ref[pl.ds(at, 8, stride=8), :] = b
            ref[pl.ds(128 + at, 8, stride=8), :] = d
            if x < 3:
                olow_ref[pl.ds(x * 64 + s, 8, stride=8), :] = o
            if x > 0:
                ohigh_ref[pl.ds((x - 1) * 64 + s, 8, stride=8), :] = o


def pack_first_body(low_ref, high_ref, xlow_ref, xhigh_ref, olow_ref, ohigh_ref, oxlow_ref, oxhigh_ref,
                    first_ref, last_ref, ofirst_ref, olast_ref):
    for f in range(2):
        for r, ref in enumerate((xlow_ref, low_ref, high_ref, xhigh_ref)):
            for k in range(2):
                first_ref[f, 2 * r + k] = ref[f, k, 0:2]
                last_ref[f, 2 * r + k] = ref[f, k, 6:8]
    rows = [oxlow_ref.at[0], oxlow_ref.at[1], oxlow_ref.at[2], olow_ref.at[0], olow_ref.at[1], olow_ref.at[2],
            ohigh_ref.at[2], oxhigh_ref.at[0], oxhigh_ref.at[1], oxhigh_ref.at[2]]
    for r, ref in enumerate(rows):
        ofirst_ref[r] = ref[0:3]
        olast_ref[r] = ref[5:8]


def setup_body(me_ref, low_ref, high_ref, xlow_ref, xhigh_ref, ylow_ref, yhigh_ref, olow_ref, ohigh_ref,
               oxlow_ref, oxhigh_ref, oylow_ref, oyhigh_ref, inverse_ref, scale_ref, offset_ref):
    px, py, last_x, last_y = me_ref[0], me_ref[1], me_ref[2], me_ref[3]
    below = jnp.where(px > 0, 1.0, 0.0).astype(F32)
    above = jnp.where(px < last_x, 1.0, 0.0).astype(F32)
    left = jnp.where(py > 0, 1.0, 0.0).astype(F32)
    right = jnp.where(py < last_y, 1.0, 0.0).astype(F32)
    for r, (ref, seen) in enumerate(((xlow_ref, below), (low_ref, None), (high_ref, None), (xhigh_ref, above))):
        for k in range(2):
            x = 2 * r + k
            s_mid = 6.0 + ref[1, k]
            s_left = 6.0 + ylow_ref[1, x]
            s_right = 6.0 + yhigh_ref[1, x]
            i_mid, i_left, i_right = 1.0 / s_mid, left / s_left, right / s_right
            if seen is not None:
                i_mid, i_left, i_right = i_mid * seen, i_left * seen, i_right * seen
            inverse_ref[x, 0:2] = i_left
            inverse_ref[x, 2:10] = i_mid
            inverse_ref[x, 10:12] = i_right
            if 1 <= x <= 6:
                scale_ref[x - 1, 0:1] = s_left[1:2]
                scale_ref[x - 1, 1:9] = s_mid
                scale_ref[x - 1, 9:10] = s_right[0:1]
    rows = [oxlow_ref.at[0], oxlow_ref.at[1], oxlow_ref.at[2], olow_ref.at[0], olow_ref.at[1], olow_ref.at[2],
            ohigh_ref.at[2], oxhigh_ref.at[0], oxhigh_ref.at[1], oxhigh_ref.at[2]]
    for r, ref in enumerate(rows):
        offset_ref[r, 0:3] = oylow_ref[r]
        offset_ref[r, 3:11] = ref[...]
        offset_ref[r, 11:14] = oyhigh_ref[r]


def pack_body(low_ref, high_ref, xlow_ref, xhigh_ref, first_ref, last_ref):
    for r, ref in enumerate((xlow_ref, low_ref, high_ref, xhigh_ref)):
        for k in range(2):
            first_ref[2 * r + k] = ref[k, 0:2]
            last_ref[2 * r + k] = ref[k, 6:8]


def restrict_body(first, *refs):
    if first:
        (low, high, xlow, xhigh, ylow, yhigh, inverse_ref, offset_ref, cdiag_ref, link_ref,
         smooth_ref, remain_ref, send_ref) = refs
        low, high, xlow, xhigh, ylow, yhigh = (r.at[0] for r in (low, high, xlow, xhigh, ylow, yhigh))
    else:
        (low, high, xlow, xhigh, ylow, yhigh, inverse_ref, offset_ref, dots_ref,
         smooth_ref, remain_ref, send_ref) = refs
    mids = [ref.at[k] for ref in (xlow, low, high, xhigh) for k in range(2)]

    def vector(x):
        return jnp.concatenate([ylow[x], mids[x][...], yhigh[x]], axis=0)

    smooth = [OMEGA * vector(x) * inverse_ref[x] for x in range(8)]
    shrunk = []
    remains = []
    for x in range(1, 7):
        near = beside(smooth[x - 1][1:11], smooth[x], smooth[x + 1][1:11])
        remain = REST * vector(x)[1:11] + near
        smooth_ref[x - 1] = smooth[x][1:11]
        remain_ref[x - 1] = remain
        remains.append(remain[1:9])
        shrunk.append(remain * inverse_ref[x, 1:11])
    sums = []
    for big_x in range(2):
        parts = []
        for x in (2 * big_x, 2 * big_x + 1):
            near = beside(shrunk[x][1:9], shrunk[x + 1], shrunk[x + 2][1:9])
            reduced = REST * remains[x + 1] + OMEGA * near
            offset = offset_ref[x + 3, 3:11]
            parts.append((
                jnp.where(jnp.abs(offset) < 0.5, reduced, 0.0),
                jnp.where(offset > 0.5, reduced, 0.0),
                jnp.where(offset < -0.5, reduced, 0.0),
            ))
        for big_y in range(2):
            cols = slice(4 * big_y, 4 * big_y + 4)
            here, up, down = (
                jnp.sum(parts[0][k][cols], axis=0) + jnp.sum(parts[1][k][cols], axis=0) for k in range(3)
            )
            sums.append(here + by_eight(up, False) + by_eight(down, True))
    stacked = jnp.concatenate(sums, axis=0)
    row = lax.broadcasted_iota(jnp.int32, (128, 128), 0)
    col = lax.broadcasted_iota(jnp.int32, (128, 128), 1)
    group = jnp.where(row // 8 == col % 16, 1.0, 0.0).astype(F32)
    grouped = jnp.dot(stacked, group, preferred_element_type=F32, precision=lax.Precision.HIGHEST)
    sub = lax.broadcasted_iota(jnp.int32, (8, 128), 0)
    lane = lax.broadcasted_iota(jnp.int32, (8, 128), 1)
    rows = [
        jnp.sum(jnp.where(lane // 16 == sub, grouped[8 * c : 8 * c + 8], 0.0), axis=0, keepdims=True)
        for c in range(4)
    ]
    zero = jnp.zeros((1, 128), F32)
    rows = rows + ([zero] if first else [dots_ref[...]]) + [zero] * 3
    tile = jnp.concatenate(rows, axis=0)
    for j in range(send_ref.shape[0]):
        send_ref[j, 0:8] = tile
    if first:
        more = [cdiag_ref[c // 2, c % 2 : c % 2 + 1, :] for c in range(4)]
        for f in range(3):
            more = more + [FACES[f] * link_ref[f, c // 2, c % 2 : c % 2 + 1, :] for c in range(4)]
        tile = jnp.concatenate(more, axis=0)
        for j in range(send_ref.shape[0]):
            send_ref[j, 8:24] = tile


def window_body(first, me_ref, got_ref, send_ref):
    px, last_x = me_ref[0], me_ref[2]
    count = got_ref.shape[0]
    total = got_ref[0, 4:5, :]
    for j in range(1, count):
        total = total + got_ref[j, 4:5, :]
    zero = jnp.zeros((1, 128), F32)
    at = [jnp.clip(px + d, 0, last_x) for d in range(-2, 3)]
    rows = []
    for big_y in range(2):
        for d in range(5):
            for big_x in range(2):
                rows.append(got_ref[at[d], 2 * big_x + big_y : 2 * big_x + big_y + 1, :])
        rows = rows + [total] + [zero] * 5
    tile = jnp.concatenate(rows, axis=0)
    for j in range(send_ref.shape[0]):
        send_ref[j, 0:32] = tile
    if first:
        rows = []
        for f in range(4):
            for big_y in range(2):
                for d in range(5):
                    for big_x in range(2):
                        r = 8 + 4 * f + 2 * big_x + big_y
                        rows.append(got_ref[at[d], r : r + 1, :])
        tile = jnp.concatenate(rows, axis=0)
        for j in range(send_ref.shape[0]):
            send_ref[j, 32:112] = tile


SPOTS = ((-2, 1), (-1, 0), (-1, 1), (0, 0), (0, 1), (1, 0), (1, 1), (2, 0))


def shift_x(value, ahead):
    return pltpu.roll(value, 15 if ahead else 1, 0)


def shift_k(value, ahead):
    return pltpu.roll(value, 127 if ahead else 1, 1)


def coarse_setup_body(me_ref, got_ref, coef_ref):
    px, py, last_x, last_y = me_ref[0], me_ref[1], me_ref[2], me_ref[3]
    row = lax.broadcasted_iota(jnp.int32, (16, 128), 0)
    lane = lax.broadcasted_iota(jnp.int32, (16, 128), 1)
    pad = jnp.zeros((6, 128), F32)
    where_x = 2 * px - 4 + row
    inside_x = (where_x >= 0) & (where_x < 2 * (last_x + 1)) & (row < 10)

    def take(y, f):
        d, big_y = SPOTS[y]
        at = jnp.clip(py + d, 0, last_y)
        start = 32 + 20 * f + 10 * big_y
        return jnp.concatenate([got_ref[at, start : start + 10, :], pad], axis=0)

    links = [[take(y, f) for y in range(8)] for f in range(1, 4)]
    for y in range(8):
        where_y = 2 * py - 3 + y
        seen = jnp.where((where_y >= 0) & (where_y < 2 * (last_y + 1)), 1.0, 0.0).astype(F32)
        diag = jnp.where(inside_x, take(y, 0), 1.0)
        inverse = jnp.where(inside_x, seen / diag, 0.0)
        coef_ref[0, y] = inverse
        if 1 <= y <= 6:
            coef_ref[1, y] = links[0][y] * inverse
            coef_ref[2, y] = shift_x(links[0][y], False) * inverse
            coef_ref[3, y] = links[1][y] * inverse
            coef_ref[4, y] = links[1][y - 1] * inverse
            coef_ref[5, y] = jnp.where(lane < 127, links[2][y] * inverse, 0.0)
            coef_ref[6, y] = jnp.where(lane > 0, shift_k(links[2][y], False) * inverse, 0.0)
        else:
            for f in range(1, 7):
                coef_ref[f, y] = jnp.zeros((16, 128), F32)


def dots_of(pairs):
    lane = lax.broadcasted_iota(jnp.int32, (1, 128), 1)
    out = jnp.zeros((1, 128), F32)
    for k, value in enumerate(pairs):
        out = jnp.where(lane == k, jnp.sum(value), out)
    return out


def correct_rows(me_ref, got_ref, coef_ref, smooth_ref, remain_ref, inverse_ref, scale_ref, offset_ref):
    py, last_y = me_ref[1], me_ref[3]
    start = []
    for y, (d, big_y) in enumerate(SPOTS):
        at = jnp.clip(py + d, 0, last_y)
        start.append(got_ref[at, 16 * big_y : 16 * big_y + 16, :] * coef_ref[0, y])

    def sweep(now, y):
        here = now[y]
        total = start[y] + coef_ref[1, y] * shift_x(here, True) + coef_ref[2, y] * shift_x(here, False)
        total = total + coef_ref[3, y] * now[y + 1] + coef_ref[4, y] * now[y - 1]
        return total + coef_ref[5, y] * shift_k(here, True) + coef_ref[6, y] * shift_k(here, False)

    second = [None] + [sweep(start, y) for y in range(1, 7)] + [None]
    third = [None, None] + [sweep(second, y) for y in range(2, 6)]
    sub = lax.broadcasted_iota(jnp.int32, (8, 128), 0)
    lane = lax.broadcasted_iota(jnp.int32, (8, 128), 1)
    index = sub * 16 + lane // 8

    def spread_out(tile, x):
        wide = jnp.broadcast_to(tile[x + 4 : x + 5, :], (8, 128))
        return jnp.take_along_axis(wide, index, axis=1)

    tables = [[], [], []]
    for y in range(2, 6):
        for k, tile in enumerate((third[y], shift_k(third[y], True), shift_k(third[y], False))):
            tables[k].append([spread_out(tile, x) for x in range(-2, 4)])
    counts = (3, 4, 4, 3)

    def lifted(x):
        big_x = x // 2
        here, up, down = (
            jnp.concatenate(
                [jnp.broadcast_to(tables[k][y][big_x + 2][None], (counts[y], 8, 128)) for y in range(4)], axis=0
            )
            for k in range(3)
        )
        offset = offset_ref[x + 3]
        return jnp.where(offset > 0.5, up, jnp.where(offset < -0.5, down, here))

    lifts = [lifted(x) for x in range(-3, 7)]
    spreads = []
    for x in range(8):
        near = beside(lifts[x][1:13], lifts[x + 1], lifts[x + 2][1:13])
        spreads.append(REST * lifts[x + 1][1:13] + OMEGA * (inverse_ref[x] * near))
    shaped = []
    for x in range(6):
        near = beside(spreads[x][1:11], spreads[x + 1], spreads[x + 2][1:11])
        spread = spreads[x + 1][1:11]
        left = remain_ref[x] - (scale_ref[x] * spread - near)
        shaped.append(smooth_ref[x] + spread + OMEGA * (inverse_ref[x + 1, 1:11] * left))
    for x in range(4):
        near = beside(shaped[x][1:9], shaped[x + 1], shaped[x + 2][1:9])
        own = shaped[x + 1][1:9]
        yield x, own, scale_ref[x + 1, 1:9] * own - near


def put(low_ref, high_ref, x, value):
    (low_ref if x < 2 else high_ref)[x % 2] = value


def begin_body(me_ref, got_ref, coef_ref, smooth_ref, remain_ref, inverse_ref, scale_ref, offset_ref,
               low_ref, high_ref, z_ref, wlow_ref, whigh_ref, dots_ref):
    gamma = jnp.zeros((8, 128), F32)
    delta = jnp.zeros((8, 128), F32)
    for x, z, w in correct_rows(me_ref, got_ref, coef_ref, smooth_ref, remain_ref, inverse_ref, scale_ref, offset_ref):
        z_ref[x] = z
        put(wlow_ref, whigh_ref, x, w)
        r = (low_ref if x < 2 else high_ref)[0, x % 2]
        gamma = gamma + jnp.sum(r * z, axis=0)
        delta = delta + jnp.sum(w * z, axis=0)
    dots_ref[...] = dots_of((gamma, delta))


def scalars_of(total, old):
    gamma, delta = total[:, 0:1], total[:, 1:2]
    if old is None:
        return gamma, gamma / delta, None
    gamma_old, alpha_old = old[:, 0:1], old[:, 1:2]
    beta = gamma / gamma_old
    return gamma, gamma / (delta - beta * gamma / alpha_old), beta


def as_row(gamma, alpha):
    lane = lax.broadcasted_iota(jnp.int32, (1, 128), 1)
    return jnp.where(lane == 0, gamma, jnp.where(lane == 1, alpha, 0.0))


def total_of(got_ref, row):
    total = got_ref[0, row : row + 1, :]
    for j in range(1, got_ref.shape[0]):
        total = total + got_ref[j, row : row + 1, :]
    return total


def step_body(first, me_ref, got_ref, coef_ref, smooth_ref, remain_ref, inverse_ref, scale_ref, offset_ref,
              z_ref, wlow_ref, whigh_ref, *refs):
    if first:
        low_ref, high_ref = refs[:2]
        refs = refs[2:]
        old = None
    else:
        x_ref, r_ref, p_ref, s_ref, q_ref, t_ref, old_ref = refs[:7]
        refs = refs[7:]
        old = old_ref[...]
    zo_ref, wolow_ref, wohigh_ref, xo_ref, ro_ref, po_ref, so_ref, qo_ref, to_ref, dots_ref, keep_ref = refs
    gamma, alpha, beta = scalars_of(total_of(got_ref, 10), old)
    keep_ref[...] = as_row(gamma, alpha)
    alpha3 = jnp.broadcast_to(alpha, (8, 128))[None]
    beta3 = None if first else jnp.broadcast_to(beta, (8, 128))[None]
    gamma_sum = jnp.zeros((8, 128), F32)
    delta_sum = jnp.zeros((8, 128), F32)
    for x, m, n in correct_rows(me_ref, got_ref, coef_ref, smooth_ref, remain_ref, inverse_ref, scale_ref, offset_ref):
        z = z_ref[x]
        w = (wlow_ref if x < 2 else whigh_ref)[x % 2]
        if first:
            p, s, q, t = z, w, m, n
            r = (low_ref if x < 2 else high_ref)[0, x % 2]
            xo_ref[x] = alpha3 * p
        else:
            p, s, q, t = z + beta3 * p_ref[x], w + beta3 * s_ref[x], m + beta3 * q_ref[x], n + beta3 * t_ref[x]
            r = r_ref[x]
            xo_ref[x] = x_ref[x] + alpha3 * p
        r = r - alpha3 * s
        z = z - alpha3 * q
        w = w - alpha3 * t
        po_ref[x], so_ref[x], qo_ref[x], to_ref[x] = p, s, q, t
        ro_ref[x], zo_ref[x] = r, z
        put(wolow_ref, wohigh_ref, x, w)
        gamma_sum = gamma_sum + jnp.sum(r * z, axis=0)
        delta_sum = delta_sum + jnp.sum(w * z, axis=0)
    dots_ref[...] = dots_of((gamma_sum, delta_sum))


def spread_dots_body(dots_ref, send_ref):
    tile = jnp.broadcast_to(dots_ref[...], (8, 128))
    for j in range(send_ref.shape[0]):
        send_ref[j] = tile


def sum_dots_body(got_ref, send_ref):
    total = got_ref[0]
    for j in range(1, got_ref.shape[0]):
        total = total + got_ref[j]
    for j in range(send_ref.shape[0]):
        send_ref[j] = total


def finish_body(got_ref, z_ref, wlow_ref, whigh_ref, x_ref, r_ref, p_ref, s_ref, old_ref, xo_ref, ro_ref,
                xs_ref, rs_ref):
    gamma, alpha, beta = scalars_of(total_of(got_ref, 0), old_ref[...])
    alpha3 = jnp.broadcast_to(alpha, (8, 128))[None]
    beta3 = jnp.broadcast_to(beta, (8, 128))[None]
    for x in range(4):
        w = (wlow_ref if x < 2 else whigh_ref)[x % 2]
        p = z_ref[x] + beta3 * p_ref[x]
        s = w + beta3 * s_ref[x]
        xs_ref[pl.ds(64 * x, 64), :] = (x_ref[x] + alpha3 * p).reshape(64, 128)
        rs_ref[pl.ds(64 * x, 64), :] = (r_ref[x] - alpha3 * s).reshape(64, 128)
    for x in range(4):
        for s in range(8):
            part = slice(s * 128, (s + 1) * 128)
            xo_ref[x, :, part] = xs_ref[pl.ds(64 * x + s, 8, stride=8), :]
            ro_ref[x, :, part] = rs_ref[pl.ds(64 * x + s, 8, stride=8), :]


def bodied(body, first):
    def run(*refs):
        body(first, *refs)

    return run


def local(right_side, diagonal, aggregate_id, coarse_diag, coarse_link):
    count_x, count_y = lax.axis_size("px"), lax.axis_size("py")
    me = jnp.stack([lax.axis_index("px"), lax.axis_index("py"), count_x - 1, count_y - 1]).astype(jnp.int32)

    def both_ways(low, high, axis):
        count = lax.axis_size(axis)
        up = [(i, (i + 1) % count) for i in range(count)]
        down = [(b, a) for a, b in up]
        return lax.ppermute(high, axis, up), lax.ppermute(low, axis, down)

    def gather(value, axis):
        return lax.all_to_all(value, axis, 0, 0)

    two, field = (2, 8, 8, 128), (4, 8, 8, 128)
    low, high, olow, ohigh = call(
        enter_body, [(256, 128)] * 2 + [(192, 128)] * 2, right_side, diagonal, aggregate_id, scalars=0
    )
    low, high = low.reshape((2,) + two), high.reshape((2,) + two)
    olow, ohigh = olow.reshape(3, 8, 8, 128), ohigh.reshape(3, 8, 8, 128)
    xlow, xhigh = both_ways(low, high, "px")
    oxlow, oxhigh = both_ways(olow, ohigh, "px")
    first, last, ofirst, olast = call(
        pack_first_body, [(2, 8, 2, 8, 128)] * 2 + [(10, 3, 8, 128)] * 2,
        low, high, xlow, xhigh, olow, ohigh, oxlow, oxhigh, scalars=0,
    )
    ylow, yhigh = both_ways(first, last, "py")
    oylow, oyhigh = both_ways(ofirst, olast, "py")
    inverse, scale, offset = call(
        setup_body, [(8, 12, 8, 128), (6, 10, 8, 128), (10, 14, 8, 128)],
        me, low, high, xlow, xhigh, ylow, yhigh, olow, ohigh, oxlow, oxhigh, oylow, oyhigh,
    )
    mid = (6, 10, 8, 128)
    smooth, remain, send = call(
        bodied(restrict_body, True), [mid, mid, (count_x, 24, 128)],
        low, high, xlow, xhigh, ylow, yhigh, inverse, offset, coarse_diag, coarse_link, scalars=0,
    )
    send, = call(bodied(window_body, True), [(count_y, 112, 128)], me, gather(send, "px"))
    got = gather(send, "py")
    coef, = call(coarse_setup_body, [(7, 8, 16, 128)], me, got)
    fixed = (inverse, scale, offset)
    z, wlow, whigh, dots = call(
        begin_body, [field, two, two, (1, 128)], me, got, coef, smooth, remain, *fixed, low, high
    )
    state = None
    for iteration in range(ITERS - 1):
        xlow, xhigh = both_ways(wlow, whigh, "px")
        first, last = call(pack_body, [(8, 2, 8, 128)] * 2, wlow, whigh, xlow, xhigh, scalars=0)
        ylow, yhigh = both_ways(first, last, "py")
        smooth, remain, send = call(
            bodied(restrict_body, False), [mid, mid, (count_x, 8, 128)],
            wlow, whigh, xlow, xhigh, ylow, yhigh, inverse, offset, dots, scalars=0,
        )
        send, = call(bodied(window_body, False), [(count_y, 32, 128)], me, gather(send, "px"))
        got = gather(send, "py")
        more = (low, high) if state is None else state
        z, wlow, whigh, x, r, p, s, q, t, dots, keep = call(
            bodied(step_body, state is None), [field, two, two] + [field] * 6 + [(1, 128)] * 2,
            me, got, coef, smooth, remain, *fixed, z, wlow, whigh, *more,
        )
        state = (x, r, p, s, q, t, keep)
    send, = call(spread_dots_body, [(count_x, 8, 128)], dots, scalars=0)
    send, = call(sum_dots_body, [(count_y, 8, 128)], gather(send, "px"), scalars=0)
    got = gather(send, "py")
    return tuple(call(
        finish_body, [right_side.shape] * 2, got, z, wlow, whigh, x, r, p, s, keep,
        scalars=0, scratch=[pltpu.VMEM((256, 128), F32)] * 2,
    ))


def solution(mesh):
    cells = P("px", "py", None)
    in_specs = (cells, cells, cells, cells, P(None, "px", "py", None))
    return jax.shard_map(local, mesh=mesh, in_specs=in_specs, out_specs=(cells, cells), check_vma=False)
```

```python
import jax
import jax.numpy as jnp
from jax import lax
from jax.experimental import pallas as pl
from jax.experimental.pallas import tpu as pltpu
from jax.sharding import PartitionSpec as P

ITERS = 4
OMEGA = 2.0 / 3.0
REST = 1.0 - OMEGA
FACES = (32.0, 16.0, 8.0)
F32 = jnp.float32


def call(body, outs, *args, scalars=1, scratch=(), flops=2_000_000):
    smem = pl.BlockSpec(memory_space=pltpu.SMEM)
    vmem = pl.BlockSpec(memory_space=pltpu.VMEM)
    specs = [smem] * scalars + [vmem] * (len(args) - scalars)
    return pl.pallas_call(
        body,
        out_shape=[jax.ShapeDtypeStruct(shape, F32) for shape in outs],
        in_specs=specs,
        out_specs=[vmem] * len(outs),
        scratch_shapes=list(scratch),
        compiler_params=pltpu.CompilerParams(vmem_limit_bytes=20 * 1024 * 1024),
        cost_estimate=pl.CostEstimate(flops=flops, bytes_accessed=1_000_000, transcendentals=0),
    )(*args)


def along_z(value):
    lane = lax.broadcasted_iota(jnp.int32, value.shape, value.ndim - 1)
    sub = lax.broadcasted_iota(jnp.int32, value.shape, value.ndim - 2)
    after = pltpu.roll(value, 127, value.ndim - 1)
    before = pltpu.roll(value, 1, value.ndim - 1)
    after_row = jnp.where(sub == 7, 0.0, pltpu.roll(after, 7, value.ndim - 2))
    before_row = jnp.where(sub == 0, 0.0, pltpu.roll(before, 1, value.ndim - 2))
    return jnp.where(lane == 127, after_row, after) + jnp.where(lane == 0, before_row, before)


def by_eight(value, ahead):
    lane = lax.broadcasted_iota(jnp.int32, value.shape, value.ndim - 1)
    if ahead:
        moved = pltpu.roll(value, 120, value.ndim - 1)
        return jnp.where(lane >= 120, pltpu.roll(moved, 7, value.ndim - 2), moved)
    moved = pltpu.roll(value, 8, value.ndim - 1)
    return jnp.where(lane < 8, pltpu.roll(moved, 1, value.ndim - 2), moved)


def beside(below, here, above):
    count = here.shape[0]
    inner = here[1 : count - 1]
    return below + above + here[0 : count - 2] + here[2:count] + along_z(inner)


def enter_body(b_ref, d_ref, a_ref, low_ref, high_ref):
    lane = lax.broadcasted_iota(jnp.int32, (8, 128), 1)
    for x in range(4):
        for s in range(8):
            part = slice(s * 128, (s + 1) * 128)
            b = b_ref[x, :, part]
            d = d_ref[x, :, part]
            home = (lane + s * 128) // 8
            o = ((a_ref[x, :, part] & 127) - home).astype(F32)
            ref = low_ref if x < 2 else high_ref
            at = (x % 2) * 64 + s
            ref[pl.ds(at, 8, stride=8), :] = b
            ref[pl.ds(128 + at, 8, stride=8), :] = d
            if x < 3:
                low_ref[pl.ds(256 + x * 64 + s, 8, stride=8), :] = o
            if x > 0:
                high_ref[pl.ds(256 + (x - 1) * 64 + s, 8, stride=8), :] = o


def field_rows(low, high, xlow, xhigh, base):
    return [ref.at[base + k] for ref in (xlow, low, high, xhigh) for k in range(2)]


def offset_rows(low, high, xlow, xhigh):
    return [ref.at[4 + k] for ref, ks in ((xlow, (0, 1, 2)), (low, (0, 1, 2)), (high, (2,)), (xhigh, (0, 1, 2))) for k in ks]


def pack_first_body(low_ref, high_ref, xlow_ref, xhigh_ref, first_ref, last_ref):
    four = (low_ref, high_ref, xlow_ref, xhigh_ref)
    for f in range(2):
        for x, ref in enumerate(field_rows(*four, 2 * f)):
            at = 16 * f + 2 * x
            first_ref[at : at + 2] = ref[0:2]
            last_ref[at : at + 2] = ref[6:8]
    for x, ref in enumerate(offset_rows(*four)):
        at = 32 + 3 * x
        first_ref[at : at + 3] = ref[0:3]
        last_ref[at : at + 3] = ref[5:8]


def setup_body(me_ref, low_ref, high_ref, xlow_ref, xhigh_ref, ylow_ref, yhigh_ref, inverse_ref, scale_ref, offset_ref):
    px, py, last_x, last_y = me_ref[0], me_ref[1], me_ref[2], me_ref[3]
    below = jnp.where(px > 0, 1.0, 0.0).astype(F32)
    above = jnp.where(px < last_x, 1.0, 0.0).astype(F32)
    left = jnp.where(py > 0, 1.0, 0.0).astype(F32)
    right = jnp.where(py < last_y, 1.0, 0.0).astype(F32)
    four = (low_ref, high_ref, xlow_ref, xhigh_ref)
    for x, ref in enumerate(field_rows(*four, 2)):
        s_mid = 6.0 + ref[...]
        s_left = 6.0 + ylow_ref[16 + 2 * x : 18 + 2 * x]
        s_right = 6.0 + yhigh_ref[16 + 2 * x : 18 + 2 * x]
        i_mid, i_left, i_right = 1.0 / s_mid, left / s_left, right / s_right
        if x < 2 or x > 5:
            seen = below if x < 2 else above
            i_mid, i_left, i_right = i_mid * seen, i_left * seen, i_right * seen
        inverse_ref[x, 0:2] = i_left
        inverse_ref[x, 2:10] = i_mid
        inverse_ref[x, 10:12] = i_right
        if 1 <= x <= 6:
            scale_ref[x - 1, 0:1] = s_left[1:2]
            scale_ref[x - 1, 1:9] = s_mid
            scale_ref[x - 1, 9:10] = s_right[0:1]
    for x, ref in enumerate(offset_rows(*four)):
        offset_ref[x, 0:3] = ylow_ref[32 + 3 * x : 35 + 3 * x]
        offset_ref[x, 3:11] = ref[...]
        offset_ref[x, 11:14] = yhigh_ref[32 + 3 * x : 35 + 3 * x]


def pack_body(low_ref, high_ref, xlow_ref, xhigh_ref, first_ref, last_ref):
    for r, ref in enumerate((xlow_ref, low_ref, high_ref, xhigh_ref)):
        for k in range(2):
            first_ref[2 * r + k] = ref[k, 0:2]
            last_ref[2 * r + k] = ref[k, 6:8]


def restrict_body(first, *refs):
    if first:
        (low, high, xlow, xhigh, ylow, yhigh, inverse_ref, offset_ref, cdiag_ref, link_ref,
         smooth_ref, remain_ref, send_ref) = refs
    else:
        (low, high, xlow, xhigh, ylow, yhigh, inverse_ref, offset_ref, dots_ref,
         smooth_ref, remain_ref, send_ref) = refs
    mids = [ref.at[k] for ref in (xlow, low, high, xhigh) for k in range(2)]

    def vector(x):
        if first:
            sides = ylow[2 * x : 2 * x + 2], yhigh[2 * x : 2 * x + 2]
        else:
            sides = ylow[x], yhigh[x]
        return jnp.concatenate([sides[0], mids[x][...], sides[1]], axis=0)

    smooth = [OMEGA * vector(x) * inverse_ref[x] for x in range(8)]
    shrunk = []
    remains = []
    for x in range(1, 7):
        near = beside(smooth[x - 1][1:11], smooth[x], smooth[x + 1][1:11])
        remain = REST * vector(x)[1:11] + near
        smooth_ref[x - 1] = smooth[x][1:11]
        remain_ref[x - 1] = remain
        remains.append(remain[1:9])
        shrunk.append(remain * inverse_ref[x, 1:11])
    sums = []
    for big_x in range(2):
        parts = []
        for x in (2 * big_x, 2 * big_x + 1):
            near = beside(shrunk[x][1:9], shrunk[x + 1], shrunk[x + 2][1:9])
            reduced = REST * remains[x + 1] + OMEGA * near
            offset = offset_ref[x + 3, 3:11]
            parts.append((
                jnp.where(jnp.abs(offset) < 0.5, reduced, 0.0),
                jnp.where(offset > 0.5, reduced, 0.0),
                jnp.where(offset < -0.5, reduced, 0.0),
            ))
        for big_y in range(2):
            cols = slice(4 * big_y, 4 * big_y + 4)
            here, up, down = (
                jnp.sum(parts[0][k][cols], axis=0) + jnp.sum(parts[1][k][cols], axis=0) for k in range(3)
            )
            sums.append(here + by_eight(up, False) + by_eight(down, True))
    stacked = jnp.concatenate(sums, axis=0)
    row = lax.broadcasted_iota(jnp.int32, (128, 128), 0)
    col = lax.broadcasted_iota(jnp.int32, (128, 128), 1)
    group = jnp.where(row // 8 == col % 16, 1.0, 0.0).astype(F32)
    grouped = jnp.dot(stacked, group, preferred_element_type=F32, precision=lax.Precision.HIGHEST)
    sub = lax.broadcasted_iota(jnp.int32, (8, 128), 0)
    lane = lax.broadcasted_iota(jnp.int32, (8, 128), 1)
    rows = [
        jnp.sum(jnp.where(lane // 16 == sub, grouped[8 * c : 8 * c + 8], 0.0), axis=0, keepdims=True)
        for c in range(4)
    ]
    zero = jnp.zeros((1, 128), F32)
    rows = rows + ([zero] if first else [dots_ref[...]]) + [zero] * 3
    tile = jnp.concatenate(rows, axis=0)
    if first:
        send_ref[0:8] = tile
        more = [cdiag_ref[c // 2, c % 2 : c % 2 + 1, :] for c in range(4)]
        for f in range(3):
            more = more + [FACES[f] * link_ref[f, c // 2, c % 2 : c % 2 + 1, :] for c in range(4)]
        send_ref[8:24] = jnp.concatenate(more, axis=0)
    else:
        for j in range(send_ref.shape[0]):
            send_ref[j] = tile


def window_rows(pieces, start):
    return [
        [ref[start + 2 * big_x + big_y : start + 2 * big_x + big_y + 1, :] for ref in pieces for big_x in range(2)]
        for big_y in range(2)
    ]


def window_first_body(*refs):
    pieces, send_ref = refs[:5], refs[5]
    zero = jnp.zeros((6, 128), F32)
    early, late = window_rows(pieces, 0)
    send_ref[0:32] = jnp.concatenate(early + [zero] + late + [zero], axis=0)
    rows = []
    for f in range(4):
        early, late = window_rows(pieces, 8 + 4 * f)
        rows = rows + early + late
    send_ref[32:112] = jnp.concatenate(rows, axis=0)


def window_body(me_ref, got_ref, send_ref):
    px, last_x = me_ref[0], me_ref[2]
    total = total_of(got_ref, 4)
    zero = jnp.zeros((5, 128), F32)
    early, late = window_rows([got_ref.at[jnp.clip(px + d, 0, last_x)] for d in range(-2, 3)], 0)
    tile = jnp.concatenate(early + [total, zero] + late + [total, zero], axis=0)
    for j in range(send_ref.shape[0]):
        send_ref[j] = tile


SPOTS = ((-2, 1), (-1, 0), (-1, 1), (0, 0), (0, 1), (1, 0), (1, 1), (2, 0))


def shift_x(value, ahead):
    return pltpu.roll(value, 15 if ahead else 1, 0)


def shift_k(value, ahead):
    return pltpu.roll(value, 127 if ahead else 1, 1)


def coarse_setup_body(me_ref, *refs):
    pieces, coef_ref = refs[:5], refs[5]
    px, py, last_x, last_y = me_ref[0], me_ref[1], me_ref[2], me_ref[3]
    row = lax.broadcasted_iota(jnp.int32, (16, 128), 0)
    lane = lax.broadcasted_iota(jnp.int32, (16, 128), 1)
    pad = jnp.zeros((6, 128), F32)
    where_x = 2 * px - 4 + row
    inside_x = (where_x >= 0) & (where_x < 2 * (last_x + 1)) & (row < 10)

    def take(y, f):
        d, big_y = SPOTS[y]
        start = 32 + 20 * f + 10 * big_y
        return jnp.concatenate([pieces[d + 2][start : start + 10, :], pad], axis=0)

    links = [[take(y, f) for y in range(8)] for f in range(1, 4)]
    for y in range(8):
        where_y = 2 * py - 3 + y
        seen = jnp.where((where_y >= 0) & (where_y < 2 * (last_y + 1)), 1.0, 0.0).astype(F32)
        diag = jnp.where(inside_x, take(y, 0), 1.0)
        inverse = jnp.where(inside_x, seen / diag, 0.0)
        coef_ref[0, y] = inverse
        if 1 <= y <= 6:
            coef_ref[1, y] = links[0][y] * inverse
            coef_ref[2, y] = shift_x(links[0][y], False) * inverse
            coef_ref[3, y] = links[1][y] * inverse
            coef_ref[4, y] = links[1][y - 1] * inverse
            coef_ref[5, y] = jnp.where(lane < 127, links[2][y] * inverse, 0.0)
            coef_ref[6, y] = jnp.where(lane > 0, shift_k(links[2][y], False) * inverse, 0.0)
        else:
            for f in range(1, 7):
                coef_ref[f, y] = jnp.zeros((16, 128), F32)


def dots_of(pairs):
    lane = lax.broadcasted_iota(jnp.int32, (1, 128), 1)
    out = jnp.zeros((1, 128), F32)
    for k, value in enumerate(pairs):
        out = jnp.where(lane == k, jnp.sum(value), out)
    return out


def correct_rows(pieces, coef_ref, smooth_ref, remain_ref, inverse_ref, scale_ref, offset_ref):
    start = [
        pieces[d + 2][16 * big_y : 16 * big_y + 16, :] * coef_ref[0, y] for y, (d, big_y) in enumerate(SPOTS)
    ]

    def sweep(now, y):
        here = now[y]
        total = start[y] + coef_ref[1, y] * shift_x(here, True) + coef_ref[2, y] * shift_x(here, False)
        total = total + coef_ref[3, y] * now[y + 1] + coef_ref[4, y] * now[y - 1]
        return total + coef_ref[5, y] * shift_k(here, True) + coef_ref[6, y] * shift_k(here, False)

    second = [None] + [sweep(start, y) for y in range(1, 7)] + [None]
    third = [None, None] + [sweep(second, y) for y in range(2, 6)]
    sub = lax.broadcasted_iota(jnp.int32, (8, 128), 0)
    lane = lax.broadcasted_iota(jnp.int32, (8, 128), 1)
    index = sub * 16 + lane // 8

    def spread_out(tile, x):
        wide = jnp.broadcast_to(tile[x + 4 : x + 5, :], (8, 128))
        return jnp.take_along_axis(wide, index, axis=1)

    tables = [[], [], []]
    for y in range(2, 6):
        for k, tile in enumerate((third[y], shift_k(third[y], True), shift_k(third[y], False))):
            tables[k].append([spread_out(tile, x) for x in range(-2, 4)])
    counts = (3, 4, 4, 3)

    def lifted(x):
        big_x = x // 2
        here, up, down = (
            jnp.concatenate(
                [jnp.broadcast_to(tables[k][y][big_x + 2][None], (counts[y], 8, 128)) for y in range(4)], axis=0
            )
            for k in range(3)
        )
        offset = offset_ref[x + 3]
        return jnp.where(offset > 0.5, up, jnp.where(offset < -0.5, down, here))

    lifts = [lifted(x) for x in range(-3, 7)]
    spreads = []
    for x in range(8):
        near = beside(lifts[x][1:13], lifts[x + 1], lifts[x + 2][1:13])
        spreads.append(REST * lifts[x + 1][1:13] + OMEGA * (inverse_ref[x] * near))
    shaped = []
    for x in range(6):
        near = beside(spreads[x][1:11], spreads[x + 1], spreads[x + 2][1:11])
        spread = spreads[x + 1][1:11]
        left = remain_ref[x] - (scale_ref[x] * spread - near)
        shaped.append(smooth_ref[x] + spread + OMEGA * (inverse_ref[x + 1, 1:11] * left))
    for x in range(4):
        near = beside(shaped[x][1:9], shaped[x + 1], shaped[x + 2][1:9])
        own = shaped[x + 1][1:9]
        yield x, own, scale_ref[x + 1, 1:9] * own - near


def put(low_ref, high_ref, x, value):
    (low_ref if x < 2 else high_ref)[x % 2] = value


def begin_body(*refs):
    pieces, refs = refs[:5], refs[5:]
    fixed, (low_ref, high_ref, z_ref, wlow_ref, whigh_ref, dots_ref) = refs[:6], refs[6:]
    gamma = jnp.zeros((8, 128), F32)
    delta = jnp.zeros((8, 128), F32)
    for x, z, w in correct_rows(pieces, *fixed):
        z_ref[x] = z
        put(wlow_ref, whigh_ref, x, w)
        r = (low_ref if x < 2 else high_ref)[x % 2]
        gamma = gamma + jnp.sum(r * z, axis=0)
        delta = delta + jnp.sum(w * z, axis=0)
    dots_ref[...] = dots_of((gamma, delta))


def scalars_of(total, old):
    gamma, delta = total[:, 0:1], total[:, 1:2]
    if old is None:
        return gamma, gamma / delta, None
    gamma_old, alpha_old = old[:, 0:1], old[:, 1:2]
    beta = gamma / gamma_old
    return gamma, gamma / (delta - beta * gamma / alpha_old), beta


def as_row(gamma, alpha):
    lane = lax.broadcasted_iota(jnp.int32, (1, 128), 1)
    return jnp.where(lane == 0, gamma, jnp.where(lane == 1, alpha, 0.0))


def total_of(got_ref, row):
    total = got_ref[0, row : row + 1, :]
    for j in range(1, got_ref.shape[0]):
        total = total + got_ref[j, row : row + 1, :]
    return total


def step_body(first, me_ref, got_ref, coef_ref, smooth_ref, remain_ref, inverse_ref, scale_ref, offset_ref,
              z_ref, wlow_ref, whigh_ref, *refs):
    if first:
        low_ref, high_ref = refs[:2]
        refs = refs[2:]
        old = None
    else:
        x_ref, r_ref, p_ref, s_ref, q_ref, t_ref, old_ref = refs[:7]
        refs = refs[7:]
        old = old_ref[...]
    zo_ref, wolow_ref, wohigh_ref, xo_ref, ro_ref, po_ref, so_ref, qo_ref, to_ref, dots_ref, keep_ref = refs
    gamma, alpha, beta = scalars_of(total_of(got_ref, 10), old)
    keep_ref[...] = as_row(gamma, alpha)
    alpha3 = jnp.broadcast_to(alpha, (8, 128))[None]
    beta3 = None if first else jnp.broadcast_to(beta, (8, 128))[None]
    gamma_sum = jnp.zeros((8, 128), F32)
    delta_sum = jnp.zeros((8, 128), F32)
    py, last_y = me_ref[1], me_ref[3]
    pieces = [got_ref.at[jnp.clip(py + d, 0, last_y)] for d in range(-2, 3)]
    fixed = (coef_ref, smooth_ref, remain_ref, inverse_ref, scale_ref, offset_ref)
    for x, m, n in correct_rows(pieces, *fixed):
        z = z_ref[x]
        w = (wlow_ref if x < 2 else whigh_ref)[x % 2]
        if first:
            p, s, q, t = z, w, m, n
            r = (low_ref if x < 2 else high_ref)[x % 2]
            xo_ref[x] = alpha3 * p
        else:
            p, s, q, t = z + beta3 * p_ref[x], w + beta3 * s_ref[x], m + beta3 * q_ref[x], n + beta3 * t_ref[x]
            r = r_ref[x]
            xo_ref[x] = x_ref[x] + alpha3 * p
        r = r - alpha3 * s
        z = z - alpha3 * q
        w = w - alpha3 * t
        po_ref[x], so_ref[x], qo_ref[x], to_ref[x] = p, s, q, t
        ro_ref[x], zo_ref[x] = r, z
        put(wolow_ref, wohigh_ref, x, w)
        gamma_sum = gamma_sum + jnp.sum(r * z, axis=0)
        delta_sum = delta_sum + jnp.sum(w * z, axis=0)
    dots_ref[...] = dots_of((gamma_sum, delta_sum))


def spread_dots_body(dots_ref, send_ref):
    tile = jnp.broadcast_to(dots_ref[...], (8, 128))
    for j in range(send_ref.shape[0]):
        send_ref[j] = tile


def sum_dots_body(got_ref, send_ref):
    total = got_ref[0]
    for j in range(1, got_ref.shape[0]):
        total = total + got_ref[j]
    for j in range(send_ref.shape[0]):
        send_ref[j] = total


def finish_body(got_ref, z_ref, wlow_ref, whigh_ref, x_ref, r_ref, p_ref, s_ref, old_ref, xo_ref, ro_ref,
                xs_ref, rs_ref):
    gamma, alpha, beta = scalars_of(total_of(got_ref, 0), old_ref[...])
    alpha3 = jnp.broadcast_to(alpha, (8, 128))[None]
    beta3 = jnp.broadcast_to(beta, (8, 128))[None]
    for x in range(4):
        w = (wlow_ref if x < 2 else whigh_ref)[x % 2]
        p = z_ref[x] + beta3 * p_ref[x]
        s = w + beta3 * s_ref[x]
        xs_ref[pl.ds(64 * x, 64), :] = (x_ref[x] + alpha3 * p).reshape(64, 128)
        rs_ref[pl.ds(64 * x, 64), :] = (r_ref[x] - alpha3 * s).reshape(64, 128)
    for x in range(4):
        for s in range(8):
            part = slice(s * 128, (s + 1) * 128)
            xo_ref[x, :, part] = xs_ref[pl.ds(64 * x + s, 8, stride=8), :]
            ro_ref[x, :, part] = rs_ref[pl.ds(64 * x + s, 8, stride=8), :]


def bodied(body, first):
    def run(*refs):
        body(first, *refs)

    return run


def local(right_side, diagonal, aggregate_id, coarse_diag, coarse_link):
    count_x, count_y = lax.axis_size("px"), lax.axis_size("py")
    me = jnp.stack([lax.axis_index("px"), lax.axis_index("py"), count_x - 1, count_y - 1]).astype(jnp.int32)

    def both_ways(low, high, axis, far=1):
        count = lax.axis_size(axis)
        up = [(i, (i + far) % count) for i in range(count)]
        down = [(b, a) for a, b in up]
        return lax.ppermute(high, axis, up), lax.ppermute(low, axis, down)

    def around(value, axis):
        one_low, one_high = both_ways(value, value, axis)
        two_low, two_high = both_ways(value, value, axis, 2)
        return two_low, one_low, value, one_high, two_high

    def gather(value, axis):
        return lax.all_to_all(value, axis, 0, 0)

    two, field = (2, 8, 8, 128), (4, 8, 8, 128)
    low, high = call(enter_body, [(448, 128)] * 2, right_side, diagonal, aggregate_id, scalars=0)
    low, high = low.reshape(7, 8, 8, 128), high.reshape(7, 8, 8, 128)
    xlow, xhigh = both_ways(low, high, "px")
    first, last = call(pack_first_body, [(62, 8, 128)] * 2, low, high, xlow, xhigh, scalars=0)
    ylow, yhigh = both_ways(first, last, "py")
    inverse, scale, offset = call(
        setup_body, [(8, 12, 8, 128), (6, 10, 8, 128), (10, 14, 8, 128)], me, low, high, xlow, xhigh, ylow, yhigh
    )
    mid = (6, 10, 8, 128)
    smooth, remain, send = call(
        bodied(restrict_body, True), [mid, mid, (24, 128)],
        low, high, xlow, xhigh, ylow, yhigh, inverse, offset, coarse_diag, coarse_link, scalars=0,
    )
    send, = call(window_first_body, [(112, 128)], *around(send, "px"), scalars=0)
    pieces = around(send, "py")
    coef, = call(coarse_setup_body, [(7, 8, 16, 128)], me, *pieces)
    fixed = (inverse, scale, offset)
    z, wlow, whigh, dots = call(
        begin_body, [field, two, two, (1, 128)], *pieces, coef, smooth, remain, *fixed, low, high, scalars=0
    )
    state = None
    for iteration in range(ITERS - 1):
        xlow, xhigh = both_ways(wlow, whigh, "px")
        first, last = call(pack_body, [(8, 2, 8, 128)] * 2, wlow, whigh, xlow, xhigh, scalars=0)
        ylow, yhigh = both_ways(first, last, "py")
        smooth, remain, send = call(
            bodied(restrict_body, False), [mid, mid, (count_x, 8, 128)],
            wlow, whigh, xlow, xhigh, ylow, yhigh, inverse, offset, dots, scalars=0,
        )
        send, = call(window_body, [(count_y, 32, 128)], me, gather(send, "px"))
        got = gather(send, "py")
        more = (low, high) if state is None else state
        z, wlow, whigh, x, r, p, s, q, t, dots, keep = call(
            bodied(step_body, state is None), [field, two, two] + [field] * 6 + [(1, 128)] * 2,
            me, got, coef, smooth, remain, *fixed, z, wlow, whigh, *more,
        )
        state = (x, r, p, s, q, t, keep)
    send, = call(spread_dots_body, [(count_x, 8, 128)], dots, scalars=0)
    send, = call(sum_dots_body, [(count_y, 8, 128)], gather(send, "px"), scalars=0)
    got = gather(send, "py")
    return tuple(call(
        finish_body, [right_side.shape] * 2, got, z, wlow, whigh, x, r, p, s, keep,
        scalars=0, scratch=[pltpu.VMEM((256, 128), F32)] * 2,
    ))


def solution(mesh):
    cells = P("px", "py", None)
    in_specs = (cells, cells, cells, cells, P(None, "px", "py", None))
    return jax.shard_map(local, mesh=mesh, in_specs=in_specs, out_specs=(cells, cells), check_vma=False)
```

```python
import jax
import jax.numpy as jnp
from jax import lax
from jax.experimental import pallas as pl
from jax.experimental.pallas import tpu as pltpu
from jax.sharding import PartitionSpec as P

OMEGA = 2.0 / 3.0
REST = 1.0 - OMEGA
FACES = (32.0, 16.0, 8.0)
F32 = jnp.float32


def call(body, outs, *args, scalars=1, scratch=(), flops=2_000_000):
    smem = pl.BlockSpec(memory_space=pltpu.SMEM)
    vmem = pl.BlockSpec(memory_space=pltpu.VMEM)
    specs = [smem] * scalars + [vmem] * (len(args) - scalars)
    return pl.pallas_call(
        body,
        out_shape=[jax.ShapeDtypeStruct(shape, F32) for shape in outs],
        in_specs=specs,
        out_specs=[vmem] * len(outs),
        scratch_shapes=list(scratch),
        compiler_params=pltpu.CompilerParams(vmem_limit_bytes=20 * 1024 * 1024),
        cost_estimate=pl.CostEstimate(flops=flops, bytes_accessed=1_000_000, transcendentals=0),
    )(*args)


def along_z(value):
    lane = lax.broadcasted_iota(jnp.int32, value.shape, value.ndim - 1)
    sub = lax.broadcasted_iota(jnp.int32, value.shape, value.ndim - 2)
    after = pltpu.roll(value, 127, value.ndim - 1)
    before = pltpu.roll(value, 1, value.ndim - 1)
    after_row = jnp.where(sub == 7, 0.0, pltpu.roll(after, 7, value.ndim - 2))
    before_row = jnp.where(sub == 0, 0.0, pltpu.roll(before, 1, value.ndim - 2))
    return jnp.where(lane == 127, after_row, after) + jnp.where(lane == 0, before_row, before)


def by_eight(value, ahead):
    lane = lax.broadcasted_iota(jnp.int32, value.shape, value.ndim - 1)
    if ahead:
        moved = pltpu.roll(value, 120, value.ndim - 1)
        return jnp.where(lane >= 120, pltpu.roll(moved, 7, value.ndim - 2), moved)
    moved = pltpu.roll(value, 8, value.ndim - 1)
    return jnp.where(lane < 8, pltpu.roll(moved, 1, value.ndim - 2), moved)


def beside(below, here, above):
    count = here.shape[0]
    inner = here[1 : count - 1]
    return below + above + here[0 : count - 2] + here[2:count] + along_z(inner)


def enter_body(b_ref, d_ref, a_ref, low_ref, high_ref):
    lane = lax.broadcasted_iota(jnp.int32, (8, 128), 1)
    for x in range(4):
        for s in range(8):
            part = slice(s * 128, (s + 1) * 128)
            b = b_ref[x, :, part]
            d = d_ref[x, :, part]
            home = (lane + s * 128) // 8
            o = ((a_ref[x, :, part] & 127) - home).astype(F32)
            ref = low_ref if x < 2 else high_ref
            at = (x % 2) * 64 + s
            ref[pl.ds(at, 8, stride=8), :] = b
            ref[pl.ds(128 + at, 8, stride=8), :] = d
            if x < 3:
                low_ref[pl.ds(256 + x * 64 + s, 8, stride=8), :] = o
            if x > 0:
                high_ref[pl.ds(256 + (x - 1) * 64 + s, 8, stride=8), :] = o


def field_rows(low, high, xlow, xhigh, base):
    return [ref.at[base + k] for ref in (xlow, low, high, xhigh) for k in range(2)]


def offset_rows(low, high, xlow, xhigh):
    return [ref.at[4 + k] for ref, ks in ((xlow, (0, 1, 2)), (low, (0, 1, 2)), (high, (2,)), (xhigh, (0, 1, 2))) for k in ks]


def pack_first_body(low_ref, high_ref, xlow_ref, xhigh_ref, first_ref, last_ref):
    four = (low_ref, high_ref, xlow_ref, xhigh_ref)
    for f in range(2):
        for x, ref in enumerate(field_rows(*four, 2 * f)):
            at = 16 * f + 2 * x
            first_ref[at : at + 2] = ref[0:2]
            last_ref[at : at + 2] = ref[6:8]
    for x, ref in enumerate(offset_rows(*four)):
        at = 32 + 3 * x
        first_ref[at : at + 3] = ref[0:3]
        last_ref[at : at + 3] = ref[5:8]


def setup_body(me_ref, low_ref, high_ref, xlow_ref, xhigh_ref, ylow_ref, yhigh_ref, inverse_ref, scale_ref, offset_ref):
    px, py, last_x, last_y = me_ref[0], me_ref[1], me_ref[2], me_ref[3]
    below = jnp.where(px > 0, 1.0, 0.0).astype(F32)
    above = jnp.where(px < last_x, 1.0, 0.0).astype(F32)
    left = jnp.where(py > 0, 1.0, 0.0).astype(F32)
    right = jnp.where(py < last_y, 1.0, 0.0).astype(F32)
    four = (low_ref, high_ref, xlow_ref, xhigh_ref)
    for x, ref in enumerate(field_rows(*four, 2)):
        s_mid = 6.0 + ref[...]
        s_left = 6.0 + ylow_ref[16 + 2 * x : 18 + 2 * x]
        s_right = 6.0 + yhigh_ref[16 + 2 * x : 18 + 2 * x]
        i_mid, i_left, i_right = 1.0 / s_mid, left / s_left, right / s_right
        if x < 2 or x > 5:
            seen = below if x < 2 else above
            i_mid, i_left, i_right = i_mid * seen, i_left * seen, i_right * seen
        inverse_ref[x, 0:2] = i_left
        inverse_ref[x, 2:10] = i_mid
        inverse_ref[x, 10:12] = i_right
        if 1 <= x <= 6:
            scale_ref[x - 1, 0:1] = s_left[1:2]
            scale_ref[x - 1, 1:9] = s_mid
            scale_ref[x - 1, 9:10] = s_right[0:1]
    for x, ref in enumerate(offset_rows(*four)):
        offset_ref[x, 0:3] = ylow_ref[32 + 3 * x : 35 + 3 * x]
        offset_ref[x, 3:11] = ref[...]
        offset_ref[x, 11:14] = yhigh_ref[32 + 3 * x : 35 + 3 * x]


def pack_body(low_ref, high_ref, xlow_ref, xhigh_ref, first_ref, last_ref):
    for r, ref in enumerate((xlow_ref, low_ref, high_ref, xhigh_ref)):
        for k in range(2):
            first_ref[2 * r + k] = ref[k, 0:2]
            last_ref[2 * r + k] = ref[k, 6:8]


def restrict_body(mode, *refs):
    low, high, xlow, xhigh, ylow, yhigh, inverse_ref, offset_ref = refs[:8]
    smooth_ref, remain_ref, send_ref = refs[-3:]
    first = mode == 0
    mids = [ref.at[k] for ref in (xlow, low, high, xhigh) for k in range(2)]

    def vector(x):
        if first:
            sides = ylow[2 * x : 2 * x + 2], yhigh[2 * x : 2 * x + 2]
        else:
            sides = ylow[x], yhigh[x]
        return jnp.concatenate([sides[0], mids[x][...], sides[1]], axis=0)

    smooth = [OMEGA * vector(x) * inverse_ref[x] for x in range(8)]
    shrunk = []
    remains = []
    for x in range(1, 7):
        near = beside(smooth[x - 1][1:11], smooth[x], smooth[x + 1][1:11])
        remain = REST * vector(x)[1:11] + near
        smooth_ref[x - 1] = smooth[x][1:11]
        remain_ref[x - 1] = remain
        remains.append(remain[1:9])
        shrunk.append(remain * inverse_ref[x, 1:11])
    sums = []
    for big_x in range(2):
        parts = []
        for x in (2 * big_x, 2 * big_x + 1):
            near = beside(shrunk[x][1:9], shrunk[x + 1], shrunk[x + 2][1:9])
            reduced = REST * remains[x + 1] + OMEGA * near
            offset = offset_ref[x + 3, 3:11]
            parts.append((
                jnp.where(jnp.abs(offset) < 0.5, reduced, 0.0),
                jnp.where(offset > 0.5, reduced, 0.0),
                jnp.where(offset < -0.5, reduced, 0.0),
            ))
        for big_y in range(2):
            cols = slice(4 * big_y, 4 * big_y + 4)
            here, up, down = (
                jnp.sum(parts[0][k][cols], axis=0) + jnp.sum(parts[1][k][cols], axis=0) for k in range(3)
            )
            sums.append(here + by_eight(up, False) + by_eight(down, True))
    stacked = jnp.concatenate(sums, axis=0)
    row = lax.broadcasted_iota(jnp.int32, (128, 128), 0)
    col = lax.broadcasted_iota(jnp.int32, (128, 128), 1)
    group = jnp.where(row // 8 == col % 16, 1.0, 0.0).astype(F32)
    grouped = jnp.dot(stacked, group, preferred_element_type=F32, precision=lax.Precision.HIGHEST)
    sub = lax.broadcasted_iota(jnp.int32, (8, 128), 0)
    lane = lax.broadcasted_iota(jnp.int32, (8, 128), 1)
    rows = [
        jnp.sum(jnp.where(lane // 16 == sub, grouped[8 * c : 8 * c + 8], 0.0), axis=0, keepdims=True)
        for c in range(4)
    ]
    zero = jnp.zeros((1, 128), F32)
    rows = rows + ([refs[8][...]] if mode == 2 else [zero]) + [zero] * 3
    tile = jnp.concatenate(rows, axis=0)
    if mode == 0:
        cdiag_ref, link_ref = refs[8:10]
        send_ref[0:8] = tile
        more = [cdiag_ref[c // 2, c % 2 : c % 2 + 1, :] for c in range(4)]
        for f in range(3):
            more = more + [FACES[f] * link_ref[f, c // 2, c % 2 : c % 2 + 1, :] for c in range(4)]
        send_ref[8:24] = jnp.concatenate(more, axis=0)
    elif mode == 1:
        send_ref[...] = tile
    else:
        for j in range(send_ref.shape[0]):
            send_ref[j] = tile


def window_rows(pieces, start):
    return [
        [ref[start + 2 * big_x + big_y : start + 2 * big_x + big_y + 1, :] for ref in pieces for big_x in range(2)]
        for big_y in range(2)
    ]


def window_near_body(*refs):
    pieces, send_ref = refs[:5], refs[5]
    zero = jnp.zeros((6, 128), F32)
    early, late = window_rows(pieces, 0)
    send_ref[0:32] = jnp.concatenate(early + [zero] + late + [zero], axis=0)
    if send_ref.shape[0] > 32:
        rows = []
        for f in range(4):
            early, late = window_rows(pieces, 8 + 4 * f)
            rows = rows + early + late
        send_ref[32:112] = jnp.concatenate(rows, axis=0)


def window_body(me_ref, got_ref, send_ref):
    px, last_x = me_ref[0], me_ref[2]
    total, rest = total_of(got_ref, 4, None)
    zero = jnp.zeros((4, 128), F32)
    early, late = window_rows([got_ref.at[jnp.clip(px + d, 0, last_x)] for d in range(-2, 3)], 0)
    tile = jnp.concatenate(early + [total, rest, zero] + late + [total, rest, zero], axis=0)
    for j in range(send_ref.shape[0]):
        send_ref[j] = tile


SPOTS = ((-2, 1), (-1, 0), (-1, 1), (0, 0), (0, 1), (1, 0), (1, 1), (2, 0))


def shift_x(value, ahead):
    return pltpu.roll(value, 15 if ahead else 1, 0)


def shift_k(value, ahead):
    return pltpu.roll(value, 127 if ahead else 1, 1)


def coarse_setup_body(me_ref, *refs):
    pieces, coef_ref = refs[:5], refs[5]
    px, py, last_x, last_y = me_ref[0], me_ref[1], me_ref[2], me_ref[3]
    row = lax.broadcasted_iota(jnp.int32, (16, 128), 0)
    lane = lax.broadcasted_iota(jnp.int32, (16, 128), 1)
    pad = jnp.zeros((6, 128), F32)
    where_x = 2 * px - 4 + row
    inside_x = (where_x >= 0) & (where_x < 2 * (last_x + 1)) & (row < 10)

    def take(y, f):
        d, big_y = SPOTS[y]
        start = 32 + 20 * f + 10 * big_y
        return jnp.concatenate([pieces[d + 2][start : start + 10, :], pad], axis=0)

    links = [[take(y, f) for y in range(8)] for f in range(1, 4)]
    for y in range(8):
        where_y = 2 * py - 3 + y
        seen = jnp.where((where_y >= 0) & (where_y < 2 * (last_y + 1)), 1.0, 0.0).astype(F32)
        diag = jnp.where(inside_x, take(y, 0), 1.0)
        inverse = jnp.where(inside_x, seen / diag, 0.0)
        coef_ref[0, y] = inverse
        if 1 <= y <= 6:
            coef_ref[1, y] = links[0][y] * inverse
            coef_ref[2, y] = shift_x(links[0][y], False) * inverse
            coef_ref[3, y] = links[1][y] * inverse
            coef_ref[4, y] = links[1][y - 1] * inverse
            coef_ref[5, y] = jnp.where(lane < 127, links[2][y] * inverse, 0.0)
            coef_ref[6, y] = jnp.where(lane > 0, shift_k(links[2][y], False) * inverse, 0.0)
        else:
            for f in range(1, 7):
                coef_ref[f, y] = jnp.zeros((16, 128), F32)


def dots_of(pairs):
    lane = lax.broadcasted_iota(jnp.int32, (1, 128), 1)
    out = jnp.zeros((1, 128), F32)
    for k, value in enumerate(pairs):
        out = jnp.where(lane == k, jnp.sum(value), out)
    return out


def correct_rows(pieces, coef_ref, smooth_ref, remain_ref, inverse_ref, scale_ref, offset_ref):
    start = [
        pieces[d + 2][16 * big_y : 16 * big_y + 16, :] * coef_ref[0, y] for y, (d, big_y) in enumerate(SPOTS)
    ]

    def sweep(now, y):
        here = now[y]
        total = start[y] + coef_ref[1, y] * shift_x(here, True) + coef_ref[2, y] * shift_x(here, False)
        total = total + coef_ref[3, y] * now[y + 1] + coef_ref[4, y] * now[y - 1]
        return total + coef_ref[5, y] * shift_k(here, True) + coef_ref[6, y] * shift_k(here, False)

    second = [None] + [sweep(start, y) for y in range(1, 7)] + [None]
    third = [None, None] + [sweep(second, y) for y in range(2, 6)]
    sub = lax.broadcasted_iota(jnp.int32, (8, 128), 0)
    lane = lax.broadcasted_iota(jnp.int32, (8, 128), 1)
    index = sub * 16 + lane // 8

    def spread_out(tile, x):
        wide = jnp.broadcast_to(tile[x + 4 : x + 5, :], (8, 128))
        return jnp.take_along_axis(wide, index, axis=1)

    tables = [[], [], []]
    for y in range(2, 6):
        for k, tile in enumerate((third[y], shift_k(third[y], True), shift_k(third[y], False))):
            tables[k].append([spread_out(tile, x) for x in range(-2, 4)])
    counts = (3, 4, 4, 3)

    def lifted(x):
        big_x = x // 2
        here, up, down = (
            jnp.concatenate(
                [jnp.broadcast_to(tables[k][y][big_x + 2][None], (counts[y], 8, 128)) for y in range(4)], axis=0
            )
            for k in range(3)
        )
        offset = offset_ref[x + 3]
        return jnp.where(offset > 0.5, up, jnp.where(offset < -0.5, down, here))

    lifts = [lifted(x) for x in range(-3, 7)]
    spreads = []
    for x in range(8):
        near = beside(lifts[x][1:13], lifts[x + 1], lifts[x + 2][1:13])
        spreads.append(REST * lifts[x + 1][1:13] + OMEGA * (inverse_ref[x] * near))
    shaped = []
    for x in range(6):
        near = beside(spreads[x][1:11], spreads[x + 1], spreads[x + 2][1:11])
        spread = spreads[x + 1][1:11]
        left = remain_ref[x] - (scale_ref[x] * spread - near)
        shaped.append(smooth_ref[x] + spread + OMEGA * (inverse_ref[x + 1, 1:11] * left))
    for x in range(4):
        near = beside(shaped[x][1:9], shaped[x + 1], shaped[x + 2][1:9])
        own = shaped[x + 1][1:9]
        yield x, own, scale_ref[x + 1, 1:9] * own - near


def put(low_ref, high_ref, x, value):
    (low_ref if x < 2 else high_ref)[x % 2] = value


def half(low_ref, high_ref, x):
    return (low_ref if x < 2 else high_ref)[x % 2]


def products(left, right):
    return [jnp.sum(a * b, axis=0) for a in left for b in right]


def begin_body(*refs):
    pieces, fixed, (z_ref, wlow_ref, whigh_ref) = refs[:5], refs[5:11], refs[11:]
    for x, z, w in correct_rows(pieces, *fixed):
        z_ref[x] = z
        put(wlow_ref, whigh_ref, x, w)


def second_body(*refs):
    pieces, fixed, refs = refs[:5], refs[5:11], refs[11:]
    low_ref, high_ref, z_ref, wlow_ref, whigh_ref, m_ref, nlow_ref, nhigh_ref, dots_ref = refs
    sums = [jnp.zeros((8, 128), F32)] * 6
    for x, m, n in correct_rows(pieces, *fixed):
        m_ref[x] = m
        put(nlow_ref, nhigh_ref, x, n)
        here = products((half(low_ref, high_ref, x), half(wlow_ref, whigh_ref, x), n), (z_ref[x], m))
        sums = [a + b for a, b in zip(sums, here)]
    dots_ref[...] = dots_of(sums)


def fourth_body(*refs):
    pieces, fixed, refs = refs[:5], refs[5:11], refs[11:]
    z_ref, wlow_ref, whigh_ref, r_ref, s_ref, q_ref, t_ref, m_ref, n_ref, dots_ref = refs
    sums = [jnp.zeros((8, 128), F32)] * 15
    for x, m, n in correct_rows(pieces, *fixed):
        m_ref[x] = m
        n_ref[x] = n
        here = products((r_ref[x], half(wlow_ref, whigh_ref, x), s_ref[x], n, t_ref[x]), (z_ref[x], m, q_ref[x]))
        sums = [a + b for a, b in zip(sums, here)]
    dots_ref[...] = dots_of(sums)


def two_sum(a, b):
    total = a + b
    part = total - a
    return total, (a - (total - part)) + (b - part)


def split(a):
    wide = a * 4097.0
    high = wide - (wide - a)
    return high, a - high


def two_product(a, b):
    product = a * b
    a_high, a_low = split(a)
    b_high, b_low = split(b)
    return product, a_low * b_low - (((product - a_high * b_high) - a_low * b_high) - a_high * b_low)


def pair_add(a, b):
    total, rest = two_sum(a[0], b[0])
    return two_sum(total, rest + (a[1] + b[1]))


def pair_scale(a, factor):
    product, rest = two_product(a[0], factor)
    return two_sum(product, rest + a[1] * factor)


def pair_times(a, b):
    product, rest = two_product(a[0], b[0])
    return two_sum(product, rest + (a[0] * b[1] + a[1] * b[0]))


def total_of(got_ref, row, rest_row):
    total = got_ref[0, row : row + 1, :]
    rest = jnp.zeros((1, 128), F32) if rest_row is None else got_ref[0, rest_row : rest_row + 1, :]
    for j in range(1, got_ref.shape[0]):
        total, lost = two_sum(total, got_ref[j, row : row + 1, :])
        rest = rest + lost
        if rest_row is not None:
            rest = rest + got_ref[j, rest_row : rest_row + 1, :]
    return total, rest


def pairs_of(got_ref, row, rest_row, count):
    total, rest = total_of(got_ref, row, rest_row)
    total, rest = two_sum(total, rest)
    return [
        (jnp.broadcast_to(total[:, k : k + 1], (1, 128)), jnp.broadcast_to(rest[:, k : k + 1], (1, 128)))
        for k in range(count)
    ]


def form(table, left, weights):
    out = None
    for i, row in enumerate(left):
        for j, entry in enumerate(table[row]):
            factor = None
            for w in (weights[i], weights[j]):
                if w is not None:
                    factor = w if factor is None else pair_times(factor, w)
            term = entry if factor is None else pair_times(entry, factor)
            out = term if out is None else pair_add(out, term)
    return out[0] + out[1]


def tiled(row):
    return jnp.broadcast_to(row, (8, 128))[None]


def negated(pair):
    return -pair[0], -pair[1]


def merge_body(me_ref, got_ref, *refs):
    py, last_y = me_ref[1], me_ref[3]
    pieces = [got_ref.at[jnp.clip(py + d, 0, last_y)] for d in range(-2, 3)]
    fixed, refs = refs[:6], refs[6:]
    low_ref, high_ref, z_ref, wlow_ref, whigh_ref, m_ref, nlow_ref, nhigh_ref = refs[:8]
    zo_ref, wolow_ref, wohigh_ref, xo_ref, ro_ref, po_ref, so_ref, qo_ref, to_ref, keep_ref = refs[8:]
    sums = pairs_of(got_ref, 10, 11, 6)
    table = [sums[0:2], sums[2:4], sums[4:6]]
    gamma0 = table[0][0][0]
    alpha0 = gamma0 / table[1][0][0]
    weights = (None, negated((alpha0, jnp.zeros_like(alpha0))))
    gamma1 = form(table, (0, 1), weights)
    delta1 = form(table, (1, 2), weights)
    beta1 = gamma1 / gamma0
    alpha1 = gamma1 / (delta1 - beta1 * gamma1 / alpha0)
    lane = lax.broadcasted_iota(jnp.int32, (1, 128), 1)
    keep_ref[...] = jnp.where(lane == 0, gamma1, jnp.where(lane == 1, alpha1, 0.0))
    alpha0, alpha1, beta1 = tiled(alpha0), tiled(alpha1), tiled(beta1)
    for x, k, l in correct_rows(pieces, *fixed):
        z0, w0 = z_ref[x], half(wlow_ref, whigh_ref, x)
        m0, n0 = m_ref[x], half(nlow_ref, nhigh_ref, x)
        z1, w1 = z0 - alpha0 * m0, w0 - alpha0 * n0
        p, s = z1 + beta1 * z0, w1 + beta1 * w0
        q = (m0 - alpha0 * k) + beta1 * m0
        t = (n0 - alpha0 * l) + beta1 * n0
        xo_ref[x] = alpha0 * z0 + alpha1 * p
        ro_ref[x] = (half(low_ref, high_ref, x) - alpha0 * w0) - alpha1 * s
        zo_ref[x] = z1 - alpha1 * q
        put(wolow_ref, wohigh_ref, x, w1 - alpha1 * t)
        po_ref[x], so_ref[x], qo_ref[x], to_ref[x] = p, s, q, t


def spread_dots_body(dots_ref, send_ref):
    tile = jnp.concatenate([dots_ref[...], jnp.zeros((7, 128), F32)], axis=0)
    for j in range(send_ref.shape[0]):
        send_ref[j] = tile


def sum_dots_body(got_ref, send_ref):
    total, rest = total_of(got_ref, 0, None)
    tile = jnp.concatenate([total, rest, jnp.zeros((6, 128), F32)], axis=0)
    for j in range(send_ref.shape[0]):
        send_ref[j] = tile


def finish_body(got_ref, z_ref, wlow_ref, whigh_ref, m_ref, n_ref, x_ref, r_ref, p_ref, s_ref, q_ref, t_ref, keep_ref,
                xo_ref, ro_ref, xs_ref, rs_ref):
    sums = pairs_of(got_ref, 0, 1, 15)
    table = [sums[3 * k : 3 * k + 3] for k in range(5)]
    keep = keep_ref[...]
    gamma1 = jnp.broadcast_to(keep[:, 0:1], (1, 128))
    alpha1 = jnp.broadcast_to(keep[:, 1:2], (1, 128))
    gamma2 = table[0][0][0]
    beta2 = gamma2 / gamma1
    alpha2 = gamma2 / (table[1][0][0] - beta2 * gamma2 / alpha1)
    weights = (None, (-alpha2, jnp.zeros_like(alpha2)), two_product(-alpha2, beta2))
    gamma3 = form(table, (0, 1, 2), weights)
    delta3 = form(table, (1, 3, 4), weights)
    beta3 = gamma3 / gamma2
    alpha3 = gamma3 / (delta3 - beta3 * gamma3 / alpha2)
    alpha2, beta2, alpha3, beta3 = tiled(alpha2), tiled(beta2), tiled(alpha3), tiled(beta3)
    for x in range(4):
        z, w, q1, t1 = z_ref[x], half(wlow_ref, whigh_ref, x), q_ref[x], t_ref[x]
        p2, s2 = z + beta2 * p_ref[x], w + beta2 * s_ref[x]
        q2, t2 = m_ref[x] + beta2 * q1, n_ref[x] + beta2 * t1
        p3 = (z - alpha2 * q2) + beta3 * p2
        s3 = (w - alpha2 * t2) + beta3 * s2
        xs_ref[pl.ds(64 * x, 64), :] = ((x_ref[x] + alpha2 * p2) + alpha3 * p3).reshape(64, 128)
        rs_ref[pl.ds(64 * x, 64), :] = ((r_ref[x] - alpha2 * s2) - alpha3 * s3).reshape(64, 128)
    for x in range(4):
        for s in range(8):
            part = slice(s * 128, (s + 1) * 128)
            xo_ref[x, :, part] = xs_ref[pl.ds(64 * x + s, 8, stride=8), :]
            ro_ref[x, :, part] = rs_ref[pl.ds(64 * x + s, 8, stride=8), :]


def bodied(body, first):
    def run(*refs):
        body(first, *refs)

    return run


def local(right_side, diagonal, aggregate_id, coarse_diag, coarse_link):
    count_x, count_y = lax.axis_size("px"), lax.axis_size("py")
    me = jnp.stack([lax.axis_index("px"), lax.axis_index("py"), count_x - 1, count_y - 1]).astype(jnp.int32)

    def both_ways(low, high, axis, far=1):
        count = lax.axis_size(axis)
        up = [(i, (i + far) % count) for i in range(count)]
        down = [(b, a) for a, b in up]
        return lax.ppermute(high, axis, up), lax.ppermute(low, axis, down)

    def around(value, axis):
        one_low, one_high = both_ways(value, value, axis)
        two_low, two_high = both_ways(value, value, axis, 2)
        return two_low, one_low, value, one_high, two_high

    def gather(value, axis):
        return lax.all_to_all(value, axis, 0, 0)

    two, field = (2, 8, 8, 128), (4, 8, 8, 128)
    low, high = call(enter_body, [(448, 128)] * 2, right_side, diagonal, aggregate_id, scalars=0)
    low, high = low.reshape(7, 8, 8, 128), high.reshape(7, 8, 8, 128)
    xlow, xhigh = both_ways(low, high, "px")
    first, last = call(pack_first_body, [(62, 8, 128)] * 2, low, high, xlow, xhigh, scalars=0)
    ylow, yhigh = both_ways(first, last, "py")
    inverse, scale, offset = call(
        setup_body, [(8, 12, 8, 128), (6, 10, 8, 128), (10, 14, 8, 128)], me, low, high, xlow, xhigh, ylow, yhigh
    )
    mid, dots = (6, 10, 8, 128), (1, 128)
    smooth, remain, send = call(
        bodied(restrict_body, 0), [mid, mid, (24, 128)],
        low, high, xlow, xhigh, ylow, yhigh, inverse, offset, coarse_diag, coarse_link, scalars=0,
    )
    send, = call(window_near_body, [(112, 128)], *around(send, "px"), scalars=0)
    pieces = around(send, "py")
    coef, = call(coarse_setup_body, [(7, 8, 16, 128)], me, *pieces)
    fixed = (inverse, scale, offset)
    z, wlow, whigh = call(begin_body, [field, two, two], *pieces, coef, smooth, remain, *fixed, scalars=0)

    def restricted(mode, low, high, outs, *more):
        xlow, xhigh = both_ways(low, high, "px")
        first, last = call(pack_body, [(8, 2, 8, 128)] * 2, low, high, xlow, xhigh, scalars=0)
        ylow, yhigh = both_ways(first, last, "py")
        return call(
            bodied(restrict_body, mode), [mid, mid, outs],
            low, high, xlow, xhigh, ylow, yhigh, inverse, offset, *more, scalars=0,
        )

    def near_window(send):
        send, = call(window_near_body, [(32, 128)], *around(send, "px"), scalars=0)
        return around(send, "py")

    smooth, remain, send = restricted(1, wlow, whigh, (8, 128))
    m, nlow, nhigh, sums = call(
        second_body, [field, two, two, dots],
        *near_window(send), coef, smooth, remain, *fixed, low, high, z, wlow, whigh, scalars=0,
    )
    smooth, remain, send = restricted(2, nlow, nhigh, (count_x, 8, 128), sums)
    send, = call(window_body, [(count_y, 32, 128)], me, gather(send, "px"))
    z, wlow, whigh, x, r, p, s, q, t, keep = call(
        merge_body, [field, two, two] + [field] * 6 + [dots],
        me, gather(send, "py"), coef, smooth, remain, *fixed, low, high, z, wlow, whigh, m, nlow, nhigh,
    )
    smooth, remain, send = restricted(1, wlow, whigh, (8, 128))
    m, n, sums = call(
        fourth_body, [field, field, dots],
        *near_window(send), coef, smooth, remain, *fixed, z, wlow, whigh, r, s, q, t, scalars=0,
    )
    send, = call(spread_dots_body, [(count_x, 8, 128)], sums, scalars=0)
    send, = call(sum_dots_body, [(count_y, 8, 128)], gather(send, "px"), scalars=0)
    return tuple(call(
        finish_body, [right_side.shape] * 2,
        gather(send, "py"), z, wlow, whigh, m, n, x, r, p, s, q, t, keep,
        scalars=0, scratch=[pltpu.VMEM((256, 128), F32)] * 2,
    ))


def solution(mesh):
    cells = P("px", "py", None)
    in_specs = (cells, cells, cells, cells, P(None, "px", "py", None))
    return jax.shard_map(local, mesh=mesh, in_specs=in_specs, out_specs=(cells, cells), check_vma=False)
```

```python
import jax
import jax.numpy as jnp
from jax import lax
from jax.experimental import pallas as pl
from jax.experimental.pallas import tpu as pltpu
from jax.sharding import PartitionSpec as P

OMEGA = 2.0 / 3.0
REST = 1.0 - OMEGA
FACES = (32.0, 16.0, 8.0)
F32 = jnp.float32


def call(body, outs, *args, scalars=1, scratch=(), flops=2_000_000):
    smem = pl.BlockSpec(memory_space=pltpu.SMEM)
    vmem = pl.BlockSpec(memory_space=pltpu.VMEM)
    specs = [smem] * scalars + [vmem] * (len(args) - scalars)
    return pl.pallas_call(
        body,
        out_shape=[jax.ShapeDtypeStruct(shape, F32) for shape in outs],
        in_specs=specs,
        out_specs=[vmem] * len(outs),
        scratch_shapes=list(scratch),
        compiler_params=pltpu.CompilerParams(vmem_limit_bytes=20 * 1024 * 1024),
        cost_estimate=pl.CostEstimate(flops=flops, bytes_accessed=1_000_000, transcendentals=0),
    )(*args)


def along_z(value):
    lane = lax.broadcasted_iota(jnp.int32, value.shape, value.ndim - 1)
    sub = lax.broadcasted_iota(jnp.int32, value.shape, value.ndim - 2)
    after = pltpu.roll(value, 127, value.ndim - 1)
    before = pltpu.roll(value, 1, value.ndim - 1)
    after_row = jnp.where(sub == 7, 0.0, pltpu.roll(after, 7, value.ndim - 2))
    before_row = jnp.where(sub == 0, 0.0, pltpu.roll(before, 1, value.ndim - 2))
    return jnp.where(lane == 127, after_row, after) + jnp.where(lane == 0, before_row, before)


def by_eight(value, ahead):
    lane = lax.broadcasted_iota(jnp.int32, value.shape, value.ndim - 1)
    if ahead:
        moved = pltpu.roll(value, 120, value.ndim - 1)
        return jnp.where(lane >= 120, pltpu.roll(moved, 7, value.ndim - 2), moved)
    moved = pltpu.roll(value, 8, value.ndim - 1)
    return jnp.where(lane < 8, pltpu.roll(moved, 1, value.ndim - 2), moved)


def beside(below, here, above):
    count = here.shape[0]
    inner = here[1 : count - 1]
    return below + above + here[0 : count - 2] + here[2:count] + along_z(inner)


def enter_body(b_ref, d_ref, a_ref, low_ref, high_ref):
    lane = lax.broadcasted_iota(jnp.int32, (8, 128), 1)
    for x in range(4):
        for s in range(8):
            part = slice(s * 128, (s + 1) * 128)
            b = b_ref[x, :, part]
            d = d_ref[x, :, part]
            home = (lane + s * 128) // 8
            o = ((a_ref[x, :, part] & 127) - home).astype(F32)
            ref = low_ref if x < 2 else high_ref
            at = (x % 2) * 64 + s
            ref[pl.ds(at, 8, stride=8), :] = b
            ref[pl.ds(128 + at, 8, stride=8), :] = d
            if x < 3:
                low_ref[pl.ds(256 + x * 64 + s, 8, stride=8), :] = o
            if x > 0:
                high_ref[pl.ds(256 + (x - 1) * 64 + s, 8, stride=8), :] = o


def field_rows(low, high, xlow, xhigh, base):
    return [ref.at[base + k] for ref in (xlow, low, high, xhigh) for k in range(2)]


def offset_rows(low, high, xlow, xhigh):
    return [ref.at[4 + k] for ref, ks in ((xlow, (0, 1, 2)), (low, (0, 1, 2)), (high, (2,)), (xhigh, (0, 1, 2))) for k in ks]


def pack_first_body(low_ref, high_ref, xlow_ref, xhigh_ref, first_ref, last_ref):
    four = (low_ref, high_ref, xlow_ref, xhigh_ref)
    for f in range(2):
        for x, ref in enumerate(field_rows(*four, 2 * f)):
            at = 16 * f + 2 * x
            first_ref[at : at + 2] = ref[0:2]
            last_ref[at : at + 2] = ref[6:8]
    for x, ref in enumerate(offset_rows(*four)):
        at = 32 + 3 * x
        first_ref[at : at + 3] = ref[0:3]
        last_ref[at : at + 3] = ref[5:8]


def setup_body(me_ref, low_ref, high_ref, xlow_ref, xhigh_ref, ylow_ref, yhigh_ref, inverse_ref, scale_ref, offset_ref):
    px, py, last_x, last_y = me_ref[0], me_ref[1], me_ref[2], me_ref[3]
    below = jnp.where(px > 0, 1.0, 0.0).astype(F32)
    above = jnp.where(px < last_x, 1.0, 0.0).astype(F32)
    left = jnp.where(py > 0, 1.0, 0.0).astype(F32)
    right = jnp.where(py < last_y, 1.0, 0.0).astype(F32)
    four = (low_ref, high_ref, xlow_ref, xhigh_ref)
    for x, ref in enumerate(field_rows(*four, 2)):
        s_mid = 6.0 + ref[...]
        s_left = 6.0 + ylow_ref[16 + 2 * x : 18 + 2 * x]
        s_right = 6.0 + yhigh_ref[16 + 2 * x : 18 + 2 * x]
        i_mid, i_left, i_right = 1.0 / s_mid, left / s_left, right / s_right
        if x < 2 or x > 5:
            seen = below if x < 2 else above
            i_mid, i_left, i_right = i_mid * seen, i_left * seen, i_right * seen
        inverse_ref[x, 0:2] = i_left
        inverse_ref[x, 2:10] = i_mid
        inverse_ref[x, 10:12] = i_right
        if 1 <= x <= 6:
            scale_ref[x - 1, 0:1] = s_left[1:2]
            scale_ref[x - 1, 1:9] = s_mid
            scale_ref[x - 1, 9:10] = s_right[0:1]
    for x, ref in enumerate(offset_rows(*four)):
        offset_ref[x, 0:3] = ylow_ref[32 + 3 * x : 35 + 3 * x]
        offset_ref[x, 3:11] = ref[...]
        offset_ref[x, 11:14] = yhigh_ref[32 + 3 * x : 35 + 3 * x]


def padded(value, width):
    zero = jnp.zeros((width, 8, 128), F32)
    return jnp.concatenate([zero, value, zero], axis=0)


def contribute_body(low_ref, high_ref, inverse_ref, offset_ref, send_ref):
    vector = [half(low_ref, high_ref, x) for x in range(4)]
    smooth = [OMEGA * vector[x] * inverse_ref[x + 2, 2:10] for x in range(4)]
    remains = [padded(smooth[0], 1)]
    for x in range(4):
        around = padded(smooth[x], 1)
        center = REST * vector[x] + (around[0:8] + around[2:10] + along_z(smooth[x]))
        for other in (x - 1, x + 1):
            if 0 <= other < 4:
                center = center + smooth[other]
        remains.append(jnp.concatenate([smooth[x][0:1], center, smooth[x][7:8]], axis=0))
    remains.append(padded(smooth[3], 1))
    shrunk = [remains[x] * inverse_ref[x + 1, 1:11] for x in range(6)]
    cells = []
    for x in range(8):
        near = None
        for other in (x - 2, x):
            if 0 <= other < 6:
                near = shrunk[other] if near is None else near + shrunk[other]
        if 1 <= x <= 6:
            near = padded(near + along_z(shrunk[x - 1]), 1)
            wide = padded(shrunk[x - 1], 2)
            value = REST * padded(remains[x - 1], 1) + OMEGA * (near + (wide[0:12] + wide[2:14]))
        else:
            value = padded(OMEGA * near, 1)
        value = jnp.where(inverse_ref[x] > 0.0, value, 0.0)
        offset = offset_ref[x + 1, 1:13]
        cells.append((
            jnp.where(jnp.abs(offset) < 0.5, value, 0.0),
            jnp.where(offset > 0.5, value, 0.0),
            jnp.where(offset < -0.5, value, 0.0),
        ))
    sums = []
    for start, stop in ((0, 2), (2, 6), (6, 10), (10, 12)):
        for i in range(4):
            here, up, down = (
                jnp.sum(cells[2 * i][k][start:stop], axis=0) + jnp.sum(cells[2 * i + 1][k][start:stop], axis=0)
                for k in range(3)
            )
            sums.append(here + by_eight(up, False) + by_eight(down, True))
    send_ref[...] = jnp.concatenate(grouped_rows(sums), axis=0)


def grouped_rows(sums):
    stacked = jnp.concatenate(sums, axis=0)
    row = lax.broadcasted_iota(jnp.int32, (128, 128), 0)
    col = lax.broadcasted_iota(jnp.int32, (128, 128), 1)
    group = jnp.where(row // 8 == col % 16, 1.0, 0.0).astype(F32)
    grouped = jnp.dot(stacked, group, preferred_element_type=F32, precision=lax.Precision.HIGHEST)
    sub = lax.broadcasted_iota(jnp.int32, (8, 128), 0)
    lane = lax.broadcasted_iota(jnp.int32, (8, 128), 1)
    return [
        jnp.sum(jnp.where(lane // 16 == sub, grouped[8 * c : 8 * c + 8], 0.0), axis=0, keepdims=True)
        for c in range(len(sums))
    ]


def pack_body(low_ref, high_ref, xlow_ref, xhigh_ref, *refs):
    pieces, (first_ref, last_ref, window_ref) = refs[:7], refs[7:]
    for r, ref in enumerate((xlow_ref, low_ref, high_ref, xhigh_ref)):
        for k in range(2):
            first_ref[2 * r + k] = ref[k, 0:2]
            last_ref[2 * r + k] = ref[k, 6:8]
    zero = jnp.zeros((6, 128), F32)
    for j in range(4):
        def row(d, i):
            return pieces[d + 3][4 * j + i : 4 * j + i + 1, :]

        rows = []
        for d in range(-2, 3):
            rows.append(row(d, 1) + row(d - 1, 3))
            rows.append(row(d, 2) + row(d + 1, 0))
        window_ref[16 * j : 16 * j + 16] = jnp.concatenate(rows + [zero], axis=0)


def smoothed_rows(vector, inverse_ref):
    smooth = [OMEGA * vector(x) * inverse_ref[x] for x in range(8)]
    remains = [
        REST * vector(x)[1:11] + beside(smooth[x - 1][1:11], smooth[x], smooth[x + 1][1:11]) for x in range(1, 7)
    ]
    return [smooth[x][1:11] for x in range(1, 7)], remains


def smoothed(low, high, xlow, xhigh, ylow, yhigh, inverse_ref):
    mids = [ref.at[k] for ref in (xlow, low, high, xhigh) for k in range(2)]
    return smoothed_rows(lambda x: jnp.concatenate([ylow[x], mids[x][...], yhigh[x]], axis=0), inverse_ref)


def restrict_body(low, high, xlow, xhigh, ylow, yhigh, inverse_ref, offset_ref, cdiag_ref, link_ref,
                  smooth_ref, remain_ref, send_ref):
    mids = [ref.at[k] for ref in (xlow, low, high, xhigh) for k in range(2)]

    def vector(x):
        return jnp.concatenate([ylow[2 * x : 2 * x + 2], mids[x][...], yhigh[2 * x : 2 * x + 2]], axis=0)

    smooth, full = smoothed_rows(vector, inverse_ref)
    shrunk, remains = [], []
    for x in range(6):
        smooth_ref[x] = smooth[x]
        remain_ref[x] = full[x]
        remains.append(full[x][1:9])
        shrunk.append(full[x] * inverse_ref[x + 1, 1:11])
    sums = []
    for big_x in range(2):
        parts = []
        for x in (2 * big_x, 2 * big_x + 1):
            near = beside(shrunk[x][1:9], shrunk[x + 1], shrunk[x + 2][1:9])
            reduced = REST * remains[x + 1] + OMEGA * near
            offset = offset_ref[x + 3, 3:11]
            parts.append((
                jnp.where(jnp.abs(offset) < 0.5, reduced, 0.0),
                jnp.where(offset > 0.5, reduced, 0.0),
                jnp.where(offset < -0.5, reduced, 0.0),
            ))
        for big_y in range(2):
            cols = slice(4 * big_y, 4 * big_y + 4)
            here, up, down = (
                jnp.sum(parts[0][k][cols], axis=0) + jnp.sum(parts[1][k][cols], axis=0) for k in range(3)
            )
            sums.append(here + by_eight(up, False) + by_eight(down, True))
    rows = grouped_rows(sums) + [jnp.zeros((4, 128), F32)]
    for ref in (cdiag_ref, link_ref.at[0], link_ref.at[1], link_ref.at[2]):
        rows = rows + [ref[c // 2, c % 2 : c % 2 + 1, :] for c in range(4)]
    send_ref[...] = jnp.concatenate(rows, axis=0)


def window_rows(pieces, start):
    return [
        [ref[start + 2 * big_x + big_y : start + 2 * big_x + big_y + 1, :] for ref in pieces for big_x in range(2)]
        for big_y in range(2)
    ]


def window_first_body(*refs):
    pieces, send_ref = refs[:5], refs[5]
    zero = jnp.zeros((6, 128), F32)
    early, late = window_rows(pieces, 0)
    send_ref[0:32] = jnp.concatenate(early + [zero] + late + [zero], axis=0)
    rows = []
    for f in range(4):
        early, late = window_rows(pieces, 8 + 4 * f)
        rows = rows + early + late
    send_ref[32:112] = jnp.concatenate(rows, axis=0)


SPOTS = ((-2, 1), (-1, 0), (-1, 1), (0, 0), (0, 1), (1, 0), (1, 1), (2, 0))


def shift_x(value, ahead):
    return pltpu.roll(value, 15 if ahead else 1, 0)


def shift_k(value, ahead):
    return pltpu.roll(value, 127 if ahead else 1, 1)


def coarse_setup_body(me_ref, *refs):
    pieces, coef_ref = refs[:5], refs[5]
    px, py, last_x, last_y = me_ref[0], me_ref[1], me_ref[2], me_ref[3]
    row = lax.broadcasted_iota(jnp.int32, (16, 128), 0)
    lane = lax.broadcasted_iota(jnp.int32, (16, 128), 1)
    pad = jnp.zeros((6, 128), F32)
    where_x = 2 * px - 4 + row
    inside_x = (where_x >= 0) & (where_x < 2 * (last_x + 1)) & (row < 10)

    def take(y, f):
        d, big_y = SPOTS[y]
        start = 32 + 20 * f + 10 * big_y
        return jnp.concatenate([pieces[d + 2][start : start + 10, :], pad], axis=0)

    links = [[FACES[f - 1] * take(y, f) for y in range(8)] for f in range(1, 4)]
    for y in range(8):
        where_y = 2 * py - 3 + y
        seen = jnp.where((where_y >= 0) & (where_y < 2 * (last_y + 1)), 1.0, 0.0).astype(F32)
        diag = jnp.where(inside_x, take(y, 0), 1.0)
        inverse = jnp.where(inside_x, seen / diag, 0.0)
        coef_ref[0, y] = inverse
        if 1 <= y <= 6:
            coef_ref[1, y] = links[0][y] * inverse
            coef_ref[2, y] = shift_x(links[0][y], False) * inverse
            coef_ref[3, y] = links[1][y] * inverse
            coef_ref[4, y] = links[1][y - 1] * inverse
            coef_ref[5, y] = jnp.where(lane < 127, links[2][y] * inverse, 0.0)
            coef_ref[6, y] = jnp.where(lane > 0, shift_k(links[2][y], False) * inverse, 0.0)
        else:
            for f in range(1, 7):
                coef_ref[f, y] = jnp.zeros((16, 128), F32)


def dots_of(pairs):
    lane = lax.broadcasted_iota(jnp.int32, (1, 128), 1)
    out = jnp.zeros((1, 128), F32)
    for k, value in enumerate(pairs):
        out = jnp.where(lane == k, jnp.sum(value), out)
    return out


def first_sums(pieces):
    return [pieces[d + 2][16 * big_y : 16 * big_y + 16, :] for d, big_y in SPOTS]


def shared_sums(pieces):
    return [
        pieces[d + 2][16 * big_y + 16 : 16 * big_y + 32, :]
        + (pieces[d + 1][48:64, :] if big_y == 0 else pieces[d + 3][0:16, :])
        for d, big_y in SPOTS
    ]


def correct_rows(sums, coef_ref, smooth, remain, inverse_ref, scale_ref, offset_ref):
    start = [sums[y] * coef_ref[0, y] for y in range(8)]

    def sweep(now, y):
        here = now[y]
        total = start[y] + coef_ref[1, y] * shift_x(here, True) + coef_ref[2, y] * shift_x(here, False)
        total = total + coef_ref[3, y] * now[y + 1] + coef_ref[4, y] * now[y - 1]
        return total + coef_ref[5, y] * shift_k(here, True) + coef_ref[6, y] * shift_k(here, False)

    second = [None] + [sweep(start, y) for y in range(1, 7)] + [None]
    third = [None, None] + [sweep(second, y) for y in range(2, 6)]
    sub = lax.broadcasted_iota(jnp.int32, (8, 128), 0)
    lane = lax.broadcasted_iota(jnp.int32, (8, 128), 1)
    index = sub * 16 + lane // 8

    def spread_out(tile, x):
        wide = jnp.broadcast_to(tile[x + 4 : x + 5, :], (8, 128))
        return jnp.take_along_axis(wide, index, axis=1)

    tables = [[], [], []]
    for y in range(2, 6):
        for k, tile in enumerate((third[y], shift_k(third[y], True), shift_k(third[y], False))):
            tables[k].append([spread_out(tile, x) for x in range(-2, 4)])
    counts = (3, 4, 4, 3)

    def lifted(x):
        big_x = x // 2
        here, up, down = (
            jnp.concatenate(
                [jnp.broadcast_to(tables[k][y][big_x + 2][None], (counts[y], 8, 128)) for y in range(4)], axis=0
            )
            for k in range(3)
        )
        offset = offset_ref[x + 3]
        return jnp.where(offset > 0.5, up, jnp.where(offset < -0.5, down, here))

    lifts = [lifted(x) for x in range(-3, 7)]
    spreads = []
    for x in range(8):
        near = beside(lifts[x][1:13], lifts[x + 1], lifts[x + 2][1:13])
        spreads.append(REST * lifts[x + 1][1:13] + OMEGA * (inverse_ref[x] * near))
    shaped = []
    for x in range(6):
        near = beside(spreads[x][1:11], spreads[x + 1], spreads[x + 2][1:11])
        spread = spreads[x + 1][1:11]
        left = remain[x] - (scale_ref[x] * spread - near)
        shaped.append(smooth[x] + spread + OMEGA * (inverse_ref[x + 1, 1:11] * left))
    for x in range(4):
        near = beside(shaped[x][1:9], shaped[x + 1], shaped[x + 2][1:9])
        own = shaped[x + 1][1:9]
        yield x, own, scale_ref[x + 1, 1:9] * own - near


def put(low_ref, high_ref, x, value):
    (low_ref if x < 2 else high_ref)[x % 2] = value


def half(low_ref, high_ref, x):
    return (low_ref if x < 2 else high_ref)[x % 2]


def products(left, right):
    return [jnp.sum(a * b, axis=0) for a in left for b in right]


def begin_body(*refs):
    pieces, fixed, (z_ref, wlow_ref, whigh_ref) = refs[:5], refs[5:11], refs[11:]
    for x, z, w in correct_rows(first_sums(pieces), *fixed):
        z_ref[x] = z
        put(wlow_ref, whigh_ref, x, w)


def corrected(refs):
    pieces, vectors, coef_ref, fixed = refs[:5], refs[5:11], refs[11], refs[12:15]
    smooth, remain = smoothed(*vectors, fixed[0])
    return correct_rows(shared_sums(pieces), coef_ref, smooth, remain, *fixed)


def second_body(*refs):
    low_ref, high_ref, z_ref, m_ref, nlow_ref, nhigh_ref, dots_ref = refs[15:]
    wlow_ref, whigh_ref = refs[5:7]
    sums = [jnp.zeros((8, 128), F32)] * 6
    for x, m, n in corrected(refs[:15]):
        m_ref[x] = m
        put(nlow_ref, nhigh_ref, x, n)
        here = products((half(low_ref, high_ref, x), half(wlow_ref, whigh_ref, x), n), (z_ref[x], m))
        sums = [a + b for a, b in zip(sums, here)]
    dots_ref[...] = dots_of(sums)


def fourth_body(*refs):
    z_ref, r_ref, s_ref, q_ref, t_ref, m_ref, n_ref, dots_ref = refs[15:]
    wlow_ref, whigh_ref = refs[5:7]
    sums = [jnp.zeros((8, 128), F32)] * 15
    for x, m, n in corrected(refs[:15]):
        m_ref[x] = m
        n_ref[x] = n
        here = products((r_ref[x], half(wlow_ref, whigh_ref, x), s_ref[x], n, t_ref[x]), (z_ref[x], m, q_ref[x]))
        sums = [a + b for a, b in zip(sums, here)]
    dots_ref[...] = dots_of(sums)


def two_sum(a, b):
    total = a + b
    part = total - a
    return total, (a - (total - part)) + (b - part)


def split(a):
    wide = a * 4097.0
    high = wide - (wide - a)
    return high, a - high


def two_product(a, b):
    product = a * b
    a_high, a_low = split(a)
    b_high, b_low = split(b)
    return product, a_low * b_low - (((product - a_high * b_high) - a_low * b_high) - a_high * b_low)


def pair_add(a, b):
    total, rest = two_sum(a[0], b[0])
    return two_sum(total, rest + (a[1] + b[1]))


def pair_scale(a, factor):
    product, rest = two_product(a[0], factor)
    return two_sum(product, rest + a[1] * factor)


def pair_times(a, b):
    product, rest = two_product(a[0], b[0])
    return two_sum(product, rest + (a[0] * b[1] + a[1] * b[0]))


def total_of(got_ref, row, rest_row):
    total = got_ref[0, row : row + 1, :]
    rest = jnp.zeros((1, 128), F32) if rest_row is None else got_ref[0, rest_row : rest_row + 1, :]
    for j in range(1, got_ref.shape[0]):
        total, lost = two_sum(total, got_ref[j, row : row + 1, :])
        rest = rest + lost
        if rest_row is not None:
            rest = rest + got_ref[j, rest_row : rest_row + 1, :]
    return total, rest


def pairs_of(got_ref, row, rest_row, count):
    total, rest = total_of(got_ref, row, rest_row)
    total, rest = two_sum(total, rest)
    return [
        (jnp.broadcast_to(total[:, k : k + 1], (1, 128)), jnp.broadcast_to(rest[:, k : k + 1], (1, 128)))
        for k in range(count)
    ]


def form(table, left, weights):
    out = None
    for i, row in enumerate(left):
        for j, entry in enumerate(table[row]):
            factor = None
            for w in (weights[i], weights[j]):
                if w is not None:
                    factor = w if factor is None else pair_times(factor, w)
            term = entry if factor is None else pair_times(entry, factor)
            out = term if out is None else pair_add(out, term)
    return out[0] + out[1]


def tiled(row):
    return jnp.broadcast_to(row, (8, 128))[None]


def negated(pair):
    return -pair[0], -pair[1]


def merge_body(*refs):
    got_ref, low_ref, high_ref, z_ref, wlow_ref, whigh_ref, m_ref = refs[15:22]
    nlow_ref, nhigh_ref = refs[5:7]
    zo_ref, wolow_ref, wohigh_ref, xo_ref, ro_ref, po_ref, so_ref, qo_ref, to_ref, keep_ref = refs[22:]
    sums = pairs_of(got_ref, 0, 1, 6)
    table = [sums[0:2], sums[2:4], sums[4:6]]
    gamma0 = table[0][0][0]
    alpha0 = gamma0 / table[1][0][0]
    weights = (None, negated((alpha0, jnp.zeros_like(alpha0))))
    gamma1 = form(table, (0, 1), weights)
    delta1 = form(table, (1, 2), weights)
    beta1 = gamma1 / gamma0
    alpha1 = gamma1 / (delta1 - beta1 * gamma1 / alpha0)
    lane = lax.broadcasted_iota(jnp.int32, (1, 128), 1)
    keep_ref[...] = jnp.where(lane == 0, gamma1, jnp.where(lane == 1, alpha1, 0.0))
    alpha0, alpha1, beta1 = tiled(alpha0), tiled(alpha1), tiled(beta1)
    for x, k, l in corrected(refs[:15]):
        z0, w0 = z_ref[x], half(wlow_ref, whigh_ref, x)
        m0, n0 = m_ref[x], half(nlow_ref, nhigh_ref, x)
        z1, w1 = z0 - alpha0 * m0, w0 - alpha0 * n0
        p, s = z1 + beta1 * z0, w1 + beta1 * w0
        q = (m0 - alpha0 * k) + beta1 * m0
        t = (n0 - alpha0 * l) + beta1 * n0
        xo_ref[x] = alpha0 * z0 + alpha1 * p
        ro_ref[x] = (half(low_ref, high_ref, x) - alpha0 * w0) - alpha1 * s
        zo_ref[x] = z1 - alpha1 * q
        put(wolow_ref, wohigh_ref, x, w1 - alpha1 * t)
        po_ref[x], so_ref[x], qo_ref[x], to_ref[x] = p, s, q, t


def spread_dots_body(dots_ref, send_ref):
    tile = jnp.concatenate([dots_ref[...], jnp.zeros((7, 128), F32)], axis=0)
    for j in range(send_ref.shape[0]):
        send_ref[j] = tile


def sum_dots_body(got_ref, send_ref):
    total, rest = total_of(got_ref, 0, None)
    tile = jnp.concatenate([total, rest, jnp.zeros((6, 128), F32)], axis=0)
    for j in range(send_ref.shape[0]):
        send_ref[j] = tile


def finish_body(got_ref, z_ref, wlow_ref, whigh_ref, m_ref, n_ref, x_ref, r_ref, p_ref, s_ref, q_ref, t_ref, keep_ref,
                xo_ref, ro_ref, xs_ref, rs_ref):
    sums = pairs_of(got_ref, 0, 1, 15)
    table = [sums[3 * k : 3 * k + 3] for k in range(5)]
    keep = keep_ref[...]
    gamma1 = jnp.broadcast_to(keep[:, 0:1], (1, 128))
    alpha1 = jnp.broadcast_to(keep[:, 1:2], (1, 128))
    gamma2 = table[0][0][0]
    beta2 = gamma2 / gamma1
    alpha2 = gamma2 / (table[1][0][0] - beta2 * gamma2 / alpha1)
    weights = (None, (-alpha2, jnp.zeros_like(alpha2)), two_product(-alpha2, beta2))
    gamma3 = form(table, (0, 1, 2), weights)
    delta3 = form(table, (1, 3, 4), weights)
    beta3 = gamma3 / gamma2
    alpha3 = gamma3 / (delta3 - beta3 * gamma3 / alpha2)
    alpha2, beta2, alpha3, beta3 = tiled(alpha2), tiled(beta2), tiled(alpha3), tiled(beta3)
    for x in range(4):
        z, w, q1, t1 = z_ref[x], half(wlow_ref, whigh_ref, x), q_ref[x], t_ref[x]
        p2, s2 = z + beta2 * p_ref[x], w + beta2 * s_ref[x]
        q2, t2 = m_ref[x] + beta2 * q1, n_ref[x] + beta2 * t1
        p3 = (z - alpha2 * q2) + beta3 * p2
        s3 = (w - alpha2 * t2) + beta3 * s2
        xs_ref[pl.ds(64 * x, 64), :] = ((x_ref[x] + alpha2 * p2) + alpha3 * p3).reshape(64, 128)
        rs_ref[pl.ds(64 * x, 64), :] = ((r_ref[x] - alpha2 * s2) - alpha3 * s3).reshape(64, 128)
    for x in range(4):
        for s in range(8):
            part = slice(s * 128, (s + 1) * 128)
            xo_ref[x, :, part] = xs_ref[pl.ds(64 * x + s, 8, stride=8), :]
            ro_ref[x, :, part] = rs_ref[pl.ds(64 * x + s, 8, stride=8), :]


def local(right_side, diagonal, aggregate_id, coarse_diag, coarse_link):
    count_x, count_y = lax.axis_size("px"), lax.axis_size("py")
    me = jnp.stack([lax.axis_index("px"), lax.axis_index("py"), count_x - 1, count_y - 1]).astype(jnp.int32)

    def both_ways(low, high, axis, far=1):
        count = lax.axis_size(axis)
        up = [(i, (i + far) % count) for i in range(count)]
        down = [(b, a) for a, b in up]
        return lax.ppermute(high, axis, up), lax.ppermute(low, axis, down)

    def around(value, axis, reach):
        sides = [both_ways(value, value, axis, far) for far in range(1, reach + 1)]
        return [low for low, _ in sides[::-1]] + [value] + [high for _, high in sides]

    def gather(value, axis):
        return lax.all_to_all(value, axis, 0, 0)

    two, field = (2, 8, 8, 128), (4, 8, 8, 128)
    low, high = call(enter_body, [(448, 128)] * 2, right_side, diagonal, aggregate_id, scalars=0)
    low, high = low.reshape(7, 8, 8, 128), high.reshape(7, 8, 8, 128)
    xlow, xhigh = both_ways(low, high, "px")
    first, last = call(pack_first_body, [(62, 8, 128)] * 2, low, high, xlow, xhigh, scalars=0)
    ylow, yhigh = both_ways(first, last, "py")
    inverse, scale, offset = call(
        setup_body, [(8, 12, 8, 128), (6, 10, 8, 128), (10, 14, 8, 128)], me, low, high, xlow, xhigh, ylow, yhigh
    )
    mid, dots = (6, 10, 8, 128), (1, 128)
    smooth, remain, send = call(
        restrict_body, [mid, mid, (24, 128)],
        low, high, xlow, xhigh, ylow, yhigh, inverse, offset, coarse_diag, coarse_link, scalars=0,
    )
    send, = call(window_first_body, [(112, 128)], *around(send, "px", 2), scalars=0)
    pieces = around(send, "py", 2)
    coef, = call(coarse_setup_body, [(7, 8, 16, 128)], me, *pieces)
    fixed = (inverse, scale, offset)
    z, wlow, whigh = call(begin_body, [field, two, two], *pieces, coef, smooth, remain, *fixed, scalars=0)

    def exchanged(low, high):
        send, = call(contribute_body, [(16, 128)], low, high, inverse, offset, scalars=0)
        xlow, xhigh = both_ways(low, high, "px")
        first, last, window = call(
            pack_body, [(8, 2, 8, 128)] * 2 + [(64, 128)],
            low, high, xlow, xhigh, *around(send, "px", 3), scalars=0,
        )
        ylow, yhigh = both_ways(first, last, "py")
        return (*around(window, "py", 2), low, high, xlow, xhigh, ylow, yhigh, coef, *fixed)

    def summed(sums):
        send, = call(spread_dots_body, [(count_x, 8, 128)], sums, scalars=0)
        send, = call(sum_dots_body, [(count_y, 8, 128)], gather(send, "px"), scalars=0)
        return gather(send, "py")

    m, nlow, nhigh, sums = call(
        second_body, [field, two, two, dots], *exchanged(wlow, whigh), low, high, z, scalars=0
    )
    z, wlow, whigh, x, r, p, s, q, t, keep = call(
        merge_body, [field, two, two] + [field] * 6 + [dots],
        *exchanged(nlow, nhigh), summed(sums), low, high, z, wlow, whigh, m, scalars=0,
    )
    m, n, sums = call(
        fourth_body, [field, field, dots], *exchanged(wlow, whigh), z, r, s, q, t, scalars=0
    )
    return tuple(call(
        finish_body, [right_side.shape] * 2,
        summed(sums), z, wlow, whigh, m, n, x, r, p, s, q, t, keep,
        scalars=0, scratch=[pltpu.VMEM((256, 128), F32)] * 2,
    ))


def solution(mesh):
    cells = P("px", "py", None)
    in_specs = (cells, cells, cells, cells, P(None, "px", "py", None))
    return jax.shard_map(local, mesh=mesh, in_specs=in_specs, out_specs=(cells, cells), check_vma=False)
```

```python
import jax
import jax.numpy as jnp
from jax import lax
from jax.experimental import pallas as pl
from jax.experimental.pallas import tpu as pltpu
from jax.sharding import PartitionSpec as P

OMEGA = 2.0 / 3.0
REST = 1.0 - OMEGA
FACES = (32.0, 16.0, 8.0)
F32 = jnp.float32


def call(body, outs, *args, scalars=1, scratch=(), flops=2_000_000):
    smem = pl.BlockSpec(memory_space=pltpu.SMEM)
    vmem = pl.BlockSpec(memory_space=pltpu.VMEM)
    specs = [smem] * scalars + [vmem] * (len(args) - scalars)
    return pl.pallas_call(
        body,
        out_shape=[jax.ShapeDtypeStruct(shape, F32) for shape in outs],
        in_specs=specs,
        out_specs=[vmem] * len(outs),
        scratch_shapes=list(scratch),
        compiler_params=pltpu.CompilerParams(vmem_limit_bytes=20 * 1024 * 1024),
        cost_estimate=pl.CostEstimate(flops=flops, bytes_accessed=1_000_000, transcendentals=0),
    )(*args)


def along_z(value):
    lane = lax.broadcasted_iota(jnp.int32, value.shape, value.ndim - 1)
    sub = lax.broadcasted_iota(jnp.int32, value.shape, value.ndim - 2)
    after = pltpu.roll(value, 127, value.ndim - 1)
    before = pltpu.roll(value, 1, value.ndim - 1)
    after_row = jnp.where(sub == 7, 0.0, pltpu.roll(after, 7, value.ndim - 2))
    before_row = jnp.where(sub == 0, 0.0, pltpu.roll(before, 1, value.ndim - 2))
    return jnp.where(lane == 127, after_row, after) + jnp.where(lane == 0, before_row, before)


def by_eight(value, ahead):
    lane = lax.broadcasted_iota(jnp.int32, value.shape, value.ndim - 1)
    if ahead:
        moved = pltpu.roll(value, 120, value.ndim - 1)
        return jnp.where(lane >= 120, pltpu.roll(moved, 7, value.ndim - 2), moved)
    moved = pltpu.roll(value, 8, value.ndim - 1)
    return jnp.where(lane < 8, pltpu.roll(moved, 1, value.ndim - 2), moved)


def beside(below, here, above):
    count = here.shape[0]
    inner = here[1 : count - 1]
    return below + above + here[0 : count - 2] + here[2:count] + along_z(inner)


def enter_body(b_ref, d_ref, a_ref, low_ref, high_ref):
    lane = lax.broadcasted_iota(jnp.int32, (8, 128), 1)
    for x in range(4):
        for s in range(8):
            part = slice(s * 128, (s + 1) * 128)
            b = b_ref[x, :, part]
            d = d_ref[x, :, part]
            home = (lane + s * 128) // 8
            o = ((a_ref[x, :, part] & 127) - home).astype(F32)
            ref = low_ref if x < 2 else high_ref
            at = (x % 2) * 64 + s
            ref[pl.ds(at, 8, stride=8), :] = b
            ref[pl.ds(128 + at, 8, stride=8), :] = d
            if x < 3:
                low_ref[pl.ds(256 + x * 64 + s, 8, stride=8), :] = o
            if x > 0:
                high_ref[pl.ds(256 + (x - 1) * 64 + s, 8, stride=8), :] = o


def field_rows(low, high, xlow, xhigh, base):
    return [ref.at[base + k] for ref in (xlow, low, high, xhigh) for k in range(2)]


def offset_rows(low, high, xlow, xhigh):
    return [ref.at[4 + k] for ref, ks in ((xlow, (0, 1, 2)), (low, (0, 1, 2)), (high, (2,)), (xhigh, (0, 1, 2))) for k in ks]


def pack_first_body(low_ref, high_ref, xlow_ref, xhigh_ref, first_ref, last_ref):
    four = (low_ref, high_ref, xlow_ref, xhigh_ref)
    for f in range(2):
        for x, ref in enumerate(field_rows(*four, 2 * f)):
            at = 16 * f + 2 * x
            first_ref[at : at + 2] = ref[0:2]
            last_ref[at : at + 2] = ref[6:8]
    for x, ref in enumerate(offset_rows(*four)):
        at = 32 + 3 * x
        first_ref[at : at + 3] = ref[0:3]
        last_ref[at : at + 3] = ref[5:8]


def setup_body(me_ref, low_ref, high_ref, xlow_ref, xhigh_ref, ylow_ref, yhigh_ref, inverse_ref, scale_ref, offset_ref):
    px, py, last_x, last_y = me_ref[0], me_ref[1], me_ref[2], me_ref[3]
    below = jnp.where(px > 0, 1.0, 0.0).astype(F32)
    above = jnp.where(px < last_x, 1.0, 0.0).astype(F32)
    left = jnp.where(py > 0, 1.0, 0.0).astype(F32)
    right = jnp.where(py < last_y, 1.0, 0.0).astype(F32)
    four = (low_ref, high_ref, xlow_ref, xhigh_ref)
    for x, ref in enumerate(field_rows(*four, 2)):
        s_mid = 6.0 + ref[...]
        s_left = 6.0 + ylow_ref[16 + 2 * x : 18 + 2 * x]
        s_right = 6.0 + yhigh_ref[16 + 2 * x : 18 + 2 * x]
        i_mid, i_left, i_right = 1.0 / s_mid, left / s_left, right / s_right
        if x < 2 or x > 5:
            seen = below if x < 2 else above
            i_mid, i_left, i_right = i_mid * seen, i_left * seen, i_right * seen
        inverse_ref[x, 0:2] = i_left
        inverse_ref[x, 2:10] = i_mid
        inverse_ref[x, 10:12] = i_right
        if 1 <= x <= 6:
            scale_ref[x - 1, 0:1] = s_left[1:2]
            scale_ref[x - 1, 1:9] = s_mid
            scale_ref[x - 1, 9:10] = s_right[0:1]
    for x, ref in enumerate(offset_rows(*four)):
        offset_ref[x, 0:3] = ylow_ref[32 + 3 * x : 35 + 3 * x]
        offset_ref[x, 3:11] = ref[...]
        offset_ref[x, 11:14] = yhigh_ref[32 + 3 * x : 35 + 3 * x]


def padded(value, width):
    zero = jnp.zeros((width, 8, 128), F32)
    return jnp.concatenate([zero, value, zero], axis=0)


def contribute_body(low_ref, high_ref, inverse_ref, offset_ref, share_ref, down_ref, up_ref):
    vector = [half(low_ref, high_ref, x) for x in range(4)]
    smooth = [OMEGA * vector[x] * inverse_ref[x + 2, 2:10] for x in range(4)]
    remains = [padded(smooth[0], 1)]
    for x in range(4):
        around = padded(smooth[x], 1)
        center = REST * vector[x] + (around[0:8] + around[2:10] + along_z(smooth[x]))
        for other in (x - 1, x + 1):
            if 0 <= other < 4:
                center = center + smooth[other]
        remains.append(jnp.concatenate([smooth[x][0:1], center, smooth[x][7:8]], axis=0))
    remains.append(padded(smooth[3], 1))
    shrunk = [remains[x] * inverse_ref[x + 1, 1:11] for x in range(6)]
    cells = []
    for x in range(8):
        near = None
        for other in (x - 2, x):
            if 0 <= other < 6:
                near = shrunk[other] if near is None else near + shrunk[other]
        if 1 <= x <= 6:
            near = padded(near + along_z(shrunk[x - 1]), 1)
            wide = padded(shrunk[x - 1], 2)
            value = REST * padded(remains[x - 1], 1) + OMEGA * (near + (wide[0:12] + wide[2:14]))
        else:
            value = padded(OMEGA * near, 1)
        value = jnp.where(inverse_ref[x] > 0.0, value, 0.0)
        offset = offset_ref[x + 1, 1:13]
        cells.append((
            jnp.where(jnp.abs(offset) < 0.5, value, 0.0),
            jnp.where(offset > 0.5, value, 0.0),
            jnp.where(offset < -0.5, value, 0.0),
        ))
    sums = []
    for start, stop in ((0, 2), (2, 6), (6, 10), (10, 12)):
        for i in range(4):
            here, up, down = (
                jnp.sum(cells[2 * i][k][start:stop], axis=0) + jnp.sum(cells[2 * i + 1][k][start:stop], axis=0)
                for k in range(3)
            )
            sums.append(here + by_eight(up, False) + by_eight(down, True))
    share = jnp.concatenate(grouped_rows(sums), axis=0)
    share_ref[...] = share
    for ref, cells in ((down_ref, vector[:2]), (up_ref, vector[2:])):
        for k in range(2):
            ref[8 * k : 8 * k + 8] = cells[k]
            ref[16 + k] = share[8 * k : 8 * k + 8]


def grouped_rows(sums):
    stacked = jnp.concatenate(sums, axis=0)
    row = lax.broadcasted_iota(jnp.int32, (128, 128), 0)
    col = lax.broadcasted_iota(jnp.int32, (128, 128), 1)
    group = jnp.where(row // 8 == col % 16, 1.0, 0.0).astype(F32)
    grouped = jnp.dot(stacked, group, preferred_element_type=F32, precision=lax.Precision.HIGHEST)
    sub = lax.broadcasted_iota(jnp.int32, (8, 128), 0)
    lane = lax.broadcasted_iota(jnp.int32, (8, 128), 1)
    return [
        jnp.sum(jnp.where(lane // 16 == sub, grouped[8 * c : 8 * c + 8], 0.0), axis=0, keepdims=True)
        for c in range(len(sums))
    ]


def pack_body(low_ref, high_ref, below3_ref, below2_ref, below_ref, share_ref, above_ref, above2_ref, above3_ref,
              first_ref, last_ref, early_ref, late_ref):
    for x, mid in enumerate(row_blocks(low_ref, high_ref, below_ref, above_ref)):
        cells = mid()
        first_ref[2 * x : 2 * x + 2] = cells[0:2]
        last_ref[2 * x : 2 * x + 2] = cells[6:8]
    zero = jnp.zeros((6, 128), F32)
    flat = {-3: below3_ref, -2: below2_ref, 0: share_ref, 2: above2_ref, 3: above3_ref}
    joined = {-1: below_ref, 1: above_ref}
    for j in range(4):
        def row(d, i):
            at = 4 * j + i
            if d in flat:
                return flat[d][at : at + 1, :]
            return joined[d][16 + at // 8, at % 8 : at % 8 + 1, :]

        rows = []
        for d in range(-2, 3):
            rows.append(row(d, 1) + row(d - 1, 3))
            rows.append(row(d, 2) + row(d + 1, 0))
        tile = jnp.concatenate(rows + [zero], axis=0)
        ref = early_ref if j < 2 else late_ref
        ref[16 * (j % 2) : 16 * (j % 2) + 16] = tile
        for k in range(2):
            first_ref[16 + 2 * j + k] = tile[8 * k : 8 * k + 8]
            last_ref[16 + 2 * j + k] = tile[8 * k : 8 * k + 8]


def row_blocks(low_ref, high_ref, below_ref, above_ref):
    def sent(ref, k):
        return lambda: ref[8 * k : 8 * k + 8]

    def own(ref, k):
        return lambda: ref[k]

    blocks = [sent(below_ref, k) for k in range(2)] + [own(low_ref, k) for k in range(2)]
    return blocks + [own(high_ref, k) for k in range(2)] + [sent(above_ref, k) for k in range(2)]


def smoothed_rows(vector, inverse_ref):
    smooth = [OMEGA * vector(x) * inverse_ref[x] for x in range(8)]
    remains = [
        REST * vector(x)[1:11] + beside(smooth[x - 1][1:11], smooth[x], smooth[x + 1][1:11]) for x in range(1, 7)
    ]
    return [smooth[x][1:11] for x in range(1, 7)], remains


def smoothed(low, high, below, above, left, right, inverse_ref):
    mids = row_blocks(low, high, below, above)

    def vector(x):
        return jnp.concatenate([left[2 * x : 2 * x + 2], mids[x](), right[2 * x : 2 * x + 2]], axis=0)

    return smoothed_rows(vector, inverse_ref)


def restrict_body(low, high, xlow, xhigh, ylow, yhigh, inverse_ref, offset_ref, cdiag_ref, link_ref,
                  smooth_ref, remain_ref, send_ref):
    mids = [ref.at[k] for ref in (xlow, low, high, xhigh) for k in range(2)]

    def vector(x):
        return jnp.concatenate([ylow[2 * x : 2 * x + 2], mids[x][...], yhigh[2 * x : 2 * x + 2]], axis=0)

    smooth, full = smoothed_rows(vector, inverse_ref)
    shrunk, remains = [], []
    for x in range(6):
        smooth_ref[x] = smooth[x]
        remain_ref[x] = full[x]
        remains.append(full[x][1:9])
        shrunk.append(full[x] * inverse_ref[x + 1, 1:11])
    sums = []
    for big_x in range(2):
        parts = []
        for x in (2 * big_x, 2 * big_x + 1):
            near = beside(shrunk[x][1:9], shrunk[x + 1], shrunk[x + 2][1:9])
            reduced = REST * remains[x + 1] + OMEGA * near
            offset = offset_ref[x + 3, 3:11]
            parts.append((
                jnp.where(jnp.abs(offset) < 0.5, reduced, 0.0),
                jnp.where(offset > 0.5, reduced, 0.0),
                jnp.where(offset < -0.5, reduced, 0.0),
            ))
        for big_y in range(2):
            cols = slice(4 * big_y, 4 * big_y + 4)
            here, up, down = (
                jnp.sum(parts[0][k][cols], axis=0) + jnp.sum(parts[1][k][cols], axis=0) for k in range(3)
            )
            sums.append(here + by_eight(up, False) + by_eight(down, True))
    rows = grouped_rows(sums) + [jnp.zeros((4, 128), F32)]
    for ref in (cdiag_ref, link_ref.at[0], link_ref.at[1], link_ref.at[2]):
        rows = rows + [ref[c // 2, c % 2 : c % 2 + 1, :] for c in range(4)]
    send_ref[...] = jnp.concatenate(rows, axis=0)


def window_rows(pieces, start):
    return [
        [ref[start + 2 * big_x + big_y : start + 2 * big_x + big_y + 1, :] for ref in pieces for big_x in range(2)]
        for big_y in range(2)
    ]


def window_first_body(*refs):
    pieces, send_ref = refs[:5], refs[5]
    zero = jnp.zeros((6, 128), F32)
    early, late = window_rows(pieces, 0)
    send_ref[0:32] = jnp.concatenate(early + [zero] + late + [zero], axis=0)
    rows = []
    for f in range(4):
        early, late = window_rows(pieces, 8 + 4 * f)
        rows = rows + early + late
    send_ref[32:112] = jnp.concatenate(rows, axis=0)


SPOTS = ((-2, 1), (-1, 0), (-1, 1), (0, 0), (0, 1), (1, 0), (1, 1), (2, 0))


def shift_x(value, ahead):
    return pltpu.roll(value, 15 if ahead else 1, 0)


def shift_k(value, ahead):
    return pltpu.roll(value, 127 if ahead else 1, 1)


def coarse_setup_body(me_ref, *refs):
    pieces, coef_ref = refs[:5], refs[5]
    px, py, last_x, last_y = me_ref[0], me_ref[1], me_ref[2], me_ref[3]
    row = lax.broadcasted_iota(jnp.int32, (16, 128), 0)
    lane = lax.broadcasted_iota(jnp.int32, (16, 128), 1)
    pad = jnp.zeros((6, 128), F32)
    where_x = 2 * px - 4 + row
    inside_x = (where_x >= 0) & (where_x < 2 * (last_x + 1)) & (row < 10)

    def take(y, f):
        d, big_y = SPOTS[y]
        start = 32 + 20 * f + 10 * big_y
        return jnp.concatenate([pieces[d + 2][start : start + 10, :], pad], axis=0)

    links = [[FACES[f - 1] * take(y, f) for y in range(8)] for f in range(1, 4)]
    for y in range(8):
        where_y = 2 * py - 3 + y
        seen = jnp.where((where_y >= 0) & (where_y < 2 * (last_y + 1)), 1.0, 0.0).astype(F32)
        diag = jnp.where(inside_x, take(y, 0), 1.0)
        inverse = jnp.where(inside_x, seen / diag, 0.0)
        coef_ref[0, y] = inverse
        if 1 <= y <= 6:
            coef_ref[1, y] = links[0][y] * inverse
            coef_ref[2, y] = shift_x(links[0][y], False) * inverse
            coef_ref[3, y] = links[1][y] * inverse
            coef_ref[4, y] = links[1][y - 1] * inverse
            coef_ref[5, y] = jnp.where(lane < 127, links[2][y] * inverse, 0.0)
            coef_ref[6, y] = jnp.where(lane > 0, shift_k(links[2][y], False) * inverse, 0.0)
        else:
            for f in range(1, 7):
                coef_ref[f, y] = jnp.zeros((16, 128), F32)


def dots_of(pairs):
    lane = lax.broadcasted_iota(jnp.int32, (1, 128), 1)
    out = jnp.zeros((1, 128), F32)
    for k, value in enumerate(pairs):
        out = jnp.where(lane == k, jnp.sum(value), out)
    return out


def first_sums(pieces):
    return [pieces[d + 2][16 * big_y : 16 * big_y + 16, :] for d, big_y in SPOTS]


def shared_sums(left2_ref, left_ref, early_ref, late_ref, right_ref, right2_ref):
    def share(d, j):
        if d in (-1, 1):
            ref = left_ref if d < 0 else right_ref
            return ref[16 + 2 * j : 18 + 2 * j].reshape(16, 128)
        ref = {-2: left2_ref, 0: early_ref if j < 2 else late_ref, 2: right2_ref}[d]
        return ref[16 * (j % 2) : 16 * (j % 2) + 16, :]

    return [share(d, big_y + 1) + (share(d - 1, 3) if big_y == 0 else share(d + 1, 0)) for d, big_y in SPOTS]


def correct_rows(sums, coef_ref, smooth, remain, inverse_ref, scale_ref, offset_ref):
    start = [sums[y] * coef_ref[0, y] for y in range(8)]

    def sweep(now, y):
        here = now[y]
        total = start[y] + coef_ref[1, y] * shift_x(here, True) + coef_ref[2, y] * shift_x(here, False)
        total = total + coef_ref[3, y] * now[y + 1] + coef_ref[4, y] * now[y - 1]
        return total + coef_ref[5, y] * shift_k(here, True) + coef_ref[6, y] * shift_k(here, False)

    second = [None] + [sweep(start, y) for y in range(1, 7)] + [None]
    third = [None, None] + [sweep(second, y) for y in range(2, 6)]
    sub = lax.broadcasted_iota(jnp.int32, (8, 128), 0)
    lane = lax.broadcasted_iota(jnp.int32, (8, 128), 1)
    index = sub * 16 + lane // 8

    def spread_out(tile, x):
        wide = jnp.broadcast_to(tile[x + 4 : x + 5, :], (8, 128))
        return jnp.take_along_axis(wide, index, axis=1)

    tables = [[], [], []]
    for y in range(2, 6):
        for k, tile in enumerate((third[y], shift_k(third[y], True), shift_k(third[y], False))):
            tables[k].append([spread_out(tile, x) for x in range(-2, 4)])
    counts = (3, 4, 4, 3)

    def lifted(x):
        big_x = x // 2
        here, up, down = (
            jnp.concatenate(
                [jnp.broadcast_to(tables[k][y][big_x + 2][None], (counts[y], 8, 128)) for y in range(4)], axis=0
            )
            for k in range(3)
        )
        offset = offset_ref[x + 3]
        return jnp.where(offset > 0.5, up, jnp.where(offset < -0.5, down, here))

    lifts = [lifted(x) for x in range(-3, 7)]
    spreads = []
    for x in range(8):
        near = beside(lifts[x][1:13], lifts[x + 1], lifts[x + 2][1:13])
        spreads.append(REST * lifts[x + 1][1:13] + OMEGA * (inverse_ref[x] * near))
    shaped = []
    for x in range(6):
        near = beside(spreads[x][1:11], spreads[x + 1], spreads[x + 2][1:11])
        spread = spreads[x + 1][1:11]
        left = remain[x] - (scale_ref[x] * spread - near)
        shaped.append(smooth[x] + spread + OMEGA * (inverse_ref[x + 1, 1:11] * left))
    for x in range(4):
        near = beside(shaped[x][1:9], shaped[x + 1], shaped[x + 2][1:9])
        own = shaped[x + 1][1:9]
        yield x, own, scale_ref[x + 1, 1:9] * own - near


def put(low_ref, high_ref, x, value):
    (low_ref if x < 2 else high_ref)[x % 2] = value


def half(low_ref, high_ref, x):
    return (low_ref if x < 2 else high_ref)[x % 2]


def products(left, right):
    return [jnp.sum(a * b, axis=0) for a in left for b in right]


def begin_body(*refs):
    pieces, fixed, (z_ref, wlow_ref, whigh_ref) = refs[:5], refs[5:11], refs[11:]
    for x, z, w in correct_rows(first_sums(pieces), *fixed):
        z_ref[x] = z
        put(wlow_ref, whigh_ref, x, w)


def corrected(refs):
    left2, early, late, right2, low, high, below, above, left, right, coef = refs[:11]
    fixed = refs[11:14]
    smooth, remain = smoothed(low, high, below, above, left, right, fixed[0])
    return correct_rows(shared_sums(left2, left, early, late, right, right2), coef, smooth, remain, *fixed)


def second_body(*refs):
    low_ref, high_ref, z_ref, m_ref, nlow_ref, nhigh_ref, dots_ref = refs[14:]
    wlow_ref, whigh_ref = refs[4:6]
    sums = [jnp.zeros((8, 128), F32)] * 6
    for x, m, n in corrected(refs[:14]):
        m_ref[x] = m
        put(nlow_ref, nhigh_ref, x, n)
        here = products((half(low_ref, high_ref, x), half(wlow_ref, whigh_ref, x), n), (z_ref[x], m))
        sums = [a + b for a, b in zip(sums, here)]
    dots_ref[...] = dots_of(sums)


def fourth_body(*refs):
    z_ref, r_ref, s_ref, q_ref, t_ref, m_ref, n_ref, dots_ref = refs[14:]
    wlow_ref, whigh_ref = refs[4:6]
    sums = [jnp.zeros((8, 128), F32)] * 15
    for x, m, n in corrected(refs[:14]):
        m_ref[x] = m
        n_ref[x] = n
        here = products((r_ref[x], half(wlow_ref, whigh_ref, x), s_ref[x], n, t_ref[x]), (z_ref[x], m, q_ref[x]))
        sums = [a + b for a, b in zip(sums, here)]
    dots_ref[...] = dots_of(sums)


def two_sum(a, b):
    total = a + b
    part = total - a
    return total, (a - (total - part)) + (b - part)


def split(a):
    wide = a * 4097.0
    high = wide - (wide - a)
    return high, a - high


def two_product(a, b):
    product = a * b
    a_high, a_low = split(a)
    b_high, b_low = split(b)
    return product, a_low * b_low - (((product - a_high * b_high) - a_low * b_high) - a_high * b_low)


def pair_add(a, b):
    total, rest = two_sum(a[0], b[0])
    return two_sum(total, rest + (a[1] + b[1]))


def pair_scale(a, factor):
    product, rest = two_product(a[0], factor)
    return two_sum(product, rest + a[1] * factor)


def pair_times(a, b):
    product, rest = two_product(a[0], b[0])
    return two_sum(product, rest + (a[0] * b[1] + a[1] * b[0]))


def total_of(got_ref, row, rest_row):
    total = got_ref[0, row : row + 1, :]
    rest = jnp.zeros((1, 128), F32) if rest_row is None else got_ref[0, rest_row : rest_row + 1, :]
    for j in range(1, got_ref.shape[0]):
        total, lost = two_sum(total, got_ref[j, row : row + 1, :])
        rest = rest + lost
        if rest_row is not None:
            rest = rest + got_ref[j, rest_row : rest_row + 1, :]
    return total, rest


def pairs_of(got_ref, row, rest_row, count):
    total, rest = total_of(got_ref, row, rest_row)
    total, rest = two_sum(total, rest)
    return [
        (jnp.broadcast_to(total[:, k : k + 1], (1, 128)), jnp.broadcast_to(rest[:, k : k + 1], (1, 128)))
        for k in range(count)
    ]


def form(table, left, weights):
    out = None
    for i, row in enumerate(left):
        for j, entry in enumerate(table[row]):
            factor = None
            for w in (weights[i], weights[j]):
                if w is not None:
                    factor = w if factor is None else pair_times(factor, w)
            term = entry if factor is None else pair_times(entry, factor)
            out = term if out is None else pair_add(out, term)
    return out[0] + out[1]


def tiled(row):
    return jnp.broadcast_to(row, (8, 128))[None]


def negated(pair):
    return -pair[0], -pair[1]


def merge_body(*refs):
    got_ref, low_ref, high_ref, z_ref, wlow_ref, whigh_ref, m_ref = refs[14:21]
    nlow_ref, nhigh_ref = refs[4:6]
    zo_ref, wolow_ref, wohigh_ref, xo_ref, ro_ref, po_ref, so_ref, qo_ref, to_ref, keep_ref = refs[21:]
    sums = pairs_of(got_ref, 0, 1, 6)
    table = [sums[0:2], sums[2:4], sums[4:6]]
    gamma0 = table[0][0][0]
    alpha0 = gamma0 / table[1][0][0]
    weights = (None, negated((alpha0, jnp.zeros_like(alpha0))))
    gamma1 = form(table, (0, 1), weights)
    delta1 = form(table, (1, 2), weights)
    beta1 = gamma1 / gamma0
    alpha1 = gamma1 / (delta1 - beta1 * gamma1 / alpha0)
    lane = lax.broadcasted_iota(jnp.int32, (1, 128), 1)
    keep_ref[...] = jnp.where(lane == 0, gamma1, jnp.where(lane == 1, alpha1, 0.0))
    alpha0, alpha1, beta1 = tiled(alpha0), tiled(alpha1), tiled(beta1)
    for x, k, l in corrected(refs[:14]):
        z0, w0 = z_ref[x], half(wlow_ref, whigh_ref, x)
        m0, n0 = m_ref[x], half(nlow_ref, nhigh_ref, x)
        z1, w1 = z0 - alpha0 * m0, w0 - alpha0 * n0
        p, s = z1 + beta1 * z0, w1 + beta1 * w0
        q = (m0 - alpha0 * k) + beta1 * m0
        t = (n0 - alpha0 * l) + beta1 * n0
        xo_ref[x] = alpha0 * z0 + alpha1 * p
        ro_ref[x] = (half(low_ref, high_ref, x) - alpha0 * w0) - alpha1 * s
        zo_ref[x] = z1 - alpha1 * q
        put(wolow_ref, wohigh_ref, x, w1 - alpha1 * t)
        po_ref[x], so_ref[x], qo_ref[x], to_ref[x] = p, s, q, t


def spread_dots_body(dots_ref, send_ref):
    tile = jnp.concatenate([dots_ref[...], jnp.zeros((7, 128), F32)], axis=0)
    for j in range(send_ref.shape[0]):
        send_ref[j] = tile


def sum_dots_body(got_ref, send_ref):
    total, rest = total_of(got_ref, 0, None)
    tile = jnp.concatenate([total, rest, jnp.zeros((6, 128), F32)], axis=0)
    for j in range(send_ref.shape[0]):
        send_ref[j] = tile


def finish_body(got_ref, z_ref, wlow_ref, whigh_ref, m_ref, n_ref, x_ref, r_ref, p_ref, s_ref, q_ref, t_ref, keep_ref,
                xo_ref, ro_ref, xs_ref, rs_ref):
    sums = pairs_of(got_ref, 0, 1, 15)
    table = [sums[3 * k : 3 * k + 3] for k in range(5)]
    keep = keep_ref[...]
    gamma1 = jnp.broadcast_to(keep[:, 0:1], (1, 128))
    alpha1 = jnp.broadcast_to(keep[:, 1:2], (1, 128))
    gamma2 = table[0][0][0]
    beta2 = gamma2 / gamma1
    alpha2 = gamma2 / (table[1][0][0] - beta2 * gamma2 / alpha1)
    weights = (None, (-alpha2, jnp.zeros_like(alpha2)), two_product(-alpha2, beta2))
    gamma3 = form(table, (0, 1, 2), weights)
    delta3 = form(table, (1, 3, 4), weights)
    beta3 = gamma3 / gamma2
    alpha3 = gamma3 / (delta3 - beta3 * gamma3 / alpha2)
    alpha2, beta2, alpha3, beta3 = tiled(alpha2), tiled(beta2), tiled(alpha3), tiled(beta3)
    for x in range(4):
        z, w, q1, t1 = z_ref[x], half(wlow_ref, whigh_ref, x), q_ref[x], t_ref[x]
        p2, s2 = z + beta2 * p_ref[x], w + beta2 * s_ref[x]
        q2, t2 = m_ref[x] + beta2 * q1, n_ref[x] + beta2 * t1
        p3 = (z - alpha2 * q2) + beta3 * p2
        s3 = (w - alpha2 * t2) + beta3 * s2
        xs_ref[pl.ds(64 * x, 64), :] = ((x_ref[x] + alpha2 * p2) + alpha3 * p3).reshape(64, 128)
        rs_ref[pl.ds(64 * x, 64), :] = ((r_ref[x] - alpha2 * s2) - alpha3 * s3).reshape(64, 128)
    for x in range(4):
        for s in range(8):
            part = slice(s * 128, (s + 1) * 128)
            xo_ref[x, :, part] = xs_ref[pl.ds(64 * x + s, 8, stride=8), :]
            ro_ref[x, :, part] = rs_ref[pl.ds(64 * x + s, 8, stride=8), :]


def local(right_side, diagonal, aggregate_id, coarse_diag, coarse_link):
    count_x, count_y = lax.axis_size("px"), lax.axis_size("py")
    me = jnp.stack([lax.axis_index("px"), lax.axis_index("py"), count_x - 1, count_y - 1]).astype(jnp.int32)

    def both_ways(low, high, axis, far=1):
        count = lax.axis_size(axis)
        up = [(i, (i + far) % count) for i in range(count)]
        down = [(b, a) for a, b in up]
        return lax.ppermute(high, axis, up), lax.ppermute(low, axis, down)

    def around(value, axis, reach):
        sides = [both_ways(value, value, axis, far) for far in range(1, reach + 1)]
        return [low for low, _ in sides[::-1]] + [value] + [high for _, high in sides]

    def gather(value, axis):
        return lax.all_to_all(value, axis, 0, 0)

    two, field = (2, 8, 8, 128), (4, 8, 8, 128)
    low, high = call(enter_body, [(448, 128)] * 2, right_side, diagonal, aggregate_id, scalars=0)
    low, high = low.reshape(7, 8, 8, 128), high.reshape(7, 8, 8, 128)
    xlow, xhigh = both_ways(low, high, "px")
    first, last = call(pack_first_body, [(62, 8, 128)] * 2, low, high, xlow, xhigh, scalars=0)
    ylow, yhigh = both_ways(first, last, "py")
    inverse, scale, offset = call(
        setup_body, [(8, 12, 8, 128), (6, 10, 8, 128), (10, 14, 8, 128)], me, low, high, xlow, xhigh, ylow, yhigh
    )
    mid, dots = (6, 10, 8, 128), (1, 128)
    smooth, remain, send = call(
        restrict_body, [mid, mid, (24, 128)],
        low, high, xlow, xhigh, ylow, yhigh, inverse, offset, coarse_diag, coarse_link, scalars=0,
    )
    send, = call(window_first_body, [(112, 128)], *around(send, "px", 2), scalars=0)
    pieces = around(send, "py", 2)
    coef, = call(coarse_setup_body, [(7, 8, 16, 128)], me, *pieces)
    fixed = (inverse, scale, offset)
    z, wlow, whigh = call(begin_body, [field, two, two], *pieces, coef, smooth, remain, *fixed, scalars=0)

    def exchanged(low, high):
        share, down, up = call(
            contribute_body, [(16, 128), (18, 8, 128), (18, 8, 128)], low, high, inverse, offset, scalars=0
        )
        below, above = both_ways(down, up, "px")
        below2, above2 = both_ways(share, share, "px", 2)
        below3, above3 = both_ways(share, share, "px", 3)
        first, last, early, late = call(
            pack_body, [(24, 8, 128)] * 2 + [(32, 128)] * 2,
            low, high, below3, below2, below, share, above, above2, above3, scalars=0,
        )
        left, right = both_ways(first, last, "py")
        left2, right2 = both_ways(early, late, "py", 2)
        return (left2, early, late, right2, low, high, below, above, left, right, coef, *fixed)

    def summed(sums):
        send, = call(spread_dots_body, [(count_x, 8, 128)], sums, scalars=0)
        send, = call(sum_dots_body, [(count_y, 8, 128)], gather(send, "px"), scalars=0)
        return gather(send, "py")

    m, nlow, nhigh, sums = call(
        second_body, [field, two, two, dots], *exchanged(wlow, whigh), low, high, z, scalars=0
    )
    z, wlow, whigh, x, r, p, s, q, t, keep = call(
        merge_body, [field, two, two] + [field] * 6 + [dots],
        *exchanged(nlow, nhigh), summed(sums), low, high, z, wlow, whigh, m, scalars=0,
    )
    m, n, sums = call(
        fourth_body, [field, field, dots], *exchanged(wlow, whigh), z, r, s, q, t, scalars=0
    )
    return tuple(call(
        finish_body, [right_side.shape] * 2,
        summed(sums), z, wlow, whigh, m, n, x, r, p, s, q, t, keep,
        scalars=0, scratch=[pltpu.VMEM((256, 128), F32)] * 2,
    ))


def solution(mesh):
    cells = P("px", "py", None)
    in_specs = (cells, cells, cells, cells, P(None, "px", "py", None))
    return jax.shard_map(local, mesh=mesh, in_specs=in_specs, out_specs=(cells, cells), check_vma=False)
```

```python
import jax
import jax.numpy as jnp
from jax import lax
from jax.experimental import pallas as pl
from jax.experimental.pallas import tpu as pltpu
from jax.sharding import PartitionSpec as P

OMEGA = 2.0 / 3.0
REST = 1.0 - OMEGA
FACES = (32.0, 16.0, 8.0)
F32 = jnp.float32


def call(body, outs, *args, scalars=1, scratch=(), flops=2_000_000, far=0):
    smem = pl.BlockSpec(memory_space=pltpu.SMEM)
    vmem = pl.BlockSpec(memory_space=pltpu.VMEM)
    hbm = pl.BlockSpec(memory_space=pltpu.HBM)
    specs = [smem] * scalars + [hbm] * far + [vmem] * (len(args) - scalars - far)
    return pl.pallas_call(
        body,
        out_shape=[jax.ShapeDtypeStruct(shape, F32) for shape in outs],
        in_specs=specs,
        out_specs=[vmem] * len(outs),
        scratch_shapes=list(scratch),
        compiler_params=pltpu.CompilerParams(vmem_limit_bytes=20 * 1024 * 1024),
        cost_estimate=pl.CostEstimate(flops=flops, bytes_accessed=1_000_000, transcendentals=0),
    )(*args)


def along_z(value):
    lane = lax.broadcasted_iota(jnp.int32, value.shape, value.ndim - 1)
    sub = lax.broadcasted_iota(jnp.int32, value.shape, value.ndim - 2)
    after = pltpu.roll(value, 127, value.ndim - 1)
    before = pltpu.roll(value, 1, value.ndim - 1)
    after_row = jnp.where(sub == 7, 0.0, pltpu.roll(after, 7, value.ndim - 2))
    before_row = jnp.where(sub == 0, 0.0, pltpu.roll(before, 1, value.ndim - 2))
    return jnp.where(lane == 127, after_row, after) + jnp.where(lane == 0, before_row, before)


def by_eight(value, ahead):
    lane = lax.broadcasted_iota(jnp.int32, value.shape, value.ndim - 1)
    if ahead:
        moved = pltpu.roll(value, 120, value.ndim - 1)
        return jnp.where(lane >= 120, pltpu.roll(moved, 7, value.ndim - 2), moved)
    moved = pltpu.roll(value, 8, value.ndim - 1)
    return jnp.where(lane < 8, pltpu.roll(moved, 1, value.ndim - 2), moved)


def beside(below, here, above):
    count = here.shape[0]
    inner = here[1 : count - 1]
    return below + above + here[0 : count - 2] + here[2:count] + along_z(inner)


def enter_body(b_hbm, d_hbm, a_hbm, cdiag_hbm, link_hbm, low_ref, high_ref, coarse_ref,
               b_ref, d_ref, a_ref, cdiag_ref, link_ref, sems):
    copies = [
        pltpu.make_async_copy(source, target, sems.at[k])
        for k, (source, target) in enumerate((
            (b_hbm, b_ref), (d_hbm, d_ref), (a_hbm, a_ref), (cdiag_hbm, cdiag_ref), (link_hbm, link_ref)
        ))
    ]
    for copy in copies:
        copy.start()
    for copy in copies:
        copy.wait()
    rows = []
    for ref in (cdiag_ref, link_ref.at[0], link_ref.at[1], link_ref.at[2]):
        rows = rows + [ref[c // 2, c % 2 : c % 2 + 1, :] for c in range(4)]
    coarse_ref[...] = jnp.concatenate(rows, axis=0)
    lane = lax.broadcasted_iota(jnp.int32, (8, 128), 1)
    for x in range(4):
        for s in range(8):
            part = slice(s * 128, (s + 1) * 128)
            b = b_ref[x, :, part]
            d = d_ref[x, :, part]
            home = (lane + s * 128) // 8
            o = ((a_ref[x, :, part] & 127) - home).astype(F32)
            ref = low_ref if x < 2 else high_ref
            at = (x % 2) * 64 + s
            ref[pl.ds(at, 8, stride=8), :] = b
            ref[pl.ds(128 + at, 8, stride=8), :] = d
            if x < 3:
                low_ref[pl.ds(256 + x * 64 + s, 8, stride=8), :] = o
            if x > 0:
                high_ref[pl.ds(256 + (x - 1) * 64 + s, 8, stride=8), :] = o


def field_rows(low, high, xlow, xhigh, base):
    return [ref.at[base + k] for ref in (xlow, low, high, xhigh) for k in range(2)]


def offset_rows(low, high, xlow, xhigh):
    return [ref.at[4 + k] for ref, ks in ((xlow, (0, 1, 2)), (low, (0, 1, 2)), (high, (2,)), (xhigh, (0, 1, 2))) for k in ks]


SIDE = {2: (0, 2), 3: (2, 2), 4: (4, 2), 5: (6, 2), 1: (8, 1), 6: (9, 1)}
WIDE = {3: (0, 3), 4: (3, 3), 5: (6, 3), 6: (9, 3), 2: (12, 2), 7: (14, 2), 1: (16, 1), 8: (17, 1)}


def send_sides(spots, rows, base, first_ref, last_ref):
    for x, (at, count) in spots.items():
        first_ref[base + at : base + at + count] = rows[x][0:count]
        last_ref[base + at : base + at + count] = rows[x][8 - count : 8]


def side(ref, spots, x, base, width, left):
    at, count = spots.get(x, (0, 0))
    zero = jnp.zeros((width - count, 8, 128), F32)
    if count == 0:
        return zero
    value = ref[base + at : base + at + count]
    if count == width:
        return value
    return jnp.concatenate([zero, value] if left else [value, zero], axis=0)


def pack_first_body(low_ref, high_ref, xlow_ref, xhigh_ref, first_ref, last_ref):
    four = (low_ref, high_ref, xlow_ref, xhigh_ref)
    for f in range(2):
        send_sides(SIDE, [ref[...] for ref in field_rows(*four, 2 * f)], 10 * f, first_ref, last_ref)
    send_sides(WIDE, [ref[...] for ref in offset_rows(*four)], 20, first_ref, last_ref)


def setup_body(me_ref, low_ref, high_ref, xlow_ref, xhigh_ref, ylow_ref, yhigh_ref, inverse_ref, scale_ref, offset_ref):
    px, py, last_x, last_y = me_ref[0], me_ref[1], me_ref[2], me_ref[3]
    below = jnp.where(px > 0, 1.0, 0.0).astype(F32)
    above = jnp.where(px < last_x, 1.0, 0.0).astype(F32)
    left = jnp.where(py > 0, 1.0, 0.0).astype(F32)
    right = jnp.where(py < last_y, 1.0, 0.0).astype(F32)
    four = (low_ref, high_ref, xlow_ref, xhigh_ref)
    for x, ref in enumerate(field_rows(*four, 2)):
        s_mid = 6.0 + ref[...]
        s_left = 6.0 + side(ylow_ref, SIDE, x, 10, 2, True)
        s_right = 6.0 + side(yhigh_ref, SIDE, x, 10, 2, False)
        i_mid, i_left, i_right = 1.0 / s_mid, left / s_left, right / s_right
        if x < 2 or x > 5:
            seen = below if x < 2 else above
            i_mid, i_left, i_right = i_mid * seen, i_left * seen, i_right * seen
        inverse_ref[x, 0:2] = i_left
        inverse_ref[x, 2:10] = i_mid
        inverse_ref[x, 10:12] = i_right
        if 1 <= x <= 6:
            scale_ref[x - 1, 0:1] = s_left[1:2]
            scale_ref[x - 1, 1:9] = s_mid
            scale_ref[x - 1, 9:10] = s_right[0:1]
    for x, ref in enumerate(offset_rows(*four)):
        offset_ref[x, 0:3] = side(ylow_ref, WIDE, x, 20, 3, True)
        offset_ref[x, 3:11] = ref[...]
        offset_ref[x, 11:14] = side(yhigh_ref, WIDE, x, 20, 3, False)


def padded(value, width):
    zero = jnp.zeros((width, 8, 128), F32)
    return jnp.concatenate([zero, value, zero], axis=0)


def contribute_body(low_ref, high_ref, inverse_ref, offset_ref, share_ref, down_ref, up_ref):
    share = shares(low_ref, high_ref, inverse_ref, offset_ref)
    share_ref[...] = share
    for ref, cells in ((down_ref, low_ref), (up_ref, high_ref)):
        for k in range(2):
            ref[8 * k : 8 * k + 8] = cells[k]
            ref[16 + k] = share[8 * k : 8 * k + 8]


def contribute_and_sum_body(low_ref, high_ref, inverse_ref, offset_ref, dots_ref, send_ref):
    share = shares(low_ref, high_ref, inverse_ref, offset_ref)
    more = jnp.concatenate([dots_ref[...], jnp.zeros((7, 128), F32)], axis=0)
    for j in range(send_ref.shape[0]):
        send_ref[j, 0:16] = share
        send_ref[j, 16:24] = more


def shares(low_ref, high_ref, inverse_ref, offset_ref):
    vector = [half(low_ref, high_ref, x) for x in range(4)]
    smooth = [OMEGA * vector[x] * inverse_ref[x + 2, 2:10] for x in range(4)]
    remains = [padded(smooth[0], 1)]
    for x in range(4):
        around = padded(smooth[x], 1)
        center = REST * vector[x] + (around[0:8] + around[2:10] + along_z(smooth[x]))
        for other in (x - 1, x + 1):
            if 0 <= other < 4:
                center = center + smooth[other]
        remains.append(jnp.concatenate([smooth[x][0:1], center, smooth[x][7:8]], axis=0))
    remains.append(padded(smooth[3], 1))
    shrunk = [remains[x] * inverse_ref[x + 1, 1:11] for x in range(6)]
    cells = []
    for x in range(8):
        near = None
        for other in (x - 2, x):
            if 0 <= other < 6:
                near = shrunk[other] if near is None else near + shrunk[other]
        if 1 <= x <= 6:
            near = padded(near + along_z(shrunk[x - 1]), 1)
            wide = padded(shrunk[x - 1], 2)
            value = REST * padded(remains[x - 1], 1) + OMEGA * (near + (wide[0:12] + wide[2:14]))
        else:
            value = padded(OMEGA * near, 1)
        value = jnp.where(inverse_ref[x] > 0.0, value, 0.0)
        offset = offset_ref[x + 1, 1:13]
        cells.append((
            jnp.where(jnp.abs(offset) < 0.5, value, 0.0),
            jnp.where(offset > 0.5, value, 0.0),
            jnp.where(offset < -0.5, value, 0.0),
        ))
    sums = []
    for start, stop in ((0, 2), (2, 6), (6, 10), (10, 12)):
        for i in range(4):
            here, up, down = (
                jnp.sum(cells[2 * i][k][start:stop], axis=0) + jnp.sum(cells[2 * i + 1][k][start:stop], axis=0)
                for k in range(3)
            )
            sums.append(here + by_eight(up, False) + by_eight(down, True))
    return jnp.concatenate(grouped_rows(sums), axis=0)


def grouped_rows(sums):
    stacked = jnp.concatenate(sums, axis=0)
    row = lax.broadcasted_iota(jnp.int32, (128, 128), 0)
    col = lax.broadcasted_iota(jnp.int32, (128, 128), 1)
    group = jnp.where(row // 8 == col % 16, 1.0, 0.0).astype(F32)
    grouped = jnp.dot(stacked, group, preferred_element_type=F32, precision=lax.Precision.HIGHEST)
    sub = lax.broadcasted_iota(jnp.int32, (8, 128), 0)
    lane = lax.broadcasted_iota(jnp.int32, (8, 128), 1)
    return [
        jnp.sum(jnp.where(lane // 16 == sub, grouped[8 * c : 8 * c + 8], 0.0), axis=0, keepdims=True)
        for c in range(len(sums))
    ]


def pack_rows(mids, row, first_ref, last_ref, early_ref, late_ref):
    send_sides(SIDE, [mid() for mid in mids], 0, first_ref, last_ref)
    zero = jnp.zeros((6, 128), F32)
    for j in range(4):
        rows = []
        for d in range(-2, 3):
            rows.append(row(d, 4 * j + 1) + row(d - 1, 4 * j + 3))
            rows.append(row(d, 4 * j + 2) + row(d + 1, 4 * j))
        tile = jnp.concatenate(rows + [zero], axis=0)
        ref = early_ref if j < 2 else late_ref
        ref[16 * (j % 2) : 16 * (j % 2) + 16] = tile
        for k in range(2):
            first_ref[10 + 2 * j + k] = tile[8 * k : 8 * k + 8]
            last_ref[10 + 2 * j + k] = tile[8 * k : 8 * k + 8]


def pack_body(low_ref, high_ref, below3_ref, below2_ref, below_ref, share_ref, above_ref, above2_ref, above3_ref, *outs):
    flat = {-3: below3_ref, -2: below2_ref, 0: share_ref, 2: above2_ref, 3: above3_ref}
    joined = {-1: below_ref, 1: above_ref}

    def row(d, at):
        if d in flat:
            return flat[d][at : at + 1, :]
        return joined[d][16 + at // 8, at % 8 : at % 8 + 1, :]

    pack_rows(row_blocks(low_ref, high_ref, below_ref, above_ref), row, *outs)


def pack_and_sum_body(me_ref, low_ref, high_ref, below_ref, above_ref, got_ref, *outs):
    count = got_ref.shape[0]
    spots = {d: lax.rem(me_ref[0] + (d + count), count) for d in range(-3, 4)}

    def row(d, at):
        return got_ref[spots[d], at : at + 1, :]

    pack_rows(row_blocks(low_ref, high_ref, below_ref, above_ref), row, *outs[:4])
    total, rest = total_of(got_ref, 16, None)
    tile = jnp.concatenate([total, rest, jnp.zeros((6, 128), F32)], axis=0)
    for j in range(outs[4].shape[0]):
        outs[4][j] = tile


def row_blocks(low_ref, high_ref, below_ref, above_ref):
    def sent(ref, k):
        return lambda: ref[8 * k : 8 * k + 8]

    def own(ref, k):
        return lambda: ref[k]

    blocks = [sent(below_ref, k) for k in range(2)] + [own(low_ref, k) for k in range(2)]
    return blocks + [own(high_ref, k) for k in range(2)] + [sent(above_ref, k) for k in range(2)]


def smoothed_rows(vector, inverse_ref):
    smooth = [OMEGA * vector(x) * inverse_ref[x] for x in range(8)]
    remains = [
        REST * vector(x)[1:11] + beside(smooth[x - 1][1:11], smooth[x], smooth[x + 1][1:11]) for x in range(1, 7)
    ]
    return [smooth[x][1:11] for x in range(1, 7)], remains


def smoothed(low, high, below, above, left, right, inverse_ref):
    mids = row_blocks(low, high, below, above)

    def vector(x):
        return jnp.concatenate([side(left, SIDE, x, 0, 2, True), mids[x](), side(right, SIDE, x, 0, 2, False)], axis=0)

    return smoothed_rows(vector, inverse_ref)


def restrict_body(low, high, xlow, xhigh, ylow, yhigh, inverse_ref, offset_ref, coarse_ref,
                  smooth_ref, remain_ref, send_ref):
    mids = [ref.at[k] for ref in (xlow, low, high, xhigh) for k in range(2)]

    def vector(x):
        return jnp.concatenate(
            [side(ylow, SIDE, x, 0, 2, True), mids[x][...], side(yhigh, SIDE, x, 0, 2, False)], axis=0
        )

    smooth, full = smoothed_rows(vector, inverse_ref)
    shrunk, remains = [], []
    for x in range(6):
        smooth_ref[x] = smooth[x]
        remain_ref[x] = full[x]
        remains.append(full[x][1:9])
        shrunk.append(full[x] * inverse_ref[x + 1, 1:11])
    sums = []
    for big_x in range(2):
        parts = []
        for x in (2 * big_x, 2 * big_x + 1):
            near = beside(shrunk[x][1:9], shrunk[x + 1], shrunk[x + 2][1:9])
            reduced = REST * remains[x + 1] + OMEGA * near
            offset = offset_ref[x + 3, 3:11]
            parts.append((
                jnp.where(jnp.abs(offset) < 0.5, reduced, 0.0),
                jnp.where(offset > 0.5, reduced, 0.0),
                jnp.where(offset < -0.5, reduced, 0.0),
            ))
        for big_y in range(2):
            cols = slice(4 * big_y, 4 * big_y + 4)
            here, up, down = (
                jnp.sum(parts[0][k][cols], axis=0) + jnp.sum(parts[1][k][cols], axis=0) for k in range(3)
            )
            sums.append(here + by_eight(up, False) + by_eight(down, True))
    send_ref[0:8] = jnp.concatenate(grouped_rows(sums) + [jnp.zeros((4, 128), F32)], axis=0)
    send_ref[8:24] = coarse_ref[...]


def window_rows(pieces, start):
    return [
        [ref[start + 2 * big_x + big_y : start + 2 * big_x + big_y + 1, :] for ref in pieces for big_x in range(2)]
        for big_y in range(2)
    ]


def window_first_body(*refs):
    pieces, send_ref = refs[:5], refs[5]
    zero = jnp.zeros((6, 128), F32)
    early, late = window_rows(pieces, 0)
    send_ref[0:32] = jnp.concatenate(early + [zero] + late + [zero], axis=0)
    rows = []
    for f in range(4):
        early, late = window_rows(pieces, 8 + 4 * f)
        rows = rows + early + late
    send_ref[32:112] = jnp.concatenate(rows, axis=0)


SPOTS = ((-2, 1), (-1, 0), (-1, 1), (0, 0), (0, 1), (1, 0), (1, 1), (2, 0))


def shift_x(value, ahead):
    return pltpu.roll(value, 15 if ahead else 1, 0)


def shift_k(value, ahead):
    return pltpu.roll(value, 127 if ahead else 1, 1)


def coarse_setup_body(me_ref, *refs):
    pieces, coef_ref = refs[:5], refs[5]
    px, py, last_x, last_y = me_ref[0], me_ref[1], me_ref[2], me_ref[3]
    row = lax.broadcasted_iota(jnp.int32, (16, 128), 0)
    lane = lax.broadcasted_iota(jnp.int32, (16, 128), 1)
    pad = jnp.zeros((6, 128), F32)
    where_x = 2 * px - 4 + row
    inside_x = (where_x >= 0) & (where_x < 2 * (last_x + 1)) & (row < 10)

    def take(y, f):
        d, big_y = SPOTS[y]
        start = 32 + 20 * f + 10 * big_y
        return jnp.concatenate([pieces[d + 2][start : start + 10, :], pad], axis=0)

    links = [[FACES[f - 1] * take(y, f) for y in range(8)] for f in range(1, 4)]
    for y in range(8):
        where_y = 2 * py - 3 + y
        seen = jnp.where((where_y >= 0) & (where_y < 2 * (last_y + 1)), 1.0, 0.0).astype(F32)
        diag = jnp.where(inside_x, take(y, 0), 1.0)
        inverse = jnp.where(inside_x, seen / diag, 0.0)
        coef_ref[0, y] = inverse
        if 1 <= y <= 6:
            coef_ref[1, y] = links[0][y] * inverse
            coef_ref[2, y] = shift_x(links[0][y], False) * inverse
            coef_ref[3, y] = links[1][y] * inverse
            coef_ref[4, y] = links[1][y - 1] * inverse
            coef_ref[5, y] = jnp.where(lane < 127, links[2][y] * inverse, 0.0)
            coef_ref[6, y] = jnp.where(lane > 0, shift_k(links[2][y], False) * inverse, 0.0)
        else:
            for f in range(1, 7):
                coef_ref[f, y] = jnp.zeros((16, 128), F32)


def dots_of(pairs):
    lane = lax.broadcasted_iota(jnp.int32, (1, 128), 1)
    out = jnp.zeros((1, 128), F32)
    for k, value in enumerate(pairs):
        out = jnp.where(lane == k, jnp.sum(value), out)
    return out


def first_sums(pieces):
    return [pieces[d + 2][16 * big_y : 16 * big_y + 16, :] for d, big_y in SPOTS]


def shared_sums(left2_ref, left_ref, early_ref, late_ref, right_ref, right2_ref):
    def share(d, j):
        if d in (-1, 1):
            ref = left_ref if d < 0 else right_ref
            return ref[10 + 2 * j : 12 + 2 * j].reshape(16, 128)
        ref = {-2: left2_ref, 0: early_ref if j < 2 else late_ref, 2: right2_ref}[d]
        return ref[16 * (j % 2) : 16 * (j % 2) + 16, :]

    return [share(d, big_y + 1) + (share(d - 1, 3) if big_y == 0 else share(d + 1, 0)) for d, big_y in SPOTS]


def correct_rows(sums, coef_ref, smooth, remain, inverse_ref, scale_ref, offset_ref):
    start = [sums[y] * coef_ref[0, y] for y in range(8)]

    def sweep(now, y):
        here = now[y]
        total = start[y] + coef_ref[1, y] * shift_x(here, True) + coef_ref[2, y] * shift_x(here, False)
        total = total + coef_ref[3, y] * now[y + 1] + coef_ref[4, y] * now[y - 1]
        return total + coef_ref[5, y] * shift_k(here, True) + coef_ref[6, y] * shift_k(here, False)

    second = [None] + [sweep(start, y) for y in range(1, 7)] + [None]
    third = [None, None] + [sweep(second, y) for y in range(2, 6)]
    sub = lax.broadcasted_iota(jnp.int32, (8, 128), 0)
    lane = lax.broadcasted_iota(jnp.int32, (8, 128), 1)
    index = sub * 16 + lane // 8

    def spread_out(tile, x):
        wide = jnp.broadcast_to(tile[x + 4 : x + 5, :], (8, 128))
        return jnp.take_along_axis(wide, index, axis=1)

    tables = [[], [], []]
    for y in range(2, 6):
        for k, tile in enumerate((third[y], shift_k(third[y], True), shift_k(third[y], False))):
            tables[k].append([spread_out(tile, x) for x in range(-2, 4)])
    counts = (3, 4, 4, 3)

    def lifted(x):
        big_x = x // 2
        here, up, down = (
            jnp.concatenate(
                [jnp.broadcast_to(tables[k][y][big_x + 2][None], (counts[y], 8, 128)) for y in range(4)], axis=0
            )
            for k in range(3)
        )
        offset = offset_ref[x + 3]
        return jnp.where(offset > 0.5, up, jnp.where(offset < -0.5, down, here))

    lifts = [lifted(x) for x in range(-3, 7)]
    spreads = []
    for x in range(8):
        near = beside(lifts[x][1:13], lifts[x + 1], lifts[x + 2][1:13])
        spreads.append(REST * lifts[x + 1][1:13] + OMEGA * (inverse_ref[x] * near))
    shaped = []
    for x in range(6):
        near = beside(spreads[x][1:11], spreads[x + 1], spreads[x + 2][1:11])
        spread = spreads[x + 1][1:11]
        left = remain[x] - (scale_ref[x] * spread - near)
        shaped.append(smooth[x] + spread + OMEGA * (inverse_ref[x + 1, 1:11] * left))
    for x in range(4):
        near = beside(shaped[x][1:9], shaped[x + 1], shaped[x + 2][1:9])
        own = shaped[x + 1][1:9]
        yield x, own, scale_ref[x + 1, 1:9] * own - near


def put(low_ref, high_ref, x, value):
    (low_ref if x < 2 else high_ref)[x % 2] = value


def half(low_ref, high_ref, x):
    return (low_ref if x < 2 else high_ref)[x % 2]


def products(left, right):
    return [jnp.sum(a * b, axis=0) for a in left for b in right]


def begin_body(*refs):
    pieces, fixed, (z_ref, wlow_ref, whigh_ref) = refs[:5], refs[5:11], refs[11:]
    for x, z, w in correct_rows(first_sums(pieces), *fixed):
        z_ref[x] = z
        put(wlow_ref, whigh_ref, x, w)


def corrected(refs):
    left2, early, late, right2, low, high, below, above, left, right, coef = refs[:11]
    fixed = refs[11:14]
    smooth, remain = smoothed(low, high, below, above, left, right, fixed[0])
    return correct_rows(shared_sums(left2, left, early, late, right, right2), coef, smooth, remain, *fixed)


def second_body(*refs):
    low_ref, high_ref, z_ref, m_ref, nlow_ref, nhigh_ref, dots_ref = refs[14:]
    wlow_ref, whigh_ref = refs[4:6]
    sums = [jnp.zeros((8, 128), F32)] * 6
    for x, m, n in corrected(refs[:14]):
        m_ref[x] = m
        put(nlow_ref, nhigh_ref, x, n)
        here = products((half(low_ref, high_ref, x), half(wlow_ref, whigh_ref, x), n), (z_ref[x], m))
        sums = [a + b for a, b in zip(sums, here)]
    dots_ref[...] = dots_of(sums)


def fourth_body(*refs):
    z_ref, r_ref, s_ref, q_ref, t_ref, m_ref, n_ref, dots_ref = refs[14:]
    wlow_ref, whigh_ref = refs[4:6]
    sums = [jnp.zeros((8, 128), F32)] * 15
    for x, m, n in corrected(refs[:14]):
        m_ref[x] = m
        n_ref[x] = n
        here = products((r_ref[x], half(wlow_ref, whigh_ref, x), s_ref[x], n, t_ref[x]), (z_ref[x], m, q_ref[x]))
        sums = [a + b for a, b in zip(sums, here)]
    dots_ref[...] = dots_of(sums)


def two_sum(a, b):
    total = a + b
    part = total - a
    return total, (a - (total - part)) + (b - part)


def split(a):
    wide = a * 4097.0
    high = wide - (wide - a)
    return high, a - high


def two_product(a, b):
    product = a * b
    a_high, a_low = split(a)
    b_high, b_low = split(b)
    return product, a_low * b_low - (((product - a_high * b_high) - a_low * b_high) - a_high * b_low)


def pair_add(a, b):
    total, rest = two_sum(a[0], b[0])
    return two_sum(total, rest + (a[1] + b[1]))


def pair_scale(a, factor):
    product, rest = two_product(a[0], factor)
    return two_sum(product, rest + a[1] * factor)


def pair_times(a, b):
    product, rest = two_product(a[0], b[0])
    return two_sum(product, rest + (a[0] * b[1] + a[1] * b[0]))


def total_of(got_ref, row, rest_row):
    total = got_ref[0, row : row + 1, :]
    rest = jnp.zeros((1, 128), F32) if rest_row is None else got_ref[0, rest_row : rest_row + 1, :]
    for j in range(1, got_ref.shape[0]):
        total, lost = two_sum(total, got_ref[j, row : row + 1, :])
        rest = rest + lost
        if rest_row is not None:
            rest = rest + got_ref[j, rest_row : rest_row + 1, :]
    return total, rest


def pairs_of(got_ref, row, rest_row, count):
    total, rest = total_of(got_ref, row, rest_row)
    total, rest = two_sum(total, rest)
    return [
        (jnp.broadcast_to(total[:, k : k + 1], (1, 128)), jnp.broadcast_to(rest[:, k : k + 1], (1, 128)))
        for k in range(count)
    ]


def form(table, left, weights):
    out = None
    for i, row in enumerate(left):
        for j, entry in enumerate(table[row]):
            factor = None
            for w in (weights[i], weights[j]):
                if w is not None:
                    factor = w if factor is None else pair_times(factor, w)
            term = entry if factor is None else pair_times(entry, factor)
            out = term if out is None else pair_add(out, term)
    return out[0] + out[1]


def tiled(row):
    return jnp.broadcast_to(row, (8, 128))[None]


def negated(pair):
    return -pair[0], -pair[1]


def merge_body(*refs):
    got_ref, low_ref, high_ref, z_ref, wlow_ref, whigh_ref, m_ref = refs[14:21]
    nlow_ref, nhigh_ref = refs[4:6]
    zo_ref, wolow_ref, wohigh_ref, xo_ref, ro_ref, po_ref, so_ref, qo_ref, to_ref, keep_ref = refs[21:]
    sums = pairs_of(got_ref, 0, 1, 6)
    table = [sums[0:2], sums[2:4], sums[4:6]]
    gamma0 = table[0][0][0]
    alpha0 = gamma0 / table[1][0][0]
    weights = (None, negated((alpha0, jnp.zeros_like(alpha0))))
    gamma1 = form(table, (0, 1), weights)
    delta1 = form(table, (1, 2), weights)
    beta1 = gamma1 / gamma0
    alpha1 = gamma1 / (delta1 - beta1 * gamma1 / alpha0)
    lane = lax.broadcasted_iota(jnp.int32, (1, 128), 1)
    keep_ref[...] = jnp.where(lane == 0, gamma1, jnp.where(lane == 1, alpha1, 0.0))
    alpha0, alpha1, beta1 = tiled(alpha0), tiled(alpha1), tiled(beta1)
    for x, k, l in corrected(refs[:14]):
        z0, w0 = z_ref[x], half(wlow_ref, whigh_ref, x)
        m0, n0 = m_ref[x], half(nlow_ref, nhigh_ref, x)
        z1, w1 = z0 - alpha0 * m0, w0 - alpha0 * n0
        p, s = z1 + beta1 * z0, w1 + beta1 * w0
        q = (m0 - alpha0 * k) + beta1 * m0
        t = (n0 - alpha0 * l) + beta1 * n0
        xo_ref[x] = alpha0 * z0 + alpha1 * p
        ro_ref[x] = (half(low_ref, high_ref, x) - alpha0 * w0) - alpha1 * s
        zo_ref[x] = z1 - alpha1 * q
        put(wolow_ref, wohigh_ref, x, w1 - alpha1 * t)
        po_ref[x], so_ref[x], qo_ref[x], to_ref[x] = p, s, q, t


def spread_dots_body(dots_ref, send_ref):
    tile = jnp.concatenate([dots_ref[...], jnp.zeros((7, 128), F32)], axis=0)
    for j in range(send_ref.shape[0]):
        send_ref[j] = tile


def sum_dots_body(got_ref, send_ref):
    total, rest = total_of(got_ref, 0, None)
    tile = jnp.concatenate([total, rest, jnp.zeros((6, 128), F32)], axis=0)
    for j in range(send_ref.shape[0]):
        send_ref[j] = tile


def finish_body(got_ref, z_ref, wlow_ref, whigh_ref, m_ref, n_ref, x_ref, r_ref, p_ref, s_ref, q_ref, t_ref, keep_ref,
                xo_ref, ro_ref, xs_ref, rs_ref):
    sums = pairs_of(got_ref, 0, 1, 15)
    table = [sums[3 * k : 3 * k + 3] for k in range(5)]
    keep = keep_ref[...]
    gamma1 = jnp.broadcast_to(keep[:, 0:1], (1, 128))
    alpha1 = jnp.broadcast_to(keep[:, 1:2], (1, 128))
    gamma2 = table[0][0][0]
    beta2 = gamma2 / gamma1
    alpha2 = gamma2 / (table[1][0][0] - beta2 * gamma2 / alpha1)
    weights = (None, (-alpha2, jnp.zeros_like(alpha2)), two_product(-alpha2, beta2))
    gamma3 = form(table, (0, 1, 2), weights)
    delta3 = form(table, (1, 3, 4), weights)
    beta3 = gamma3 / gamma2
    alpha3 = gamma3 / (delta3 - beta3 * gamma3 / alpha2)
    alpha2, beta2, alpha3, beta3 = tiled(alpha2), tiled(beta2), tiled(alpha3), tiled(beta3)
    for x in range(4):
        z, w, q1, t1 = z_ref[x], half(wlow_ref, whigh_ref, x), q_ref[x], t_ref[x]
        p2, s2 = z + beta2 * p_ref[x], w + beta2 * s_ref[x]
        q2, t2 = m_ref[x] + beta2 * q1, n_ref[x] + beta2 * t1
        p3 = (z - alpha2 * q2) + beta3 * p2
        s3 = (w - alpha2 * t2) + beta3 * s2
        xs_ref[pl.ds(64 * x, 64), :] = ((x_ref[x] + alpha2 * p2) + alpha3 * p3).reshape(64, 128)
        rs_ref[pl.ds(64 * x, 64), :] = ((r_ref[x] - alpha2 * s2) - alpha3 * s3).reshape(64, 128)
    for x in range(4):
        for s in range(8):
            part = slice(s * 128, (s + 1) * 128)
            xo_ref[x, :, part] = xs_ref[pl.ds(64 * x + s, 8, stride=8), :]
            ro_ref[x, :, part] = rs_ref[pl.ds(64 * x + s, 8, stride=8), :]


def local(right_side, diagonal, aggregate_id, coarse_diag, coarse_link):
    count_x, count_y = lax.axis_size("px"), lax.axis_size("py")
    me = jnp.stack([lax.axis_index("px"), lax.axis_index("py"), count_x - 1, count_y - 1]).astype(jnp.int32)

    def both_ways(low, high, axis, far=1):
        count = lax.axis_size(axis)
        up = [(i, (i + far) % count) for i in range(count)]
        down = [(b, a) for a, b in up]
        return lax.ppermute(high, axis, up), lax.ppermute(low, axis, down)

    def around(value, axis, reach):
        sides = [both_ways(value, value, axis, far) for far in range(1, reach + 1)]
        return [low for low, _ in sides[::-1]] + [value] + [high for _, high in sides]

    def gather(value, axis):
        return lax.all_to_all(value, axis, 0, 0)

    two, field = (2, 8, 8, 128), (4, 8, 8, 128)
    given = (right_side, diagonal, aggregate_id, coarse_diag, coarse_link)
    low, high, coarse = call(
        enter_body, [(448, 128)] * 2 + [(16, 128)], *given, scalars=0, far=5,
        scratch=[pltpu.VMEM(a.shape, a.dtype) for a in given] + [pltpu.SemaphoreType.DMA((5,))],
    )
    low, high = low.reshape(7, 8, 8, 128), high.reshape(7, 8, 8, 128)
    xlow, xhigh = both_ways(low, high, "px")
    first, last = call(pack_first_body, [(38, 8, 128)] * 2, low, high, xlow, xhigh, scalars=0)
    ylow, yhigh = both_ways(first, last, "py")
    inverse, scale, offset = call(
        setup_body, [(8, 12, 8, 128), (6, 10, 8, 128), (10, 14, 8, 128)], me, low, high, xlow, xhigh, ylow, yhigh
    )
    mid, dots = (6, 10, 8, 128), (1, 128)
    smooth, remain, send = call(
        restrict_body, [mid, mid, (24, 128)],
        low, high, xlow, xhigh, ylow, yhigh, inverse, offset, coarse, scalars=0,
    )
    send, = call(window_first_body, [(112, 128)], *around(send, "px", 2), scalars=0)
    pieces = around(send, "py", 2)
    coef, = call(coarse_setup_body, [(7, 8, 16, 128)], me, *pieces)
    fixed = (inverse, scale, offset)
    z, wlow, whigh = call(begin_body, [field, two, two], *pieces, coef, smooth, remain, *fixed, scalars=0)

    packed = [(18, 8, 128)] * 2 + [(32, 128)] * 2

    def beside_y(low, high, below, above, first, last, early, late):
        left, right = both_ways(first, last, "py")
        left2, right2 = both_ways(early, late, "py", 2)
        return (left2, early, late, right2, low, high, below, above, left, right, coef, *fixed)

    def exchanged(low, high):
        share, down, up = call(
            contribute_body, [(16, 128), (18, 8, 128), (18, 8, 128)], low, high, inverse, offset, scalars=0
        )
        below, above = both_ways(down, up, "px")
        below2, above2 = both_ways(share, share, "px", 2)
        below3, above3 = both_ways(share, share, "px", 3)
        outs = call(
            pack_body, packed, low, high, below3, below2, below, share, above, above2, above3, scalars=0
        )
        return beside_y(low, high, below, above, *outs)

    def exchanged_and_summed(low, high, sums):
        send, = call(
            contribute_and_sum_body, [(count_x, 24, 128)], low, high, inverse, offset, sums, scalars=0
        )
        below, above = (a.reshape(16, 8, 128) for a in both_ways(low, high, "px"))
        *outs, send = call(
            pack_and_sum_body, packed + [(count_y, 8, 128)], me, low, high, below, above, gather(send, "px")
        )
        return *beside_y(low, high, below, above, *outs), gather(send, "py")

    def summed(sums):
        send, = call(spread_dots_body, [(count_x, 8, 128)], sums, scalars=0)
        send, = call(sum_dots_body, [(count_y, 8, 128)], gather(send, "px"), scalars=0)
        return gather(send, "py")

    m, nlow, nhigh, sums = call(
        second_body, [field, two, two, dots], *exchanged(wlow, whigh), low, high, z, scalars=0
    )
    z, wlow, whigh, x, r, p, s, q, t, keep = call(
        merge_body, [field, two, two] + [field] * 6 + [dots],
        *exchanged_and_summed(nlow, nhigh, sums), low, high, z, wlow, whigh, m, scalars=0,
    )
    m, n, sums = call(
        fourth_body, [field, field, dots], *exchanged(wlow, whigh), z, r, s, q, t, scalars=0
    )
    return tuple(call(
        finish_body, [right_side.shape] * 2,
        summed(sums), z, wlow, whigh, m, n, x, r, p, s, q, t, keep,
        scalars=0, scratch=[pltpu.VMEM((256, 128), F32)] * 2,
    ))


def solution(mesh):
    cells = P("px", "py", None)
    in_specs = (cells, cells, cells, cells, P(None, "px", "py", None))
    return jax.shard_map(local, mesh=mesh, in_specs=in_specs, out_specs=(cells, cells), check_vma=False)
```

```python
import jax
import jax.numpy as jnp
from jax import lax
from jax.experimental import pallas as pl
from jax.experimental.pallas import tpu as pltpu
from jax.sharding import PartitionSpec as P

OMEGA = 2.0 / 3.0
REST = 1.0 - OMEGA
FACES = (32.0, 16.0, 8.0)
F32 = jnp.float32


def call(body, outs, *args, scalars=1, scratch=(), flops=2_000_000, far=0):
    smem = pl.BlockSpec(memory_space=pltpu.SMEM)
    vmem = pl.BlockSpec(memory_space=pltpu.VMEM)
    hbm = pl.BlockSpec(memory_space=pltpu.HBM)
    specs = [smem] * scalars + [hbm] * far + [vmem] * (len(args) - scalars - far)
    return pl.pallas_call(
        body,
        out_shape=[jax.ShapeDtypeStruct(shape, F32) for shape in outs],
        in_specs=specs,
        out_specs=[vmem] * len(outs),
        scratch_shapes=list(scratch),
        compiler_params=pltpu.CompilerParams(vmem_limit_bytes=62_000_000 if far else 20 * 1024 * 1024),
        cost_estimate=pl.CostEstimate(flops=flops, bytes_accessed=1_000_000, transcendentals=0),
    )(*args)


def along_z(value):
    lane = lax.broadcasted_iota(jnp.int32, value.shape, value.ndim - 1)
    sub = lax.broadcasted_iota(jnp.int32, value.shape, value.ndim - 2)
    after = pltpu.roll(value, 127, value.ndim - 1)
    before = pltpu.roll(value, 1, value.ndim - 1)
    after_row = jnp.where(sub == 7, 0.0, pltpu.roll(after, 7, value.ndim - 2))
    before_row = jnp.where(sub == 0, 0.0, pltpu.roll(before, 1, value.ndim - 2))
    return jnp.where(lane == 127, after_row, after) + jnp.where(lane == 0, before_row, before)


def by_eight(value, ahead):
    lane = lax.broadcasted_iota(jnp.int32, value.shape, value.ndim - 1)
    if ahead:
        moved = pltpu.roll(value, 120, value.ndim - 1)
        return jnp.where(lane >= 120, pltpu.roll(moved, 7, value.ndim - 2), moved)
    moved = pltpu.roll(value, 8, value.ndim - 1)
    return jnp.where(lane < 8, pltpu.roll(moved, 1, value.ndim - 2), moved)


def beside(below, here, above):
    count = here.shape[0]
    inner = here[1 : count - 1]
    return below + above + here[0 : count - 2] + here[2:count] + along_z(inner)


def enter_body(b_hbm, d_hbm, a_hbm, cdiag_hbm, link_hbm, low_ref, high_ref, coarse_ref,
               b_ref, d_ref, a_ref, cdiag_ref, link_ref, sems):
    copies = [
        pltpu.make_async_copy(source, target, sems.at[k])
        for k, (source, target) in enumerate((
            (b_hbm, b_ref), (d_hbm, d_ref), (a_hbm, a_ref), (cdiag_hbm, cdiag_ref), (link_hbm, link_ref)
        ))
    ]
    for copy in copies:
        copy.start()
    for copy in copies:
        copy.wait()
    rows = []
    for ref in (cdiag_ref, link_ref.at[0], link_ref.at[1], link_ref.at[2]):
        rows = rows + [ref[c // 2, c % 2 : c % 2 + 1, :] for c in range(4)]
    coarse_ref[...] = jnp.concatenate(rows, axis=0)
    lane = lax.broadcasted_iota(jnp.int32, (8, 128), 1)
    for x in range(4):
        for s in range(8):
            part = slice(s * 128, (s + 1) * 128)
            b = b_ref[x, :, part]
            d = d_ref[x, :, part]
            home = (lane + s * 128) // 8
            o = ((a_ref[x, :, part] & 127) - home).astype(F32)
            ref = low_ref if x < 2 else high_ref
            at = (x % 2) * 64 + s
            ref[pl.ds(at, 8, stride=8), :] = b
            ref[pl.ds(128 + at, 8, stride=8), :] = d
            if x < 3:
                low_ref[pl.ds(256 + x * 64 + s, 8, stride=8), :] = o
            if x > 0:
                high_ref[pl.ds(256 + (x - 1) * 64 + s, 8, stride=8), :] = o


def field_rows(low, high, xlow, xhigh, base):
    return [ref.at[base + k] for ref in (xlow, low, high, xhigh) for k in range(2)]


def offset_rows(low, high, xlow, xhigh):
    return [ref.at[4 + k] for ref, ks in ((xlow, (0, 1, 2)), (low, (0, 1, 2)), (high, (2,)), (xhigh, (0, 1, 2))) for k in ks]


SIDE = {2: (0, 2), 3: (2, 2), 4: (4, 2), 5: (6, 2), 1: (8, 1), 6: (9, 1)}
WIDE = {3: (0, 3), 4: (3, 3), 5: (6, 3), 6: (9, 3), 2: (12, 2), 7: (14, 2), 1: (16, 1), 8: (17, 1)}


def send_sides(spots, rows, base, first_ref, last_ref):
    for x, (at, count) in spots.items():
        first_ref[base + at : base + at + count] = rows[x][0:count]
        last_ref[base + at : base + at + count] = rows[x][8 - count : 8]


def side(ref, spots, x, base, width, left):
    at, count = spots.get(x, (0, 0))
    zero = jnp.zeros((width - count, 8, 128), F32)
    if count == 0:
        return zero
    value = ref[base + at : base + at + count]
    if count == width:
        return value
    return jnp.concatenate([zero, value] if left else [value, zero], axis=0)


def pack_first_body(low_ref, high_ref, xlow_ref, xhigh_ref, first_ref, last_ref):
    four = (low_ref, high_ref, xlow_ref, xhigh_ref)
    for f in range(2):
        send_sides(SIDE, [ref[...] for ref in field_rows(*four, 2 * f)], 10 * f, first_ref, last_ref)
    send_sides(WIDE, [ref[...] for ref in offset_rows(*four)], 20, first_ref, last_ref)


def setup_body(me_ref, low_ref, high_ref, xlow_ref, xhigh_ref, ylow_ref, yhigh_ref, inverse_ref, scale_ref, offset_ref):
    px, py, last_x, last_y = me_ref[0], me_ref[1], me_ref[2], me_ref[3]
    below = jnp.where(px > 0, 1.0, 0.0).astype(F32)
    above = jnp.where(px < last_x, 1.0, 0.0).astype(F32)
    left = jnp.where(py > 0, 1.0, 0.0).astype(F32)
    right = jnp.where(py < last_y, 1.0, 0.0).astype(F32)
    four = (low_ref, high_ref, xlow_ref, xhigh_ref)
    for x, ref in enumerate(field_rows(*four, 2)):
        s_mid = 6.0 + ref[...]
        s_left = 6.0 + side(ylow_ref, SIDE, x, 10, 2, True)
        s_right = 6.0 + side(yhigh_ref, SIDE, x, 10, 2, False)
        i_mid, i_left, i_right = 1.0 / s_mid, left / s_left, right / s_right
        if x < 2 or x > 5:
            seen = below if x < 2 else above
            i_mid, i_left, i_right = i_mid * seen, i_left * seen, i_right * seen
        inverse_ref[x, 0:2] = i_left
        inverse_ref[x, 2:10] = i_mid
        inverse_ref[x, 10:12] = i_right
        if 1 <= x <= 6:
            scale_ref[x - 1, 0:1] = s_left[1:2]
            scale_ref[x - 1, 1:9] = s_mid
            scale_ref[x - 1, 9:10] = s_right[0:1]
    for x, ref in enumerate(offset_rows(*four)):
        offset_ref[x, 0:3] = side(ylow_ref, WIDE, x, 20, 3, True)
        offset_ref[x, 3:11] = ref[...]
        offset_ref[x, 11:14] = side(yhigh_ref, WIDE, x, 20, 3, False)


def padded(value, width):
    zero = jnp.zeros((width, 8, 128), F32)
    return jnp.concatenate([zero, value, zero], axis=0)


def contribute_body(low_ref, high_ref, inverse_ref, offset_ref, share_ref, down_ref, up_ref):
    share = shares(low_ref, high_ref, inverse_ref, offset_ref)
    share_ref[...] = share
    for ref, cells in ((down_ref, low_ref), (up_ref, high_ref)):
        for k in range(2):
            ref[8 * k : 8 * k + 8] = cells[k]
            ref[16 + k] = share[8 * k : 8 * k + 8]


def contribute_and_sum_body(low_ref, high_ref, inverse_ref, offset_ref, dots_ref, send_ref):
    share = shares(low_ref, high_ref, inverse_ref, offset_ref)
    more = jnp.concatenate([dots_ref[...], jnp.zeros((7, 128), F32)], axis=0)
    for j in range(send_ref.shape[0]):
        send_ref[j, 0:16] = share
        send_ref[j, 16:24] = more


def shares(low_ref, high_ref, inverse_ref, offset_ref):
    vector = [half(low_ref, high_ref, x) for x in range(4)]
    smooth = [OMEGA * vector[x] * inverse_ref[x + 2, 2:10] for x in range(4)]
    remains = [padded(smooth[0], 1)]
    for x in range(4):
        around = padded(smooth[x], 1)
        center = REST * vector[x] + (around[0:8] + around[2:10] + along_z(smooth[x]))
        for other in (x - 1, x + 1):
            if 0 <= other < 4:
                center = center + smooth[other]
        remains.append(jnp.concatenate([smooth[x][0:1], center, smooth[x][7:8]], axis=0))
    remains.append(padded(smooth[3], 1))
    shrunk = [remains[x] * inverse_ref[x + 1, 1:11] for x in range(6)]
    cells = []
    for x in range(8):
        near = None
        for other in (x - 2, x):
            if 0 <= other < 6:
                near = shrunk[other] if near is None else near + shrunk[other]
        if 1 <= x <= 6:
            near = padded(near + along_z(shrunk[x - 1]), 1)
            wide = padded(shrunk[x - 1], 2)
            value = REST * padded(remains[x - 1], 1) + OMEGA * (near + (wide[0:12] + wide[2:14]))
        else:
            value = padded(OMEGA * near, 1)
        value = jnp.where(inverse_ref[x] > 0.0, value, 0.0)
        offset = offset_ref[x + 1, 1:13]
        cells.append((
            jnp.where(jnp.abs(offset) < 0.5, value, 0.0),
            jnp.where(offset > 0.5, value, 0.0),
            jnp.where(offset < -0.5, value, 0.0),
        ))
    sums = []
    for start, stop in ((0, 2), (2, 6), (6, 10), (10, 12)):
        for i in range(4):
            here, up, down = (
                jnp.sum(cells[2 * i][k][start:stop], axis=0) + jnp.sum(cells[2 * i + 1][k][start:stop], axis=0)
                for k in range(3)
            )
            sums.append(here + by_eight(up, False) + by_eight(down, True))
    return jnp.concatenate(grouped_rows(sums), axis=0)


def grouped_rows(sums):
    stacked = jnp.concatenate(sums, axis=0)
    row = lax.broadcasted_iota(jnp.int32, (128, 128), 0)
    col = lax.broadcasted_iota(jnp.int32, (128, 128), 1)
    group = jnp.where(row // 8 == col % 16, 1.0, 0.0).astype(F32)
    grouped = jnp.dot(stacked, group, preferred_element_type=F32, precision=lax.Precision.HIGHEST)
    sub = lax.broadcasted_iota(jnp.int32, (8, 128), 0)
    lane = lax.broadcasted_iota(jnp.int32, (8, 128), 1)
    return [
        jnp.sum(jnp.where(lane // 16 == sub, grouped[8 * c : 8 * c + 8], 0.0), axis=0, keepdims=True)
        for c in range(len(sums))
    ]


def pack_rows(mids, row, first_ref, last_ref, early_ref, late_ref):
    send_sides(SIDE, [mid() for mid in mids], 0, first_ref, last_ref)
    zero = jnp.zeros((6, 128), F32)
    for j in range(4):
        rows = []
        for d in range(-2, 3):
            rows.append(row(d, 4 * j + 1) + row(d - 1, 4 * j + 3))
            rows.append(row(d, 4 * j + 2) + row(d + 1, 4 * j))
        tile = jnp.concatenate(rows + [zero], axis=0)
        ref = early_ref if j < 2 else late_ref
        ref[16 * (j % 2) : 16 * (j % 2) + 16] = tile
        for k in range(2):
            first_ref[10 + 2 * j + k] = tile[8 * k : 8 * k + 8]
            last_ref[10 + 2 * j + k] = tile[8 * k : 8 * k + 8]


def pack_body(low_ref, high_ref, below3_ref, below2_ref, below_ref, share_ref, above_ref, above2_ref, above3_ref, *outs):
    flat = {-3: below3_ref, -2: below2_ref, 0: share_ref, 2: above2_ref, 3: above3_ref}
    joined = {-1: below_ref, 1: above_ref}

    def row(d, at):
        if d in flat:
            return flat[d][at : at + 1, :]
        return joined[d][16 + at // 8, at % 8 : at % 8 + 1, :]

    pack_rows(row_blocks(low_ref, high_ref, below_ref, above_ref), row, *outs)


def pack_and_sum_body(me_ref, low_ref, high_ref, below_ref, above_ref, got_ref, *outs):
    count = got_ref.shape[0]
    spots = {d: lax.rem(me_ref[0] + (d + count), count) for d in range(-3, 4)}

    def row(d, at):
        return got_ref[spots[d], at : at + 1, :]

    pack_rows(row_blocks(low_ref, high_ref, below_ref, above_ref), row, *outs)
    total, rest = total_of(got_ref, 16, None)
    tile = jnp.concatenate([total, rest, jnp.zeros((6, 128), F32)], axis=0)
    for ref in outs[:2]:
        ref[18] = tile
    for ref in outs[2:]:
        ref[32:40] = tile


def row_blocks(low_ref, high_ref, below_ref, above_ref):
    def sent(ref, k):
        return lambda: ref[8 * k : 8 * k + 8]

    def own(ref, k):
        return lambda: ref[k]

    blocks = [sent(below_ref, k) for k in range(2)] + [own(low_ref, k) for k in range(2)]
    return blocks + [own(high_ref, k) for k in range(2)] + [sent(above_ref, k) for k in range(2)]


def smoothed_rows(vector, inverse_ref):
    smooth = [OMEGA * vector(x) * inverse_ref[x] for x in range(8)]
    remains = [
        REST * vector(x)[1:11] + beside(smooth[x - 1][1:11], smooth[x], smooth[x + 1][1:11]) for x in range(1, 7)
    ]
    return [smooth[x][1:11] for x in range(1, 7)], remains


def widened(low, high, below, above, left, right):
    mids = row_blocks(low, high, below, above)

    def vector(x):
        return jnp.concatenate([side(left, SIDE, x, 0, 2, True), mids[x](), side(right, SIDE, x, 0, 2, False)], axis=0)

    return [vector(x) for x in range(8)]


def restrict_body(low, high, xlow, xhigh, ylow, yhigh, inverse_ref, offset_ref, coarse_ref,
                  smooth_ref, remain_ref, send_ref):
    mids = [ref.at[k] for ref in (xlow, low, high, xhigh) for k in range(2)]

    def vector(x):
        return jnp.concatenate(
            [side(ylow, SIDE, x, 0, 2, True), mids[x][...], side(yhigh, SIDE, x, 0, 2, False)], axis=0
        )

    smooth, full = smoothed_rows(vector, inverse_ref)
    shrunk, remains = [], []
    for x in range(6):
        smooth_ref[x] = smooth[x]
        remain_ref[x] = full[x]
        remains.append(full[x][1:9])
        shrunk.append(full[x] * inverse_ref[x + 1, 1:11])
    sums = []
    for big_x in range(2):
        parts = []
        for x in (2 * big_x, 2 * big_x + 1):
            near = beside(shrunk[x][1:9], shrunk[x + 1], shrunk[x + 2][1:9])
            reduced = REST * remains[x + 1] + OMEGA * near
            offset = offset_ref[x + 3, 3:11]
            parts.append((
                jnp.where(jnp.abs(offset) < 0.5, reduced, 0.0),
                jnp.where(offset > 0.5, reduced, 0.0),
                jnp.where(offset < -0.5, reduced, 0.0),
            ))
        for big_y in range(2):
            cols = slice(4 * big_y, 4 * big_y + 4)
            here, up, down = (
                jnp.sum(parts[0][k][cols], axis=0) + jnp.sum(parts[1][k][cols], axis=0) for k in range(3)
            )
            sums.append(here + by_eight(up, False) + by_eight(down, True))
    send_ref[0:8] = jnp.concatenate(grouped_rows(sums) + [jnp.zeros((4, 128), F32)], axis=0)
    send_ref[8:24] = coarse_ref[...]


def window_rows(pieces, start):
    return [
        [ref[start + 2 * big_x + big_y : start + 2 * big_x + big_y + 1, :] for ref in pieces for big_x in range(2)]
        for big_y in range(2)
    ]


def window_first_body(*refs):
    pieces, send_ref = refs[:5], refs[5]
    zero = jnp.zeros((6, 128), F32)
    early, late = window_rows(pieces, 0)
    send_ref[0:32] = jnp.concatenate(early + [zero] + late + [zero], axis=0)
    rows = []
    for f in range(4):
        early, late = window_rows(pieces, 8 + 4 * f)
        rows = rows + early + late
    send_ref[32:112] = jnp.concatenate(rows, axis=0)


SPOTS = ((-2, 1), (-1, 0), (-1, 1), (0, 0), (0, 1), (1, 0), (1, 1), (2, 0))


def shift_x(value, ahead):
    return pltpu.roll(value, 15 if ahead else 1, 0)


def shift_k(value, ahead):
    return pltpu.roll(value, 127 if ahead else 1, 1)


def coarse_setup_body(me_ref, *refs):
    pieces, coef_ref = refs[:5], refs[5]
    px, py, last_x, last_y = me_ref[0], me_ref[1], me_ref[2], me_ref[3]
    row = lax.broadcasted_iota(jnp.int32, (16, 128), 0)
    lane = lax.broadcasted_iota(jnp.int32, (16, 128), 1)
    pad = jnp.zeros((6, 128), F32)
    where_x = 2 * px - 4 + row
    inside_x = (where_x >= 0) & (where_x < 2 * (last_x + 1)) & (row < 10)

    def take(y, f):
        d, big_y = SPOTS[y]
        start = 32 + 20 * f + 10 * big_y
        return jnp.concatenate([pieces[d + 2][start : start + 10, :], pad], axis=0)

    links = [[FACES[f - 1] * take(y, f) for y in range(8)] for f in range(1, 4)]
    for y in range(8):
        where_y = 2 * py - 3 + y
        seen = jnp.where((where_y >= 0) & (where_y < 2 * (last_y + 1)), 1.0, 0.0).astype(F32)
        diag = jnp.where(inside_x, take(y, 0), 1.0)
        inverse = jnp.where(inside_x, seen / diag, 0.0)
        coef_ref[0, y] = inverse
        if 1 <= y <= 6:
            coef_ref[1, y] = links[0][y] * inverse
            coef_ref[2, y] = shift_x(links[0][y], False) * inverse
            coef_ref[3, y] = links[1][y] * inverse
            coef_ref[4, y] = links[1][y - 1] * inverse
            coef_ref[5, y] = jnp.where(lane < 127, links[2][y] * inverse, 0.0)
            coef_ref[6, y] = jnp.where(lane > 0, shift_k(links[2][y], False) * inverse, 0.0)
        else:
            for f in range(1, 7):
                coef_ref[f, y] = jnp.zeros((16, 128), F32)


def dots_of(pairs):
    lane = lax.broadcasted_iota(jnp.int32, (1, 128), 1)
    out = jnp.zeros((1, 128), F32)
    for k, value in enumerate(pairs):
        out = jnp.where(lane == k, jnp.sum(value), out)
    return out


def first_sums(pieces):
    return [pieces[d + 2][16 * big_y : 16 * big_y + 16, :] for d, big_y in SPOTS]


def shared_sums(left2_ref, left_ref, early_ref, late_ref, right_ref, right2_ref):
    def share(d, j):
        if d in (-1, 1):
            ref = left_ref if d < 0 else right_ref
            return ref[10 + 2 * j : 12 + 2 * j].reshape(16, 128)
        ref = {-2: left2_ref, 0: early_ref if j < 2 else late_ref, 2: right2_ref}[d]
        return ref[16 * (j % 2) : 16 * (j % 2) + 16, :]

    return [share(d, big_y + 1) + (share(d - 1, 3) if big_y == 0 else share(d + 1, 0)) for d, big_y in SPOTS]


def correct_rows(sums, coef_ref, smooth, remain, inverse_ref, scale_ref, offset_ref):
    start = [sums[y] * coef_ref[0, y] for y in range(8)]

    def sweep(now, y):
        here = now[y]
        total = start[y] + coef_ref[1, y] * shift_x(here, True) + coef_ref[2, y] * shift_x(here, False)
        total = total + coef_ref[3, y] * now[y + 1] + coef_ref[4, y] * now[y - 1]
        return total + coef_ref[5, y] * shift_k(here, True) + coef_ref[6, y] * shift_k(here, False)

    second = [None] + [sweep(start, y) for y in range(1, 7)] + [None]
    third = [None, None] + [sweep(second, y) for y in range(2, 6)]
    sub = lax.broadcasted_iota(jnp.int32, (8, 128), 0)
    lane = lax.broadcasted_iota(jnp.int32, (8, 128), 1)
    index = sub * 16 + lane // 8

    def spread_out(tile, x):
        wide = jnp.broadcast_to(tile[x + 4 : x + 5, :], (8, 128))
        return jnp.take_along_axis(wide, index, axis=1)

    tables = [[], [], []]
    for y in range(2, 6):
        for k, tile in enumerate((third[y], shift_k(third[y], True), shift_k(third[y], False))):
            tables[k].append([spread_out(tile, x) for x in range(-2, 4)])
    counts = (3, 4, 4, 3)

    def lifted(x):
        big_x = x // 2
        here, up, down = (
            jnp.concatenate(
                [jnp.broadcast_to(tables[k][y][big_x + 2][None], (counts[y], 8, 128)) for y in range(4)], axis=0
            )
            for k in range(3)
        )
        offset = offset_ref[x + 3]
        return jnp.where(offset > 0.5, up, jnp.where(offset < -0.5, down, here))

    lifts = [lifted(x) for x in range(-3, 7)]
    spreads = []
    for x in range(8):
        near = beside(lifts[x][1:13], lifts[x + 1], lifts[x + 2][1:13])
        spreads.append(REST * lifts[x + 1][1:13] + OMEGA * (inverse_ref[x] * near))
    shaped = []
    for x in range(6):
        near = beside(spreads[x][1:11], spreads[x + 1], spreads[x + 2][1:11])
        spread = spreads[x + 1][1:11]
        left = remain[x] - (scale_ref[x] * spread - near)
        shaped.append(smooth[x] + spread + OMEGA * (inverse_ref[x + 1, 1:11] * left))
    for x in range(4):
        near = beside(shaped[x][1:9], shaped[x + 1], shaped[x + 2][1:9])
        own = shaped[x + 1][1:9]
        yield x, own, scale_ref[x + 1, 1:9] * own - near


def put(low_ref, high_ref, x, value):
    (low_ref if x < 2 else high_ref)[x % 2] = value


def half(low_ref, high_ref, x):
    return (low_ref if x < 2 else high_ref)[x % 2]


def products(left, right):
    return [jnp.sum(a * b, axis=0) for a in left for b in right]


def begin_body(*refs):
    pieces, fixed, (z_ref, wlow_ref, whigh_ref) = refs[:5], refs[5:11], refs[11:]
    for x, z, w in correct_rows(first_sums(pieces), *fixed):
        z_ref[x] = z
        put(wlow_ref, whigh_ref, x, w)


EXCHANGED = 10


def received(refs):
    left2, early, late, right2, low, high, below, above, left, right = refs
    return widened(low, high, below, above, left, right), shared_sums(left2, left, early, late, right, right2)


def corrected(vectors, sums, refs):
    coef, fixed = refs[0], refs[1:4]
    smooth, remain = smoothed_rows(lambda x: vectors[x], fixed[0])
    return correct_rows(sums, coef, smooth, remain, *fixed)


def second_body(*refs):
    low_ref, high_ref, z_ref, m_ref, nlow_ref, nhigh_ref, dots_ref = refs[14:]
    wlow_ref, whigh_ref = refs[4:6]
    sums = [jnp.zeros((8, 128), F32)] * 6
    for x, m, n in corrected(*received(refs[:10]), refs[10:14]):
        m_ref[x] = m
        put(nlow_ref, nhigh_ref, x, n)
        here = products((half(low_ref, high_ref, x), half(wlow_ref, whigh_ref, x), n), (z_ref[x], m))
        sums = [a + b for a, b in zip(sums, here)]
    dots_ref[...] = dots_of(sums)


def two_sum(a, b):
    total = a + b
    part = total - a
    return total, (a - (total - part)) + (b - part)


def split(a):
    wide = a * 4097.0
    high = wide - (wide - a)
    return high, a - high


def two_product(a, b):
    product = a * b
    a_high, a_low = split(a)
    b_high, b_low = split(b)
    return product, a_low * b_low - (((product - a_high * b_high) - a_low * b_high) - a_high * b_low)


def pair_add(a, b):
    total, rest = two_sum(a[0], b[0])
    return two_sum(total, rest + (a[1] + b[1]))


def pair_scale(a, factor):
    product, rest = two_product(a[0], factor)
    return two_sum(product, rest + a[1] * factor)


def pair_times(a, b):
    product, rest = two_product(a[0], b[0])
    return two_sum(product, rest + (a[0] * b[1] + a[1] * b[0]))


def total_of(got_ref, row, rest_row):
    total = got_ref[0, row : row + 1, :]
    rest = jnp.zeros((1, 128), F32) if rest_row is None else got_ref[0, rest_row : rest_row + 1, :]
    for j in range(1, got_ref.shape[0]):
        total, lost = two_sum(total, got_ref[j, row : row + 1, :])
        rest = rest + lost
        if rest_row is not None:
            rest = rest + got_ref[j, rest_row : rest_row + 1, :]
    return total, rest


def gathered(tiles):
    total, rest = tiles[0][0:1], tiles[0][1:2]
    for tile in tiles[1:]:
        total, lost = two_sum(total, tile[0:1])
        rest = rest + (lost + tile[1:2])
    return two_sum(total, rest)


def pairs_of(total, rest, count):
    return [
        (jnp.broadcast_to(total[:, k : k + 1], (1, 128)), jnp.broadcast_to(rest[:, k : k + 1], (1, 128)))
        for k in range(count)
    ]


def form(table, left, weights):
    out = None
    for i, row in enumerate(left):
        for j, entry in enumerate(table[row]):
            factor = None
            for w in (weights[i], weights[j]):
                if w is not None:
                    factor = w if factor is None else pair_times(factor, w)
            term = entry if factor is None else pair_times(entry, factor)
            out = term if out is None else pair_add(out, term)
    return out[0] + out[1]


def tiled(row):
    return jnp.broadcast_to(row, (8, 128))[None]


def negated(pair):
    return -pair[0], -pair[1]


def third_body(*refs):
    k_ref, llow_ref, lhigh_ref, part_ref = refs[14:]
    early, right2, left, right = refs[1], refs[3], refs[8], refs[9]
    total, rest = gathered([early[32:40, :], left[18], right[18], right2[32:40, :]])
    part_ref[...] = jnp.concatenate([total, rest, jnp.zeros((6, 128), F32)], axis=0)
    for x, k, l in corrected(*received(refs[:10]), refs[10:14]):
        k_ref[x] = k
        put(llow_ref, lhigh_ref, x, l)


def fourth_body(*refs):
    rows, window = zip(*(received(refs[10 * i : 10 * i + 10]) for i in range(3)))
    rest = refs[30:34]
    parts, refs = refs[34:38], refs[38:]
    low_ref, high_ref, z_ref, m_ref, k_ref = refs[:5]
    zo_ref, wolow_ref, wohigh_ref, mo_ref, no_ref, xo_ref, ro_ref, po_ref, so_ref, qo_ref, to_ref = refs[5:16]
    keep_ref, dots_ref = refs[16:]
    sums = pairs_of(*gathered([part[...] for part in parts]), 6)
    table = [sums[0:2], sums[2:4], sums[4:6]]
    gamma0 = table[0][0][0]
    alpha0 = gamma0 / table[1][0][0]
    weights = (None, negated((alpha0, jnp.zeros_like(alpha0))))
    gamma1 = form(table, (0, 1), weights)
    delta1 = form(table, (1, 2), weights)
    beta1 = gamma1 / gamma0
    alpha1 = gamma1 / (delta1 - beta1 * gamma1 / alpha0)
    lane = lax.broadcasted_iota(jnp.int32, (1, 128), 1)
    keep_ref[...] = jnp.where(lane == 0, gamma1, jnp.where(lane == 1, alpha1, 0.0))
    alphas = [(tiled(alpha0), tiled(alpha1), tiled(beta1)), (alpha0, alpha1, beta1)]

    def turned(w, n, l, alpha0, alpha1, beta1):
        t = (n - alpha0 * l) + beta1 * n
        return (w - alpha0 * n) - alpha1 * t, t

    vectors = [turned(*(rows[i][x] for i in range(3)), *alphas[0])[0] for x in range(8)]
    window = [turned(*(window[i][y] for i in range(3)), *alphas[1])[0] for y in range(8)]
    alpha0, alpha1, beta1 = alphas[0]
    sums = [jnp.zeros((8, 128), F32)] * 15
    for x, m2, n2 in corrected(vectors, window, rest):
        w0, n0, l = (rows[i][x + 2][2:10] for i in range(3))
        z0, m0, k = z_ref[x], m_ref[x], k_ref[x]
        w2, t = turned(w0, n0, l, *alphas[0])
        z2, q = turned(z0, m0, k, *alphas[0])
        p, s = (z0 - alpha0 * m0) + beta1 * z0, (w0 - alpha0 * n0) + beta1 * w0
        r2 = (half(low_ref, high_ref, x) - alpha0 * w0) - alpha1 * s
        xo_ref[x] = alpha0 * z0 + alpha1 * p
        ro_ref[x], zo_ref[x] = r2, z2
        put(wolow_ref, wohigh_ref, x, w2)
        mo_ref[x], no_ref[x] = m2, n2
        po_ref[x], so_ref[x], qo_ref[x], to_ref[x] = p, s, q, t
        sums = [a + b for a, b in zip(sums, products((r2, w2, s, n2, t), (z2, m2, q)))]
    dots_ref[...] = dots_of(sums)


def spread_dots_body(dots_ref, send_ref):
    tile = jnp.concatenate([dots_ref[...], jnp.zeros((7, 128), F32)], axis=0)
    for j in range(send_ref.shape[0]):
        send_ref[j] = tile


def sum_dots_body(got_ref, send_ref):
    total, rest = total_of(got_ref, 0, None)
    tile = jnp.concatenate([total, rest, jnp.zeros((6, 128), F32)], axis=0)
    for j in range(send_ref.shape[0]):
        send_ref[j] = tile


def finish_body(got_ref, z_ref, wlow_ref, whigh_ref, m_ref, n_ref, x_ref, r_ref, p_ref, s_ref, q_ref, t_ref, keep_ref,
                xo_ref, ro_ref, xs_ref, rs_ref):
    sums = pairs_of(*two_sum(*total_of(got_ref, 0, 1)), 15)
    table = [sums[3 * k : 3 * k + 3] for k in range(5)]
    keep = keep_ref[...]
    gamma1 = jnp.broadcast_to(keep[:, 0:1], (1, 128))
    alpha1 = jnp.broadcast_to(keep[:, 1:2], (1, 128))
    gamma2 = table[0][0][0]
    beta2 = gamma2 / gamma1
    alpha2 = gamma2 / (table[1][0][0] - beta2 * gamma2 / alpha1)
    weights = (None, (-alpha2, jnp.zeros_like(alpha2)), two_product(-alpha2, beta2))
    gamma3 = form(table, (0, 1, 2), weights)
    delta3 = form(table, (1, 3, 4), weights)
    beta3 = gamma3 / gamma2
    alpha3 = gamma3 / (delta3 - beta3 * gamma3 / alpha2)
    alpha2, beta2, alpha3, beta3 = tiled(alpha2), tiled(beta2), tiled(alpha3), tiled(beta3)
    for x in range(4):
        z, w, q1, t1 = z_ref[x], half(wlow_ref, whigh_ref, x), q_ref[x], t_ref[x]
        p2, s2 = z + beta2 * p_ref[x], w + beta2 * s_ref[x]
        q2, t2 = m_ref[x] + beta2 * q1, n_ref[x] + beta2 * t1
        p3 = (z - alpha2 * q2) + beta3 * p2
        s3 = (w - alpha2 * t2) + beta3 * s2
        xs_ref[pl.ds(64 * x, 64), :] = ((x_ref[x] + alpha2 * p2) + alpha3 * p3).reshape(64, 128)
        rs_ref[pl.ds(64 * x, 64), :] = ((r_ref[x] - alpha2 * s2) - alpha3 * s3).reshape(64, 128)
    for x in range(4):
        for s in range(8):
            part = slice(s * 128, (s + 1) * 128)
            xo_ref[x, :, part] = xs_ref[pl.ds(64 * x + s, 8, stride=8), :]
            ro_ref[x, :, part] = rs_ref[pl.ds(64 * x + s, 8, stride=8), :]


def local(right_side, diagonal, aggregate_id, coarse_diag, coarse_link):
    count_x, count_y = lax.axis_size("px"), lax.axis_size("py")
    me = jnp.stack([lax.axis_index("px"), lax.axis_index("py"), count_x - 1, count_y - 1]).astype(jnp.int32)

    def both_ways(low, high, axis, far=1):
        count = lax.axis_size(axis)
        up = [(i, (i + far) % count) for i in range(count)]
        down = [(b, a) for a, b in up]
        return lax.ppermute(high, axis, up), lax.ppermute(low, axis, down)

    def around(value, axis, reach):
        sides = [both_ways(value, value, axis, far) for far in range(1, reach + 1)]
        return [low for low, _ in sides[::-1]] + [value] + [high for _, high in sides]

    def gather(value, axis):
        return lax.all_to_all(value, axis, 0, 0)

    two, field = (2, 8, 8, 128), (4, 8, 8, 128)
    given = (right_side, diagonal, aggregate_id, coarse_diag, coarse_link)
    low, high, coarse = call(
        enter_body, [(448, 128)] * 2 + [(16, 128)], *given, scalars=0, far=5,
        scratch=[pltpu.VMEM(a.shape, a.dtype) for a in given] + [pltpu.SemaphoreType.DMA((5,))],
    )
    low, high = low.reshape(7, 8, 8, 128), high.reshape(7, 8, 8, 128)
    xlow, xhigh = both_ways(low, high, "px")
    first, last = call(pack_first_body, [(38, 8, 128)] * 2, low, high, xlow, xhigh, scalars=0)
    ylow, yhigh = both_ways(first, last, "py")
    inverse, scale, offset = call(
        setup_body, [(8, 12, 8, 128), (6, 10, 8, 128), (10, 14, 8, 128)], me, low, high, xlow, xhigh, ylow, yhigh
    )
    mid, dots = (6, 10, 8, 128), (1, 128)
    smooth, remain, send = call(
        restrict_body, [mid, mid, (24, 128)],
        low, high, xlow, xhigh, ylow, yhigh, inverse, offset, coarse, scalars=0,
    )
    send, = call(window_first_body, [(112, 128)], *around(send, "px", 2), scalars=0)
    pieces = around(send, "py", 2)
    coef, = call(coarse_setup_body, [(7, 8, 16, 128)], me, *pieces)
    fixed = (inverse, scale, offset)
    z, wlow, whigh = call(begin_body, [field, two, two], *pieces, coef, smooth, remain, *fixed, scalars=0)

    packed = [(18, 8, 128)] * 2 + [(32, 128)] * 2

    def beside_y(low, high, below, above, first, last, early, late):
        left, right = both_ways(first, last, "py")
        left2, right2 = both_ways(early, late, "py", 2)
        return left2, early, late, right2, low, high, below, above, left, right

    def exchanged(low, high):
        share, down, up = call(
            contribute_body, [(16, 128), (18, 8, 128), (18, 8, 128)], low, high, inverse, offset, scalars=0
        )
        below, above = both_ways(down, up, "px")
        below2, above2 = both_ways(share, share, "px", 2)
        below3, above3 = both_ways(share, share, "px", 3)
        outs = call(
            pack_body, packed, low, high, below3, below2, below, share, above, above2, above3, scalars=0
        )
        return beside_y(low, high, below, above, *outs)

    def exchanged_and_summed(low, high, sums):
        send, = call(
            contribute_and_sum_body, [(count_x, 24, 128)], low, high, inverse, offset, sums, scalars=0
        )
        below, above = (a.reshape(16, 8, 128) for a in both_ways(low, high, "px"))
        outs = call(
            pack_and_sum_body, [(19, 8, 128)] * 2 + [(40, 128)] * 2, me, low, high, below, above, gather(send, "px")
        )
        return beside_y(low, high, below, above, *outs)

    def summed(sums):
        send, = call(spread_dots_body, [(count_x, 8, 128)], sums, scalars=0)
        send, = call(sum_dots_body, [(count_y, 8, 128)], gather(send, "px"), scalars=0)
        return gather(send, "py")

    fixed = (coef, *fixed)
    first = exchanged(wlow, whigh)
    m, nlow, nhigh, sums = call(
        second_body, [field, two, two, dots], *first, *fixed, low, high, z, scalars=0
    )
    second = exchanged_and_summed(nlow, nhigh, sums)
    k, llow, lhigh, part = call(third_body, [field, two, two, (8, 128)], *second, *fixed, scalars=0)
    parts = (part, *both_ways(part, part, "py", 4), both_ways(part, part, "py", 8)[0])
    third = exchanged(llow, lhigh)
    z, wlow, whigh, m, n, x, r, p, s, q, t, keep, sums = call(
        fourth_body, [field, two, two] + [field] * 8 + [dots] * 2,
        *first, *second, *third, *fixed, *parts, low, high, z, m, k, scalars=0,
    )
    return tuple(call(
        finish_body, [right_side.shape] * 2,
        summed(sums), z, wlow, whigh, m, n, x, r, p, s, q, t, keep,
        scalars=0, scratch=[pltpu.VMEM((256, 128), F32)] * 2,
    ))


def solution(mesh):
    cells = P("px", "py", None)
    in_specs = (cells, cells, cells, cells, P(None, "px", "py", None))
    return jax.shard_map(local, mesh=mesh, in_specs=in_specs, out_specs=(cells, cells), check_vma=False)
```

```python
import jax
import jax.numpy as jnp
from jax import lax
from jax.experimental import pallas as pl
from jax.experimental.pallas import tpu as pltpu
from jax.sharding import PartitionSpec as P

OMEGA = 2.0 / 3.0
REST = 1.0 - OMEGA
FACES = (32.0, 16.0, 8.0)
F32 = jnp.float32


def call(body, outs, *args, scalars=1, scratch=(), flops=2_000_000):
    smem = pl.BlockSpec(memory_space=pltpu.SMEM)
    vmem = pl.BlockSpec(memory_space=pltpu.VMEM)
    specs = [smem] * scalars + [vmem] * (len(args) - scalars)
    return pl.pallas_call(
        body,
        out_shape=[jax.ShapeDtypeStruct(shape, F32) for shape in outs],
        in_specs=specs,
        out_specs=[vmem] * len(outs),
        scratch_shapes=list(scratch),
        compiler_params=pltpu.CompilerParams(vmem_limit_bytes=20 * 1024 * 1024),
        cost_estimate=pl.CostEstimate(flops=flops, bytes_accessed=1_000_000, transcendentals=0),
    )(*args)


def along_z(value):
    lane = lax.broadcasted_iota(jnp.int32, value.shape, value.ndim - 1)
    sub = lax.broadcasted_iota(jnp.int32, value.shape, value.ndim - 2)
    after = pltpu.roll(value, 127, value.ndim - 1)
    before = pltpu.roll(value, 1, value.ndim - 1)
    after_row = jnp.where(sub == 7, 0.0, pltpu.roll(after, 7, value.ndim - 2))
    before_row = jnp.where(sub == 0, 0.0, pltpu.roll(before, 1, value.ndim - 2))
    return jnp.where(lane == 127, after_row, after) + jnp.where(lane == 0, before_row, before)


def by_eight(value, ahead):
    lane = lax.broadcasted_iota(jnp.int32, value.shape, value.ndim - 1)
    if ahead:
        moved = pltpu.roll(value, 120, value.ndim - 1)
        return jnp.where(lane >= 120, pltpu.roll(moved, 7, value.ndim - 2), moved)
    moved = pltpu.roll(value, 8, value.ndim - 1)
    return jnp.where(lane < 8, pltpu.roll(moved, 1, value.ndim - 2), moved)


def beside(below, here, above):
    count = here.shape[0]
    inner = here[1 : count - 1]
    return below + above + here[0 : count - 2] + here[2:count] + along_z(inner)


def enter_body(b_ref, d_ref, low_ref, high_ref):
    for x in range(4):
        for s in range(8):
            part = slice(s * 128, (s + 1) * 128)
            ref = low_ref if x < 2 else high_ref
            at = (x % 2) * 64 + s
            ref[pl.ds(at, 8, stride=8), :] = b_ref[x, :, part]
            ref[pl.ds(128 + at, 8, stride=8), :] = d_ref[x, :, part]


def enter_more_body(a_ref, cdiag_ref, link_ref, after_ref, olow_ref, ohigh_ref, coarse_ref):
    lane = lax.broadcasted_iota(jnp.int32, (8, 128), 1)
    for x in range(4):
        for s in range(8):
            home = (lane + s * 128) // 8
            o = ((a_ref[x, :, s * 128 : (s + 1) * 128] & 127) - home).astype(F32)
            if x < 3:
                olow_ref[pl.ds(x * 64 + s, 8, stride=8), :] = o
            if x > 0:
                ohigh_ref[pl.ds((x - 1) * 64 + s, 8, stride=8), :] = o
    rows = []
    for ref in (cdiag_ref, link_ref.at[0], link_ref.at[1], link_ref.at[2]):
        rows = rows + [ref[c // 2, c % 2 : c % 2 + 1, :] for c in range(4)]
    coarse_ref[...] = jnp.concatenate(rows, axis=0)


def field_rows(low, high, xlow, xhigh, base):
    return [ref.at[base + k] for ref in (xlow, low, high, xhigh) for k in range(2)]


def offset_rows(olow, ohigh, below, above):
    rows = [below[8 * k : 8 * k + 8] for k in range(3)] + [olow[k] for k in range(3)] + [ohigh[2]]
    return rows + [above[8 * k : 8 * k + 8] for k in range(3)]


SIDE = {2: (0, 2), 3: (2, 2), 4: (4, 2), 5: (6, 2), 1: (8, 1), 6: (9, 1)}
WIDE = {3: (0, 3), 4: (3, 3), 5: (6, 3), 6: (9, 3), 2: (12, 2), 7: (14, 2), 1: (16, 1), 8: (17, 1)}


def send_sides(spots, rows, base, first_ref, last_ref):
    for x, (at, count) in spots.items():
        first_ref[base + at : base + at + count] = rows[x][0:count]
        last_ref[base + at : base + at + count] = rows[x][8 - count : 8]


def side(ref, spots, x, base, width, left):
    at, count = spots.get(x, (0, 0))
    zero = jnp.zeros((width - count, 8, 128), F32)
    if count == 0:
        return zero
    value = ref[base + at : base + at + count]
    if count == width:
        return value
    return jnp.concatenate([zero, value] if left else [value, zero], axis=0)


def pack_first_body(low_ref, high_ref, xlow_ref, xhigh_ref, first_ref, last_ref):
    four = (low_ref, high_ref, xlow_ref, xhigh_ref)
    for f in range(2):
        send_sides(SIDE, [ref[...] for ref in field_rows(*four, 2 * f)], 10 * f, first_ref, last_ref)


def setup_body(me_ref, low_ref, high_ref, xlow_ref, xhigh_ref, ylow_ref, yhigh_ref, inverse_ref, scale_ref):
    px, py, last_x, last_y = me_ref[0], me_ref[1], me_ref[2], me_ref[3]
    below = jnp.where(px > 0, 1.0, 0.0).astype(F32)
    above = jnp.where(px < last_x, 1.0, 0.0).astype(F32)
    left = jnp.where(py > 0, 1.0, 0.0).astype(F32)
    right = jnp.where(py < last_y, 1.0, 0.0).astype(F32)
    four = (low_ref, high_ref, xlow_ref, xhigh_ref)
    for x, ref in enumerate(field_rows(*four, 2)):
        s_mid = 6.0 + ref[...]
        s_left = 6.0 + side(ylow_ref, SIDE, x, 10, 2, True)
        s_right = 6.0 + side(yhigh_ref, SIDE, x, 10, 2, False)
        i_mid, i_left, i_right = 1.0 / s_mid, left / s_left, right / s_right
        if x < 2 or x > 5:
            seen = below if x < 2 else above
            i_mid, i_left, i_right = i_mid * seen, i_left * seen, i_right * seen
        inverse_ref[x, 0:2] = i_left
        inverse_ref[x, 2:10] = i_mid
        inverse_ref[x, 10:12] = i_right
        if 1 <= x <= 6:
            scale_ref[x - 1, 0:1] = s_left[1:2]
            scale_ref[x - 1, 1:9] = s_mid
            scale_ref[x - 1, 9:10] = s_right[0:1]


def padded(value, width):
    zero = jnp.zeros((width, 8, 128), F32)
    return jnp.concatenate([zero, value, zero], axis=0)


def contribute_body(low_ref, high_ref, inverse_ref, offset_ref, share_ref, down_ref, up_ref):
    share = shares(low_ref, high_ref, inverse_ref, offset_ref)
    share_ref[...] = share
    for ref, cells in ((down_ref, low_ref), (up_ref, high_ref)):
        for k in range(2):
            ref[8 * k : 8 * k + 8] = cells[k]
            ref[16 + k] = share[8 * k : 8 * k + 8]


def contribute_and_sum_body(low_ref, high_ref, inverse_ref, offset_ref, dots_ref, send_ref):
    share = shares(low_ref, high_ref, inverse_ref, offset_ref)
    more = jnp.concatenate([dots_ref[...], jnp.zeros((7, 128), F32)], axis=0)
    for j in range(send_ref.shape[0]):
        send_ref[j, 0:16] = share
        send_ref[j, 16:24] = more


def shares(low_ref, high_ref, inverse_ref, offset_ref):
    vector = [half(low_ref, high_ref, x) for x in range(4)]
    smooth = [OMEGA * vector[x] * inverse_ref[x + 2, 2:10] for x in range(4)]
    remains = [padded(smooth[0], 1)]
    for x in range(4):
        around = padded(smooth[x], 1)
        center = REST * vector[x] + (around[0:8] + around[2:10] + along_z(smooth[x]))
        for other in (x - 1, x + 1):
            if 0 <= other < 4:
                center = center + smooth[other]
        remains.append(jnp.concatenate([smooth[x][0:1], center, smooth[x][7:8]], axis=0))
    remains.append(padded(smooth[3], 1))
    shrunk = [remains[x] * inverse_ref[x + 1, 1:11] for x in range(6)]
    cells = []
    for x in range(8):
        near = None
        for other in (x - 2, x):
            if 0 <= other < 6:
                near = shrunk[other] if near is None else near + shrunk[other]
        if 1 <= x <= 6:
            near = padded(near + along_z(shrunk[x - 1]), 1)
            wide = padded(shrunk[x - 1], 2)
            value = REST * padded(remains[x - 1], 1) + OMEGA * (near + (wide[0:12] + wide[2:14]))
        else:
            value = padded(OMEGA * near, 1)
        value = jnp.where(inverse_ref[x] > 0.0, value, 0.0)
        offset = offset_ref[x + 1, 1:13]
        cells.append((
            jnp.where(jnp.abs(offset) < 0.5, value, 0.0),
            jnp.where(offset > 0.5, value, 0.0),
            jnp.where(offset < -0.5, value, 0.0),
        ))
    sums = []
    for start, stop in ((0, 2), (2, 6), (6, 10), (10, 12)):
        for i in range(4):
            here, up, down = (
                jnp.sum(cells[2 * i][k][start:stop], axis=0) + jnp.sum(cells[2 * i + 1][k][start:stop], axis=0)
                for k in range(3)
            )
            sums.append(here + by_eight(up, False) + by_eight(down, True))
    return jnp.concatenate(grouped_rows(sums), axis=0)


def grouped_rows(sums):
    stacked = jnp.concatenate(sums, axis=0)
    row = lax.broadcasted_iota(jnp.int32, (128, 128), 0)
    col = lax.broadcasted_iota(jnp.int32, (128, 128), 1)
    group = jnp.where(row // 8 == col % 16, 1.0, 0.0).astype(F32)
    grouped = jnp.dot(stacked, group, preferred_element_type=F32, precision=lax.Precision.HIGHEST)
    sub = lax.broadcasted_iota(jnp.int32, (8, 128), 0)
    lane = lax.broadcasted_iota(jnp.int32, (8, 128), 1)
    return [
        jnp.sum(jnp.where(lane // 16 == sub, grouped[8 * c : 8 * c + 8], 0.0), axis=0, keepdims=True)
        for c in range(len(sums))
    ]


def pack_rows(mids, row, first_ref, last_ref, early_ref, late_ref):
    send_sides(SIDE, [mid() for mid in mids], 0, first_ref, last_ref)
    zero = jnp.zeros((6, 128), F32)
    for j in range(4):
        rows = []
        for d in range(-2, 3):
            rows.append(row(d, 4 * j + 1) + row(d - 1, 4 * j + 3))
            rows.append(row(d, 4 * j + 2) + row(d + 1, 4 * j))
        tile = jnp.concatenate(rows + [zero], axis=0)
        ref = early_ref if j < 2 else late_ref
        ref[16 * (j % 2) : 16 * (j % 2) + 16] = tile
        for k in range(2):
            first_ref[10 + 2 * j + k] = tile[8 * k : 8 * k + 8]
            last_ref[10 + 2 * j + k] = tile[8 * k : 8 * k + 8]


def pack_body(low_ref, high_ref, below3_ref, below2_ref, below_ref, share_ref, above_ref, above2_ref, above3_ref, *outs):
    flat = {-3: below3_ref, -2: below2_ref, 0: share_ref, 2: above2_ref, 3: above3_ref}
    joined = {-1: below_ref, 1: above_ref}

    def row(d, at):
        if d in flat:
            return flat[d][at : at + 1, :]
        return joined[d][16 + at // 8, at % 8 : at % 8 + 1, :]

    pack_rows(row_blocks(low_ref, high_ref, below_ref, above_ref), row, *outs)


def pack_and_sum_body(me_ref, low_ref, high_ref, below_ref, above_ref, got_ref, *outs):
    count = got_ref.shape[0]
    spots = {d: lax.rem(me_ref[0] + (d + count), count) for d in range(-3, 4)}

    def row(d, at):
        return got_ref[spots[d], at : at + 1, :]

    pack_rows(row_blocks(low_ref, high_ref, below_ref, above_ref), row, *outs)
    total, rest = total_of(got_ref, 16, None)
    tile = jnp.concatenate([total, rest, jnp.zeros((6, 128), F32)], axis=0)
    for ref in outs[:2]:
        ref[18] = tile
    for ref in outs[2:]:
        ref[32:40] = tile


def row_blocks(low_ref, high_ref, below_ref, above_ref):
    def sent(ref, k):
        return lambda: ref[8 * k : 8 * k + 8]

    def own(ref, k):
        return lambda: ref[k]

    blocks = [sent(below_ref, k) for k in range(2)] + [own(low_ref, k) for k in range(2)]
    return blocks + [own(high_ref, k) for k in range(2)] + [sent(above_ref, k) for k in range(2)]


def smoothed_rows(vector, inverse_ref):
    smooth = [OMEGA * vector(x) * inverse_ref[x] for x in range(8)]
    remains = [
        REST * vector(x)[1:11] + beside(smooth[x - 1][1:11], smooth[x], smooth[x + 1][1:11]) for x in range(1, 7)
    ]
    return [smooth[x][1:11] for x in range(1, 7)], remains


def widened(low, high, below, above, left, right):
    mids = row_blocks(low, high, below, above)

    def vector(x):
        return jnp.concatenate([side(left, SIDE, x, 0, 2, True), mids[x](), side(right, SIDE, x, 0, 2, False)], axis=0)

    return [vector(x) for x in range(8)]


def restrict_body(low, high, xlow, xhigh, ylow, yhigh, inverse_ref, olow, ohigh, coarse_ref,
                  smooth_ref, remain_ref, send_ref, down_ref, up_ref):
    mids = [ref.at[k] for ref in (xlow, low, high, xhigh) for k in range(2)]

    def vector(x):
        return jnp.concatenate(
            [side(ylow, SIDE, x, 0, 2, True), mids[x][...], side(yhigh, SIDE, x, 0, 2, False)], axis=0
        )

    smooth, full = smoothed_rows(vector, inverse_ref)
    shrunk, remains = [], []
    for x in range(6):
        smooth_ref[x] = smooth[x]
        remain_ref[x] = full[x]
        remains.append(full[x][1:9])
        shrunk.append(full[x] * inverse_ref[x + 1, 1:11])
    sums = []
    for big_x in range(2):
        parts = []
        for x in (2 * big_x, 2 * big_x + 1):
            near = beside(shrunk[x][1:9], shrunk[x + 1], shrunk[x + 2][1:9])
            reduced = REST * remains[x + 1] + OMEGA * near
            offset = olow[x] if x < 3 else ohigh[2]
            parts.append((
                jnp.where(jnp.abs(offset) < 0.5, reduced, 0.0),
                jnp.where(offset > 0.5, reduced, 0.0),
                jnp.where(offset < -0.5, reduced, 0.0),
            ))
        for big_y in range(2):
            cols = slice(4 * big_y, 4 * big_y + 4)
            here, up, down = (
                jnp.sum(parts[0][k][cols], axis=0) + jnp.sum(parts[1][k][cols], axis=0) for k in range(3)
            )
            sums.append(here + by_eight(up, False) + by_eight(down, True))
    send_ref[0:8] = jnp.concatenate(grouped_rows(sums) + [jnp.zeros((4, 128), F32)], axis=0)
    send_ref[8:24] = coarse_ref[...]
    for ref, cells in ((down_ref, olow), (up_ref, ohigh)):
        for k in range(3):
            ref[8 * k : 8 * k + 8] = cells[k]
            ref[24 + k] = send_ref[8 * k : 8 * k + 8]


def window_rows(row, start):
    return [[row(d, start + 2 * big_x + big_y) for d in range(-2, 3) for big_x in range(2)] for big_y in range(2)]


def window_first_body(below2_ref, below_ref, own_ref, above_ref, above2_ref, olow, ohigh, first_ref, last_ref, send_ref):
    flat, joined = {-2: below2_ref, 0: own_ref, 2: above2_ref}, {-1: below_ref, 1: above_ref}

    def row(d, at):
        if d in flat:
            return flat[d][at : at + 1, :]
        return joined[d][24 + at // 8, at % 8 : at % 8 + 1, :]

    zero = jnp.zeros((6, 128), F32)
    early, late = window_rows(row, 0)
    rows = early + [zero] + late + [zero]
    for f in range(4):
        early, late = window_rows(row, 8 + 4 * f)
        rows = rows + early + late
    send_ref[...] = jnp.concatenate(rows, axis=0)
    send_sides(WIDE, offset_rows(olow, ohigh, below_ref, above_ref), 0, first_ref, last_ref)
    for k in range(14):
        first_ref[18 + k] = send_ref[8 * k : 8 * k + 8]
        last_ref[18 + k] = send_ref[8 * k : 8 * k + 8]


SPOTS = ((-2, 1), (-1, 0), (-1, 1), (0, 0), (0, 1), (1, 0), (1, 1), (2, 0))


def shift_x(value, ahead):
    return pltpu.roll(value, 15 if ahead else 1, 0)


def shift_k(value, ahead):
    return pltpu.roll(value, 127 if ahead else 1, 1)


def coarse_setup_body(me_ref, left2_ref, left_ref, own_ref, right_ref, right2_ref, olow, ohigh, below_ref, above_ref,
                      coef_ref, sums_ref, offset_ref):
    pieces = [left2_ref[...], left_ref[18:32].reshape(112, 128), own_ref[...],
              right_ref[18:32].reshape(112, 128), right2_ref[...]]
    for x, cells in enumerate(offset_rows(olow, ohigh, below_ref, above_ref)):
        offset_ref[x, 0:3] = side(left_ref, WIDE, x, 0, 3, True)
        offset_ref[x, 3:11] = cells
        offset_ref[x, 11:14] = side(right_ref, WIDE, x, 0, 3, False)
    for y, (d, big_y) in enumerate(SPOTS):
        sums_ref[y] = pieces[d + 2][16 * big_y : 16 * big_y + 16]
    px, py, last_x, last_y = me_ref[0], me_ref[1], me_ref[2], me_ref[3]
    row = lax.broadcasted_iota(jnp.int32, (16, 128), 0)
    lane = lax.broadcasted_iota(jnp.int32, (16, 128), 1)
    pad = jnp.zeros((6, 128), F32)
    where_x = 2 * px - 4 + row
    inside_x = (where_x >= 0) & (where_x < 2 * (last_x + 1)) & (row < 10)

    def take(y, f):
        d, big_y = SPOTS[y]
        start = 32 + 20 * f + 10 * big_y
        return jnp.concatenate([pieces[d + 2][start : start + 10], pad], axis=0)

    links = [[FACES[f - 1] * take(y, f) for y in range(8)] for f in range(1, 4)]
    for y in range(8):
        where_y = 2 * py - 3 + y
        seen = jnp.where((where_y >= 0) & (where_y < 2 * (last_y + 1)), 1.0, 0.0).astype(F32)
        diag = jnp.where(inside_x, take(y, 0), 1.0)
        inverse = jnp.where(inside_x, seen / diag, 0.0)
        coef_ref[0, y] = inverse
        if 1 <= y <= 6:
            coef_ref[1, y] = links[0][y] * inverse
            coef_ref[2, y] = shift_x(links[0][y], False) * inverse
            coef_ref[3, y] = links[1][y] * inverse
            coef_ref[4, y] = links[1][y - 1] * inverse
            coef_ref[5, y] = jnp.where(lane < 127, links[2][y] * inverse, 0.0)
            coef_ref[6, y] = jnp.where(lane > 0, shift_k(links[2][y], False) * inverse, 0.0)
        else:
            for f in range(1, 7):
                coef_ref[f, y] = jnp.zeros((16, 128), F32)


def dots_of(pairs):
    lane = lax.broadcasted_iota(jnp.int32, (1, 128), 1)
    out = jnp.zeros((1, 128), F32)
    for k, value in enumerate(pairs):
        out = jnp.where(lane == k, jnp.sum(value), out)
    return out


def shared_sums(left2_ref, left_ref, early_ref, late_ref, right_ref, right2_ref):
    def share(d, j):
        if d in (-1, 1):
            ref = left_ref if d < 0 else right_ref
            return ref[10 + 2 * j : 12 + 2 * j].reshape(16, 128)
        ref = {-2: left2_ref, 0: early_ref if j < 2 else late_ref, 2: right2_ref}[d]
        return ref[16 * (j % 2) : 16 * (j % 2) + 16, :]

    return [share(d, big_y + 1) + (share(d - 1, 3) if big_y == 0 else share(d + 1, 0)) for d, big_y in SPOTS]


def correct_rows(sums, coef_ref, smooth, remain, inverse_ref, scale_ref, offset_ref):
    start = [sums[y] * coef_ref[0, y] for y in range(8)]

    def sweep(now, y):
        here = now[y]
        total = start[y] + coef_ref[1, y] * shift_x(here, True) + coef_ref[2, y] * shift_x(here, False)
        total = total + coef_ref[3, y] * now[y + 1] + coef_ref[4, y] * now[y - 1]
        return total + coef_ref[5, y] * shift_k(here, True) + coef_ref[6, y] * shift_k(here, False)

    second = [None] + [sweep(start, y) for y in range(1, 7)] + [None]
    third = [None, None] + [sweep(second, y) for y in range(2, 6)]
    sub = lax.broadcasted_iota(jnp.int32, (8, 128), 0)
    lane = lax.broadcasted_iota(jnp.int32, (8, 128), 1)
    index = sub * 16 + lane // 8

    def spread_out(tile, x):
        wide = jnp.broadcast_to(tile[x + 4 : x + 5, :], (8, 128))
        return jnp.take_along_axis(wide, index, axis=1)

    tables = [[], [], []]
    for y in range(2, 6):
        for k, tile in enumerate((third[y], shift_k(third[y], True), shift_k(third[y], False))):
            tables[k].append([spread_out(tile, x) for x in range(-2, 4)])
    counts = (3, 4, 4, 3)

    def lifted(x):
        big_x = x // 2
        here, up, down = (
            jnp.concatenate(
                [jnp.broadcast_to(tables[k][y][big_x + 2][None], (counts[y], 8, 128)) for y in range(4)], axis=0
            )
            for k in range(3)
        )
        offset = offset_ref[x + 3]
        return jnp.where(offset > 0.5, up, jnp.where(offset < -0.5, down, here))

    lifts = [lifted(x) for x in range(-3, 7)]
    spreads = []
    for x in range(8):
        near = beside(lifts[x][1:13], lifts[x + 1], lifts[x + 2][1:13])
        spreads.append(REST * lifts[x + 1][1:13] + OMEGA * (inverse_ref[x] * near))
    shaped = []
    for x in range(6):
        near = beside(spreads[x][1:11], spreads[x + 1], spreads[x + 2][1:11])
        spread = spreads[x + 1][1:11]
        left = remain[x] - (scale_ref[x] * spread - near)
        shaped.append(smooth[x] + spread + OMEGA * (inverse_ref[x + 1, 1:11] * left))
    for x in range(4):
        near = beside(shaped[x][1:9], shaped[x + 1], shaped[x + 2][1:9])
        own = shaped[x + 1][1:9]
        yield x, own, scale_ref[x + 1, 1:9] * own - near


def put(low_ref, high_ref, x, value):
    (low_ref if x < 2 else high_ref)[x % 2] = value


def half(low_ref, high_ref, x):
    return (low_ref if x < 2 else high_ref)[x % 2]


def products(left, right):
    return [jnp.sum(a * b, axis=0) for a in left for b in right]


def begin_body(*refs):
    sums, fixed, (z_ref, wlow_ref, whigh_ref) = refs[0], refs[1:7], refs[7:]
    for x, z, w in correct_rows([sums[y] for y in range(8)], *fixed):
        z_ref[x] = z
        put(wlow_ref, whigh_ref, x, w)


EXCHANGED = 10


def received(refs):
    left2, early, late, right2, low, high, below, above, left, right = refs
    return widened(low, high, below, above, left, right), shared_sums(left2, left, early, late, right, right2)


def corrected(vectors, sums, refs):
    coef, fixed = refs[0], refs[1:4]
    smooth, remain = smoothed_rows(lambda x: vectors[x], fixed[0])
    return correct_rows(sums, coef, smooth, remain, *fixed)


def second_body(*refs):
    low_ref, high_ref, z_ref, m_ref, nlow_ref, nhigh_ref, dots_ref = refs[14:]
    wlow_ref, whigh_ref = refs[4:6]
    sums = [jnp.zeros((8, 128), F32)] * 6
    for x, m, n in corrected(*received(refs[:10]), refs[10:14]):
        m_ref[x] = m
        put(nlow_ref, nhigh_ref, x, n)
        here = products((half(low_ref, high_ref, x), half(wlow_ref, whigh_ref, x), n), (z_ref[x], m))
        sums = [a + b for a, b in zip(sums, here)]
    dots_ref[...] = dots_of(sums)


def two_sum(a, b):
    total = a + b
    part = total - a
    return total, (a - (total - part)) + (b - part)


def split(a):
    wide = a * 4097.0
    high = wide - (wide - a)
    return high, a - high


def two_product(a, b):
    product = a * b
    a_high, a_low = split(a)
    b_high, b_low = split(b)
    return product, a_low * b_low - (((product - a_high * b_high) - a_low * b_high) - a_high * b_low)


def pair_add(a, b):
    total, rest = two_sum(a[0], b[0])
    return two_sum(total, rest + (a[1] + b[1]))


def pair_scale(a, factor):
    product, rest = two_product(a[0], factor)
    return two_sum(product, rest + a[1] * factor)


def pair_times(a, b):
    product, rest = two_product(a[0], b[0])
    return two_sum(product, rest + (a[0] * b[1] + a[1] * b[0]))


def total_of(got_ref, row, rest_row):
    total = got_ref[0, row : row + 1, :]
    rest = jnp.zeros((1, 128), F32) if rest_row is None else got_ref[0, rest_row : rest_row + 1, :]
    for j in range(1, got_ref.shape[0]):
        total, lost = two_sum(total, got_ref[j, row : row + 1, :])
        rest = rest + lost
        if rest_row is not None:
            rest = rest + got_ref[j, rest_row : rest_row + 1, :]
    return total, rest


def gathered(tiles):
    total, rest = tiles[0][0:1], tiles[0][1:2]
    for tile in tiles[1:]:
        total, lost = two_sum(total, tile[0:1])
        rest = rest + (lost + tile[1:2])
    return two_sum(total, rest)


def pairs_of(total, rest, count):
    return [
        (jnp.broadcast_to(total[:, k : k + 1], (1, 128)), jnp.broadcast_to(rest[:, k : k + 1], (1, 128)))
        for k in range(count)
    ]


def form(table, left, weights):
    out = None
    for i, row in enumerate(left):
        for j, entry in enumerate(table[row]):
            factor = None
            for w in (weights[i], weights[j]):
                if w is not None:
                    factor = w if factor is None else pair_times(factor, w)
            term = entry if factor is None else pair_times(entry, factor)
            out = term if out is None else pair_add(out, term)
    return out[0] + out[1]


def tiled(row):
    return jnp.broadcast_to(row, (8, 128))[None]


def negated(pair):
    return -pair[0], -pair[1]


def third_body(*refs):
    k_ref, llow_ref, lhigh_ref, part_ref = refs[14:]
    early, right2, left, right = refs[1], refs[3], refs[8], refs[9]
    total, rest = gathered([early[32:40, :], left[18], right[18], right2[32:40, :]])
    part_ref[...] = jnp.concatenate([total, rest, jnp.zeros((6, 128), F32)], axis=0)
    for x, k, l in corrected(*received(refs[:10]), refs[10:14]):
        k_ref[x] = k
        put(llow_ref, lhigh_ref, x, l)


def fourth_body(*refs):
    rows, window = zip(*(received(refs[10 * i : 10 * i + 10]) for i in range(3)))
    rest = refs[30:34]
    parts, refs = refs[34:38], refs[38:]
    low_ref, high_ref, z_ref, m_ref, k_ref = refs[:5]
    zo_ref, wolow_ref, wohigh_ref, mo_ref, no_ref, xo_ref, ro_ref, po_ref, so_ref, qo_ref, to_ref = refs[5:16]
    keep_ref, dots_ref = refs[16:]
    sums = pairs_of(*gathered([part[...] for part in parts]), 6)
    table = [sums[0:2], sums[2:4], sums[4:6]]
    gamma0 = table[0][0][0]
    alpha0 = gamma0 / table[1][0][0]
    weights = (None, negated((alpha0, jnp.zeros_like(alpha0))))
    gamma1 = form(table, (0, 1), weights)
    delta1 = form(table, (1, 2), weights)
    beta1 = gamma1 / gamma0
    alpha1 = gamma1 / (delta1 - beta1 * gamma1 / alpha0)
    lane = lax.broadcasted_iota(jnp.int32, (1, 128), 1)
    keep_ref[...] = jnp.where(lane == 0, gamma1, jnp.where(lane == 1, alpha1, 0.0))
    alphas = [(tiled(alpha0), tiled(alpha1), tiled(beta1)), (alpha0, alpha1, beta1)]

    def turned(w, n, l, alpha0, alpha1, beta1):
        t = (n - alpha0 * l) + beta1 * n
        return (w - alpha0 * n) - alpha1 * t, t

    vectors = [turned(*(rows[i][x] for i in range(3)), *alphas[0])[0] for x in range(8)]
    window = [turned(*(window[i][y] for i in range(3)), *alphas[1])[0] for y in range(8)]
    alpha0, alpha1, beta1 = alphas[0]
    sums = [jnp.zeros((8, 128), F32)] * 15
    for x, m2, n2 in corrected(vectors, window, rest):
        w0, n0, l = (rows[i][x + 2][2:10] for i in range(3))
        z0, m0, k = z_ref[x], m_ref[x], k_ref[x]
        w2, t = turned(w0, n0, l, *alphas[0])
        z2, q = turned(z0, m0, k, *alphas[0])
        p, s = (z0 - alpha0 * m0) + beta1 * z0, (w0 - alpha0 * n0) + beta1 * w0
        r2 = (half(low_ref, high_ref, x) - alpha0 * w0) - alpha1 * s
        xo_ref[x] = alpha0 * z0 + alpha1 * p
        ro_ref[x], zo_ref[x] = r2, z2
        put(wolow_ref, wohigh_ref, x, w2)
        mo_ref[x], no_ref[x] = m2, n2
        po_ref[x], so_ref[x], qo_ref[x], to_ref[x] = p, s, q, t
        sums = [a + b for a, b in zip(sums, products((r2, w2, s, n2, t), (z2, m2, q)))]
    dots_ref[...] = dots_of(sums)


def spread_dots_body(dots_ref, send_ref):
    tile = jnp.concatenate([dots_ref[...], jnp.zeros((7, 128), F32)], axis=0)
    for j in range(send_ref.shape[0]):
        send_ref[j] = tile


def sum_dots_body(got_ref, send_ref):
    total, rest = total_of(got_ref, 0, None)
    tile = jnp.concatenate([total, rest, jnp.zeros((6, 128), F32)], axis=0)
    for j in range(send_ref.shape[0]):
        send_ref[j] = tile


def finish_body(got_ref, z_ref, wlow_ref, whigh_ref, m_ref, n_ref, x_ref, r_ref, p_ref, s_ref, q_ref, t_ref, keep_ref,
                xo_ref, ro_ref, xs_ref, rs_ref):
    sums = pairs_of(*two_sum(*total_of(got_ref, 0, 1)), 15)
    table = [sums[3 * k : 3 * k + 3] for k in range(5)]
    keep = keep_ref[...]
    gamma1 = jnp.broadcast_to(keep[:, 0:1], (1, 128))
    alpha1 = jnp.broadcast_to(keep[:, 1:2], (1, 128))
    gamma2 = table[0][0][0]
    beta2 = gamma2 / gamma1
    alpha2 = gamma2 / (table[1][0][0] - beta2 * gamma2 / alpha1)
    weights = (None, (-alpha2, jnp.zeros_like(alpha2)), two_product(-alpha2, beta2))
    gamma3 = form(table, (0, 1, 2), weights)
    delta3 = form(table, (1, 3, 4), weights)
    beta3 = gamma3 / gamma2
    alpha3 = gamma3 / (delta3 - beta3 * gamma3 / alpha2)
    alpha2, beta2, alpha3, beta3 = tiled(alpha2), tiled(beta2), tiled(alpha3), tiled(beta3)
    for x in range(4):
        z, w, q1, t1 = z_ref[x], half(wlow_ref, whigh_ref, x), q_ref[x], t_ref[x]
        p2, s2 = z + beta2 * p_ref[x], w + beta2 * s_ref[x]
        q2, t2 = m_ref[x] + beta2 * q1, n_ref[x] + beta2 * t1
        p3 = (z - alpha2 * q2) + beta3 * p2
        s3 = (w - alpha2 * t2) + beta3 * s2
        xs_ref[pl.ds(64 * x, 64), :] = ((x_ref[x] + alpha2 * p2) + alpha3 * p3).reshape(64, 128)
        rs_ref[pl.ds(64 * x, 64), :] = ((r_ref[x] - alpha2 * s2) - alpha3 * s3).reshape(64, 128)
    for x in range(4):
        for s in range(8):
            part = slice(s * 128, (s + 1) * 128)
            xo_ref[x, :, part] = xs_ref[pl.ds(64 * x + s, 8, stride=8), :]
            ro_ref[x, :, part] = rs_ref[pl.ds(64 * x + s, 8, stride=8), :]


def local(right_side, diagonal, aggregate_id, coarse_diag, coarse_link):
    count_x, count_y = lax.axis_size("px"), lax.axis_size("py")
    me = jnp.stack([lax.axis_index("px"), lax.axis_index("py"), count_x - 1, count_y - 1]).astype(jnp.int32)

    def both_ways(low, high, axis, far=1):
        count = lax.axis_size(axis)
        up = [(i, (i + far) % count) for i in range(count)]
        down = [(b, a) for a, b in up]
        return lax.ppermute(high, axis, up), lax.ppermute(low, axis, down)

    def gather(value, axis):
        return lax.all_to_all(value, axis, 0, 0)

    two, field = (2, 8, 8, 128), (4, 8, 8, 128)
    low, high = call(enter_body, [(256, 128)] * 2, right_side, diagonal, scalars=0)
    low, high = low.reshape(4, 8, 8, 128), high.reshape(4, 8, 8, 128)
    xlow, xhigh = both_ways(low, high, "px")
    olow, ohigh, coarse = call(
        enter_more_body, [(192, 128)] * 2 + [(16, 128)], aggregate_id, coarse_diag, coarse_link, low, scalars=0
    )
    olow, ohigh = olow.reshape(3, 8, 8, 128), ohigh.reshape(3, 8, 8, 128)
    first, last = call(pack_first_body, [(20, 8, 128)] * 2, low, high, xlow, xhigh, scalars=0)
    ylow, yhigh = both_ways(first, last, "py")
    inverse, scale = call(
        setup_body, [(8, 12, 8, 128), (6, 10, 8, 128)], me, low, high, xlow, xhigh, ylow, yhigh
    )
    mid, dots = (6, 10, 8, 128), (1, 128)
    smooth, remain, send, down, up = call(
        restrict_body, [mid, mid, (24, 128)] + [(27, 8, 128)] * 2,
        low, high, xlow, xhigh, ylow, yhigh, inverse, olow, ohigh, coarse, scalars=0,
    )
    below, above = both_ways(down, up, "px")
    below2, above2 = both_ways(send, send, "px", 2)
    first, last, send = call(
        window_first_body, [(32, 8, 128)] * 2 + [(112, 128)],
        below2, below, send, above, above2, olow, ohigh, scalars=0,
    )
    left, right = both_ways(first, last, "py")
    left2, right2 = both_ways(send, send, "py", 2)
    coef, sums, offset = call(
        coarse_setup_body, [(7, 8, 16, 128), (8, 16, 128), (10, 14, 8, 128)],
        me, left2, left, send, right, right2, olow, ohigh, below, above,
    )
    fixed = (inverse, scale, offset)
    z, wlow, whigh = call(begin_body, [field, two, two], sums, coef, smooth, remain, *fixed, scalars=0)

    packed = [(18, 8, 128)] * 2 + [(32, 128)] * 2

    def beside_y(low, high, below, above, first, last, early, late):
        left, right = both_ways(first, last, "py")
        left2, right2 = both_ways(early, late, "py", 2)
        return left2, early, late, right2, low, high, below, above, left, right

    def exchanged(low, high):
        share, down, up = call(
            contribute_body, [(16, 128), (18, 8, 128), (18, 8, 128)], low, high, inverse, offset, scalars=0
        )
        below, above = both_ways(down, up, "px")
        below2, above2 = both_ways(share, share, "px", 2)
        below3, above3 = both_ways(share, share, "px", 3)
        outs = call(
            pack_body, packed, low, high, below3, below2, below, share, above, above2, above3, scalars=0
        )
        return beside_y(low, high, below, above, *outs)

    def exchanged_and_summed(low, high, sums):
        send, = call(
            contribute_and_sum_body, [(count_x, 24, 128)], low, high, inverse, offset, sums, scalars=0
        )
        below, above = (a.reshape(16, 8, 128) for a in both_ways(low, high, "px"))
        outs = call(
            pack_and_sum_body, [(19, 8, 128)] * 2 + [(40, 128)] * 2, me, low, high, below, above, gather(send, "px")
        )
        return beside_y(low, high, below, above, *outs)

    def summed(sums):
        send, = call(spread_dots_body, [(count_x, 8, 128)], sums, scalars=0)
        send, = call(sum_dots_body, [(count_y, 8, 128)], gather(send, "px"), scalars=0)
        return gather(send, "py")

    fixed = (coef, *fixed)
    first = exchanged(wlow, whigh)
    m, nlow, nhigh, sums = call(
        second_body, [field, two, two, dots], *first, *fixed, low, high, z, scalars=0
    )
    second = exchanged_and_summed(nlow, nhigh, sums)
    k, llow, lhigh, part = call(third_body, [field, two, two, (8, 128)], *second, *fixed, scalars=0)
    parts = (part, *both_ways(part, part, "py", 4), both_ways(part, part, "py", 8)[0])
    third = exchanged(llow, lhigh)
    z, wlow, whigh, m, n, x, r, p, s, q, t, keep, sums = call(
        fourth_body, [field, two, two] + [field] * 8 + [dots] * 2,
        *first, *second, *third, *fixed, *parts, low, high, z, m, k, scalars=0,
    )
    return tuple(call(
        finish_body, [right_side.shape] * 2,
        summed(sums), z, wlow, whigh, m, n, x, r, p, s, q, t, keep,
        scalars=0, scratch=[pltpu.VMEM((256, 128), F32)] * 2,
    ))


def solution(mesh):
    cells = P("px", "py", None)
    in_specs = (cells, cells, cells, cells, P(None, "px", "py", None))
    return jax.shard_map(local, mesh=mesh, in_specs=in_specs, out_specs=(cells, cells), check_vma=False)
```

```python
import jax
import jax.numpy as jnp
from jax import lax
from jax.experimental import pallas as pl
from jax.experimental.pallas import tpu as pltpu
from jax.sharding import PartitionSpec as P


OMEGA = 2.0 / 3.0
REST = 1.0 - OMEGA
FACES = (32.0, 16.0, 8.0)
F32 = jnp.float32


def call(body, outs, *args, scalars=1, scratch=(), flops=2_000_000):
    smem = pl.BlockSpec(memory_space=pltpu.SMEM)
    vmem = pl.BlockSpec(memory_space=pltpu.VMEM)
    specs = [smem] * scalars + [vmem] * (len(args) - scalars)
    return pl.pallas_call(
        body,
        out_shape=[jax.ShapeDtypeStruct(shape, F32) for shape in outs],
        in_specs=specs,
        out_specs=[vmem] * len(outs),
        scratch_shapes=list(scratch),
        compiler_params=pltpu.CompilerParams(vmem_limit_bytes=20 * 1024 * 1024),
        cost_estimate=pl.CostEstimate(flops=flops, bytes_accessed=1_000_000, transcendentals=0),
    )(*args)


def along_z(value):
    lane = lax.broadcasted_iota(jnp.int32, value.shape, value.ndim - 1)
    sub = lax.broadcasted_iota(jnp.int32, value.shape, value.ndim - 2)
    after = pltpu.roll(value, 127, value.ndim - 1)
    before = pltpu.roll(value, 1, value.ndim - 1)
    after_row = jnp.where(sub == 7, 0.0, pltpu.roll(after, 7, value.ndim - 2))
    before_row = jnp.where(sub == 0, 0.0, pltpu.roll(before, 1, value.ndim - 2))
    return jnp.where(lane == 127, after_row, after) + jnp.where(lane == 0, before_row, before)


def by_eight(value, ahead):
    lane = lax.broadcasted_iota(jnp.int32, value.shape, value.ndim - 1)
    if ahead:
        moved = pltpu.roll(value, 120, value.ndim - 1)
        return jnp.where(lane >= 120, pltpu.roll(moved, 7, value.ndim - 2), moved)
    moved = pltpu.roll(value, 8, value.ndim - 1)
    return jnp.where(lane < 8, pltpu.roll(moved, 1, value.ndim - 2), moved)


def beside(below, here, above):
    count = here.shape[0]
    inner = here[1 : count - 1]
    return below + above + here[0 : count - 2] + here[2:count] + along_z(inner)


def enter_body(b_ref, d_ref, low_ref, high_ref):
    for x in range(4):
        for s in range(8):
            part = slice(s * 128, (s + 1) * 128)
            ref = low_ref if x < 2 else high_ref
            at = (x % 2) * 64 + s
            ref[pl.ds(at, 8, stride=8), :] = b_ref[x, :, part]
            ref[pl.ds(128 + at, 8, stride=8), :] = d_ref[x, :, part]


def enter_more_body(a_ref, cdiag_ref, link_ref, after_ref, olow_ref, ohigh_ref, coarse_ref):
    lane = lax.broadcasted_iota(jnp.int32, (8, 128), 1)
    for x in range(4):
        for s in range(8):
            home = (lane + s * 128) // 8
            o = ((a_ref[x, :, s * 128 : (s + 1) * 128] & 127) - home).astype(F32)
            if x < 3:
                olow_ref[pl.ds(x * 64 + s, 8, stride=8), :] = o
            if x > 0:
                ohigh_ref[pl.ds((x - 1) * 64 + s, 8, stride=8), :] = o
    rows = []
    for ref in (cdiag_ref, link_ref.at[0], link_ref.at[1], link_ref.at[2]):
        rows = rows + [ref[c // 2, c % 2 : c % 2 + 1, :] for c in range(4)]
    coarse_ref[...] = jnp.concatenate(rows, axis=0)


def field_rows(low, high, xlow, xhigh, base):
    return [ref.at[base + k] for ref in (xlow, low, high, xhigh) for k in range(2)]


def offset_rows(olow, ohigh, below, above):
    rows = [below[8 * k : 8 * k + 8] for k in range(3)] + [olow[k] for k in range(3)] + [ohigh[2]]
    return rows + [above[8 * k : 8 * k + 8] for k in range(3)]


SIDE = {2: (0, 2), 3: (2, 2), 4: (4, 2), 5: (6, 2), 1: (8, 1), 6: (9, 1)}
WIDE = {3: (0, 3), 4: (3, 3), 5: (6, 3), 6: (9, 3), 2: (12, 2), 7: (14, 2), 1: (16, 1), 8: (17, 1)}


def send_sides(spots, rows, base, first_ref, last_ref):
    for x, (at, count) in spots.items():
        first_ref[base + at : base + at + count] = rows[x][0:count]
        last_ref[base + at : base + at + count] = rows[x][8 - count : 8]


def side(ref, spots, x, base, width, left):
    at, count = spots.get(x, (0, 0))
    zero = jnp.zeros((width - count, 8, 128), F32)
    if count == 0:
        return zero
    value = ref[base + at : base + at + count]
    if count == width:
        return value
    return jnp.concatenate([zero, value] if left else [value, zero], axis=0)


def pack_first_body(low_ref, high_ref, xlow_ref, xhigh_ref, first_ref, last_ref):
    four = (low_ref, high_ref, xlow_ref, xhigh_ref)
    for f in range(2):
        send_sides(SIDE, [ref[...] for ref in field_rows(*four, 2 * f)], 10 * f, first_ref, last_ref)


def setup_body(me_ref, low_ref, high_ref, xlow_ref, xhigh_ref, ylow_ref, yhigh_ref, inverse_ref, scale_ref):
    px, py, last_x, last_y = me_ref[0], me_ref[1], me_ref[2], me_ref[3]
    below = jnp.where(px > 0, 1.0, 0.0).astype(F32)
    above = jnp.where(px < last_x, 1.0, 0.0).astype(F32)
    left = jnp.where(py > 0, 1.0, 0.0).astype(F32)
    right = jnp.where(py < last_y, 1.0, 0.0).astype(F32)
    four = (low_ref, high_ref, xlow_ref, xhigh_ref)
    for x, ref in enumerate(field_rows(*four, 2)):
        s_mid = 6.0 + ref[...]
        s_left = 6.0 + side(ylow_ref, SIDE, x, 10, 2, True)
        s_right = 6.0 + side(yhigh_ref, SIDE, x, 10, 2, False)
        i_mid, i_left, i_right = 1.0 / s_mid, left / s_left, right / s_right
        if x < 2 or x > 5:
            seen = below if x < 2 else above
            i_mid, i_left, i_right = i_mid * seen, i_left * seen, i_right * seen
        inverse_ref[x, 0:2] = i_left
        inverse_ref[x, 2:10] = i_mid
        inverse_ref[x, 10:12] = i_right
        if 1 <= x <= 6:
            scale_ref[x - 1, 0:1] = s_left[1:2]
            scale_ref[x - 1, 1:9] = s_mid
            scale_ref[x - 1, 9:10] = s_right[0:1]


def padded(value, width):
    zero = jnp.zeros((width, 8, 128), F32)
    return jnp.concatenate([zero, value, zero], axis=0)


def contribute_body(low_ref, high_ref, inverse_ref, offset_ref, share_ref, down_ref, up_ref):
    share = shares(low_ref, high_ref, inverse_ref, offset_ref)
    share_ref[...] = share
    for ref, cells in ((down_ref, low_ref), (up_ref, high_ref)):
        for k in range(2):
            ref[8 * k : 8 * k + 8] = cells[k]
            ref[16 + k] = share[8 * k : 8 * k + 8]


def contribute_and_sum_body(low_ref, high_ref, inverse_ref, offset_ref, dots_ref, send_ref):
    share = shares(low_ref, high_ref, inverse_ref, offset_ref)
    more = jnp.concatenate([dots_ref[...], jnp.zeros((7, 128), F32)], axis=0)
    for j in range(send_ref.shape[0]):
        send_ref[j, 0:16] = share
        send_ref[j, 16:24] = more


def shares(low_ref, high_ref, inverse_ref, offset_ref):
    vector = [half(low_ref, high_ref, x) for x in range(4)]
    smooth = [OMEGA * vector[x] * inverse_ref[x + 2, 2:10] for x in range(4)]
    remains = [padded(smooth[0], 1)]
    for x in range(4):
        around = padded(smooth[x], 1)
        center = REST * vector[x] + (around[0:8] + around[2:10] + along_z(smooth[x]))
        for other in (x - 1, x + 1):
            if 0 <= other < 4:
                center = center + smooth[other]
        remains.append(jnp.concatenate([smooth[x][0:1], center, smooth[x][7:8]], axis=0))
    remains.append(padded(smooth[3], 1))
    shrunk = [remains[x] * inverse_ref[x + 1, 1:11] for x in range(6)]
    cells = []
    for x in range(8):
        near = None
        for other in (x - 2, x):
            if 0 <= other < 6:
                near = shrunk[other] if near is None else near + shrunk[other]
        if 1 <= x <= 6:
            near = padded(near + along_z(shrunk[x - 1]), 1)
            wide = padded(shrunk[x - 1], 2)
            value = REST * padded(remains[x - 1], 1) + OMEGA * (near + (wide[0:12] + wide[2:14]))
        else:
            value = padded(OMEGA * near, 1)
        value = jnp.where(inverse_ref[x] > 0.0, value, 0.0)
        offset = offset_ref[x + 1, 1:13]
        cells.append((
            jnp.where(jnp.abs(offset) < 0.5, value, 0.0),
            jnp.where(offset > 0.5, value, 0.0),
            jnp.where(offset < -0.5, value, 0.0),
        ))
    sums = []
    for start, stop in ((0, 2), (2, 6), (6, 10), (10, 12)):
        for i in range(4):
            here, up, down = (
                jnp.sum(cells[2 * i][k][start:stop], axis=0) + jnp.sum(cells[2 * i + 1][k][start:stop], axis=0)
                for k in range(3)
            )
            sums.append(here + by_eight(up, False) + by_eight(down, True))
    return jnp.concatenate(grouped_rows(sums), axis=0)


def grouped_rows(sums):
    stacked = jnp.concatenate(sums, axis=0)
    row = lax.broadcasted_iota(jnp.int32, (128, 128), 0)
    col = lax.broadcasted_iota(jnp.int32, (128, 128), 1)
    group = jnp.where(row // 8 == col % 16, 1.0, 0.0).astype(F32)
    grouped = jnp.dot(stacked, group, preferred_element_type=F32, precision=lax.Precision.HIGHEST)
    sub = lax.broadcasted_iota(jnp.int32, (8, 128), 0)
    lane = lax.broadcasted_iota(jnp.int32, (8, 128), 1)
    return [
        jnp.sum(jnp.where(lane // 16 == sub, grouped[8 * c : 8 * c + 8], 0.0), axis=0, keepdims=True)
        for c in range(len(sums))
    ]


def pack_rows(mids, row, first_ref, last_ref, early_ref, late_ref):
    send_sides(SIDE, [mid() for mid in mids], 0, first_ref, last_ref)
    zero = jnp.zeros((6, 128), F32)
    for j in range(4):
        rows = []
        for d in range(-2, 3):
            rows.append(row(d, 4 * j + 1) + row(d - 1, 4 * j + 3))
            rows.append(row(d, 4 * j + 2) + row(d + 1, 4 * j))
        tile = jnp.concatenate(rows + [zero], axis=0)
        ref = early_ref if j < 2 else late_ref
        ref[16 * (j % 2) : 16 * (j % 2) + 16] = tile
        for k in range(2):
            first_ref[10 + 2 * j + k] = tile[8 * k : 8 * k + 8]
            last_ref[10 + 2 * j + k] = tile[8 * k : 8 * k + 8]


def pack_body(low_ref, high_ref, below3_ref, below2_ref, below_ref, share_ref, above_ref, above2_ref, above3_ref, *outs):
    flat = {-3: below3_ref, -2: below2_ref, 0: share_ref, 2: above2_ref, 3: above3_ref}
    joined = {-1: below_ref, 1: above_ref}

    def row(d, at):
        if d in flat:
            return flat[d][at : at + 1, :]
        return joined[d][16 + at // 8, at % 8 : at % 8 + 1, :]

    pack_rows(row_blocks(low_ref, high_ref, below_ref, above_ref), row, *outs)


def pack_and_sum_body(me_ref, low_ref, high_ref, below_ref, above_ref, got_ref, *outs):
    count = got_ref.shape[0]
    spots = {d: lax.rem(me_ref[0] + (d + count), count) for d in range(-3, 4)}

    def row(d, at):
        return got_ref[spots[d], at : at + 1, :]

    pack_rows(row_blocks(low_ref, high_ref, below_ref, above_ref), row, *outs)
    total, rest = total_of(got_ref, 16, None)
    tile = jnp.concatenate([total, rest, jnp.zeros((6, 128), F32)], axis=0)
    for ref in outs[:2]:
        ref[18] = tile
    for ref in outs[2:]:
        ref[32:40] = tile


def row_blocks(low_ref, high_ref, below_ref, above_ref):
    def sent(ref, k):
        return lambda: ref[8 * k : 8 * k + 8]

    def own(ref, k):
        return lambda: ref[k]

    blocks = [sent(below_ref, k) for k in range(2)] + [own(low_ref, k) for k in range(2)]
    return blocks + [own(high_ref, k) for k in range(2)] + [sent(above_ref, k) for k in range(2)]


def smoothed_rows(vector, inverse_ref):
    smooth = [OMEGA * vector(x) * inverse_ref[x] for x in range(8)]
    remains = [
        REST * vector(x)[1:11] + beside(smooth[x - 1][1:11], smooth[x], smooth[x + 1][1:11]) for x in range(1, 7)
    ]
    return [smooth[x][1:11] for x in range(1, 7)], remains


def widened(low, high, below, above, left, right):
    mids = row_blocks(low, high, below, above)

    def vector(x):
        return jnp.concatenate([side(left, SIDE, x, 0, 2, True), mids[x](), side(right, SIDE, x, 0, 2, False)], axis=0)

    return [vector(x) for x in range(8)]


def restrict_body(low, high, xlow, xhigh, ylow, yhigh, inverse_ref, olow, ohigh, coarse_ref,
                  smooth_ref, remain_ref, send_ref, down_ref, up_ref):
    mids = [ref.at[k] for ref in (xlow, low, high, xhigh) for k in range(2)]

    def vector(x):
        return jnp.concatenate(
            [side(ylow, SIDE, x, 0, 2, True), mids[x][...], side(yhigh, SIDE, x, 0, 2, False)], axis=0
        )

    smooth, full = smoothed_rows(vector, inverse_ref)
    shrunk, remains = [], []
    for x in range(6):
        smooth_ref[x] = smooth[x]
        remain_ref[x] = full[x]
        remains.append(full[x][1:9])
        shrunk.append(full[x] * inverse_ref[x + 1, 1:11])
    sums = []
    for big_x in range(2):
        parts = []
        for x in (2 * big_x, 2 * big_x + 1):
            near = beside(shrunk[x][1:9], shrunk[x + 1], shrunk[x + 2][1:9])
            reduced = REST * remains[x + 1] + OMEGA * near
            offset = olow[x] if x < 3 else ohigh[2]
            parts.append((
                jnp.where(jnp.abs(offset) < 0.5, reduced, 0.0),
                jnp.where(offset > 0.5, reduced, 0.0),
                jnp.where(offset < -0.5, reduced, 0.0),
            ))
        for big_y in range(2):
            cols = slice(4 * big_y, 4 * big_y + 4)
            here, up, down = (
                jnp.sum(parts[0][k][cols], axis=0) + jnp.sum(parts[1][k][cols], axis=0) for k in range(3)
            )
            sums.append(here + by_eight(up, False) + by_eight(down, True))
    send_ref[0:8] = jnp.concatenate(grouped_rows(sums) + [jnp.zeros((4, 128), F32)], axis=0)
    send_ref[8:24] = coarse_ref[...]
    for ref, cells in ((down_ref, olow), (up_ref, ohigh)):
        for k in range(3):
            ref[8 * k : 8 * k + 8] = cells[k]
            ref[24 + k] = send_ref[8 * k : 8 * k + 8]


def window_rows(row, start):
    return [[row(d, start + 2 * big_x + big_y) for d in range(-2, 3) for big_x in range(2)] for big_y in range(2)]


def window_first_body(below2_ref, below_ref, own_ref, above_ref, above2_ref, olow, ohigh, first_ref, last_ref, send_ref):
    flat, joined = {-2: below2_ref, 0: own_ref, 2: above2_ref}, {-1: below_ref, 1: above_ref}

    def row(d, at):
        if d in flat:
            return flat[d][at : at + 1, :]
        return joined[d][24 + at // 8, at % 8 : at % 8 + 1, :]

    zero = jnp.zeros((6, 128), F32)
    early, late = window_rows(row, 0)
    rows = early + [zero] + late + [zero]
    for f in range(4):
        early, late = window_rows(row, 8 + 4 * f)
        rows = rows + early + late
    send_ref[...] = jnp.concatenate(rows, axis=0)
    send_sides(WIDE, offset_rows(olow, ohigh, below_ref, above_ref), 0, first_ref, last_ref)
    for k in range(14):
        first_ref[18 + k] = send_ref[8 * k : 8 * k + 8]
        last_ref[18 + k] = send_ref[8 * k : 8 * k + 8]


SPOTS = ((-2, 1), (-1, 0), (-1, 1), (0, 0), (0, 1), (1, 0), (1, 1), (2, 0))


def shift_x(value, ahead):
    return pltpu.roll(value, 15 if ahead else 1, 0)


def shift_k(value, ahead):
    return pltpu.roll(value, 127 if ahead else 1, 1)


def coarse_setup_body(me_ref, left2_ref, left_ref, own_ref, right_ref, right2_ref, olow, ohigh, below_ref, above_ref,
                      coef_ref, sums_ref, offset_ref):
    pieces = [left2_ref[...], left_ref[18:32].reshape(112, 128), own_ref[...],
              right_ref[18:32].reshape(112, 128), right2_ref[...]]
    for x, cells in enumerate(offset_rows(olow, ohigh, below_ref, above_ref)):
        offset_ref[x, 0:3] = side(left_ref, WIDE, x, 0, 3, True)
        offset_ref[x, 3:11] = cells
        offset_ref[x, 11:14] = side(right_ref, WIDE, x, 0, 3, False)
    for y, (d, big_y) in enumerate(SPOTS):
        sums_ref[y] = pieces[d + 2][16 * big_y : 16 * big_y + 16]
    px, py, last_x, last_y = me_ref[0], me_ref[1], me_ref[2], me_ref[3]
    row = lax.broadcasted_iota(jnp.int32, (16, 128), 0)
    lane = lax.broadcasted_iota(jnp.int32, (16, 128), 1)
    pad = jnp.zeros((6, 128), F32)
    where_x = 2 * px - 4 + row
    inside_x = (where_x >= 0) & (where_x < 2 * (last_x + 1)) & (row < 10)

    def take(y, f):
        d, big_y = SPOTS[y]
        start = 32 + 20 * f + 10 * big_y
        return jnp.concatenate([pieces[d + 2][start : start + 10], pad], axis=0)

    links = [[FACES[f - 1] * take(y, f) for y in range(8)] for f in range(1, 4)]
    for y in range(8):
        where_y = 2 * py - 3 + y
        seen = jnp.where((where_y >= 0) & (where_y < 2 * (last_y + 1)), 1.0, 0.0).astype(F32)
        diag = jnp.where(inside_x, take(y, 0), 1.0)
        inverse = jnp.where(inside_x, seen / diag, 0.0)
        coef_ref[0, y] = inverse
        if 1 <= y <= 6:
            coef_ref[1, y] = links[0][y] * inverse
            coef_ref[2, y] = shift_x(links[0][y], False) * inverse
            coef_ref[3, y] = links[1][y] * inverse
            coef_ref[4, y] = links[1][y - 1] * inverse
            coef_ref[5, y] = jnp.where(lane < 127, links[2][y] * inverse, 0.0)
            coef_ref[6, y] = jnp.where(lane > 0, shift_k(links[2][y], False) * inverse, 0.0)
        else:
            for f in range(1, 7):
                coef_ref[f, y] = jnp.zeros((16, 128), F32)


def dots_of(pairs):
    lane = lax.broadcasted_iota(jnp.int32, (1, 128), 1)
    out = jnp.zeros((1, 128), F32)
    for k, value in enumerate(pairs):
        out = jnp.where(lane == k, jnp.sum(value), out)
    return out


def shared_sums(left2_ref, left_ref, early_ref, late_ref, right_ref, right2_ref):
    def share(d, j):
        if d in (-1, 1):
            ref = left_ref if d < 0 else right_ref
            return ref[10 + 2 * j : 12 + 2 * j].reshape(16, 128)
        ref = {-2: left2_ref, 0: early_ref if j < 2 else late_ref, 2: right2_ref}[d]
        return ref[16 * (j % 2) : 16 * (j % 2) + 16, :]

    return [share(d, big_y + 1) + (share(d - 1, 3) if big_y == 0 else share(d + 1, 0)) for d, big_y in SPOTS]


def correct_rows(sums, coef_ref, smooth, remain, inverse_ref, scale_ref, offset_ref):
    start = [sums[y] * coef_ref[0, y] for y in range(8)]

    def sweep(now, y):
        here = now[y]
        total = start[y] + coef_ref[1, y] * shift_x(here, True) + coef_ref[2, y] * shift_x(here, False)
        total = total + coef_ref[3, y] * now[y + 1] + coef_ref[4, y] * now[y - 1]
        return total + coef_ref[5, y] * shift_k(here, True) + coef_ref[6, y] * shift_k(here, False)

    second = [None] + [sweep(start, y) for y in range(1, 7)] + [None]
    third = [None, None] + [sweep(second, y) for y in range(2, 6)]
    sub = lax.broadcasted_iota(jnp.int32, (8, 128), 0)
    lane = lax.broadcasted_iota(jnp.int32, (8, 128), 1)
    index = sub * 16 + lane // 8

    def spread_out(tile, x):
        wide = jnp.broadcast_to(tile[x + 4 : x + 5, :], (8, 128))
        return jnp.take_along_axis(wide, index, axis=1)

    tables = [[], [], []]
    for y in range(2, 6):
        for k, tile in enumerate((third[y], shift_k(third[y], True), shift_k(third[y], False))):
            tables[k].append([spread_out(tile, x) for x in range(-2, 4)])
    counts = (3, 4, 4, 3)

    def lifted(x):
        big_x = x // 2
        here, up, down = (
            jnp.concatenate(
                [jnp.broadcast_to(tables[k][y][big_x + 2][None], (counts[y], 8, 128)) for y in range(4)], axis=0
            )
            for k in range(3)
        )
        offset = offset_ref[x + 3]
        return jnp.where(offset > 0.5, up, jnp.where(offset < -0.5, down, here))

    lifts = [lifted(x) for x in range(-3, 7)]
    spreads = []
    for x in range(8):
        near = beside(lifts[x][1:13], lifts[x + 1], lifts[x + 2][1:13])
        spreads.append(REST * lifts[x + 1][1:13] + OMEGA * (inverse_ref[x] * near))
    shaped = []
    for x in range(6):
        near = beside(spreads[x][1:11], spreads[x + 1], spreads[x + 2][1:11])
        spread = spreads[x + 1][1:11]
        left = remain[x] - (scale_ref[x] * spread - near)
        shaped.append(smooth[x] + spread + OMEGA * (inverse_ref[x + 1, 1:11] * left))
    for x in range(4):
        near = beside(shaped[x][1:9], shaped[x + 1], shaped[x + 2][1:9])
        own = shaped[x + 1][1:9]
        yield x, own, scale_ref[x + 1, 1:9] * own - near


def put(low_ref, high_ref, x, value):
    (low_ref if x < 2 else high_ref)[x % 2] = value


def half(low_ref, high_ref, x):
    return (low_ref if x < 2 else high_ref)[x % 2]


def products(left, right):
    return [jnp.sum(a * b, axis=0) for a in left for b in right]


def begin_body(*refs):
    sums, fixed, (z_ref, wlow_ref, whigh_ref) = refs[0], refs[1:7], refs[7:]
    for x, z, w in correct_rows([sums[y] for y in range(8)], *fixed):
        z_ref[x] = z
        put(wlow_ref, whigh_ref, x, w)


def received(refs):
    left2, early, late, right2, low, high, below, above, left, right = refs
    return widened(low, high, below, above, left, right), shared_sums(left2, left, early, late, right, right2)


def corrected(vectors, sums, refs):
    coef, fixed = refs[0], refs[1:4]
    smooth, remain = smoothed_rows(lambda x: vectors[x], fixed[0])
    return correct_rows(sums, coef, smooth, remain, *fixed)


def second_body(*refs):
    low_ref, high_ref, z_ref, m_ref, nlow_ref, nhigh_ref, dots_ref = refs[14:]
    wlow_ref, whigh_ref = refs[4:6]
    sums = [jnp.zeros((8, 128), F32)] * 6
    for x, m, n in corrected(*received(refs[:10]), refs[10:14]):
        m_ref[x] = m
        put(nlow_ref, nhigh_ref, x, n)
        here = products((half(low_ref, high_ref, x), half(wlow_ref, whigh_ref, x), n), (z_ref[x], m))
        sums = [a + b for a, b in zip(sums, here)]
    dots_ref[...] = dots_of(sums)


def two_sum(a, b):
    total = a + b
    part = total - a
    return total, (a - (total - part)) + (b - part)


def split(a):
    wide = a * 4097.0
    high = wide - (wide - a)
    return high, a - high


def two_product(a, b):
    product = a * b
    a_high, a_low = split(a)
    b_high, b_low = split(b)
    return product, a_low * b_low - (((product - a_high * b_high) - a_low * b_high) - a_high * b_low)


def pair_add(a, b):
    total, rest = two_sum(a[0], b[0])
    return two_sum(total, rest + (a[1] + b[1]))


def pair_times(a, b):
    product, rest = two_product(a[0], b[0])
    return two_sum(product, rest + (a[0] * b[1] + a[1] * b[0]))


def total_of(got_ref, row, rest_row):
    total = got_ref[0, row : row + 1, :]
    rest = jnp.zeros((1, 128), F32) if rest_row is None else got_ref[0, rest_row : rest_row + 1, :]
    for j in range(1, got_ref.shape[0]):
        total, lost = two_sum(total, got_ref[j, row : row + 1, :])
        rest = rest + lost
        if rest_row is not None:
            rest = rest + got_ref[j, rest_row : rest_row + 1, :]
    return total, rest


def gathered(tiles):
    total, rest = tiles[0][0:1], tiles[0][1:2]
    for tile in tiles[1:]:
        total, lost = two_sum(total, tile[0:1])
        rest = rest + (lost + tile[1:2])
    return two_sum(total, rest)


def pairs_of(total, rest, count):
    return [
        (jnp.broadcast_to(total[:, k : k + 1], (1, 128)), jnp.broadcast_to(rest[:, k : k + 1], (1, 128)))
        for k in range(count)
    ]


def form(table, left, weights):
    out = None
    for i, row in enumerate(left):
        for j, entry in enumerate(table[row]):
            factor = None
            for w in (weights[i], weights[j]):
                if w is not None:
                    factor = w if factor is None else pair_times(factor, w)
            term = entry if factor is None else pair_times(entry, factor)
            out = term if out is None else pair_add(out, term)
    return out[0] + out[1]


def tiled(row):
    return jnp.broadcast_to(row, (8, 128))[None]


def negated(pair):
    return -pair[0], -pair[1]


def third_body(*refs):
    k_ref, llow_ref, lhigh_ref, part_ref = refs[14:]
    early, right2, left, right = refs[1], refs[3], refs[8], refs[9]
    total, rest = gathered([early[32:40, :], left[18], right[18], right2[32:40, :]])
    part_ref[...] = jnp.concatenate([total, rest, jnp.zeros((6, 128), F32)], axis=0)
    for x, k, l in corrected(*received(refs[:10]), refs[10:14]):
        k_ref[x] = k
        put(llow_ref, lhigh_ref, x, l)


def fourth_body(*refs):
    rows, window = zip(*(received(refs[10 * i : 10 * i + 10]) for i in range(3)))
    rest = refs[30:34]
    parts, refs = refs[34:38], refs[38:]
    low_ref, high_ref, z_ref, m_ref, k_ref = refs[:5]
    zo_ref, wolow_ref, wohigh_ref, mo_ref, no_ref, xo_ref, ro_ref, po_ref, so_ref, qo_ref, to_ref = refs[5:16]
    keep_ref, dots_ref = refs[16:]
    sums = pairs_of(*gathered([part[...] for part in parts]), 6)
    table = [sums[0:2], sums[2:4], sums[4:6]]
    gamma0 = table[0][0][0]
    alpha0 = gamma0 / table[1][0][0]
    weights = (None, negated((alpha0, jnp.zeros_like(alpha0))))
    gamma1 = form(table, (0, 1), weights)
    delta1 = form(table, (1, 2), weights)
    beta1 = gamma1 / gamma0
    alpha1 = gamma1 / (delta1 - beta1 * gamma1 / alpha0)
    lane = lax.broadcasted_iota(jnp.int32, (1, 128), 1)
    keep_ref[...] = jnp.where(lane == 0, gamma1, jnp.where(lane == 1, alpha1, 0.0))
    alphas = [(tiled(alpha0), tiled(alpha1), tiled(beta1)), (alpha0, alpha1, beta1)]

    def turned(w, n, l, alpha0, alpha1, beta1):
        t = (n - alpha0 * l) + beta1 * n
        return (w - alpha0 * n) - alpha1 * t, t

    vectors = [turned(*(rows[i][x] for i in range(3)), *alphas[0])[0] for x in range(8)]
    window = [turned(*(window[i][y] for i in range(3)), *alphas[1])[0] for y in range(8)]
    alpha0, alpha1, beta1 = alphas[0]
    sums = [jnp.zeros((8, 128), F32)] * 15
    for x, m2, n2 in corrected(vectors, window, rest):
        w0, n0, l = (rows[i][x + 2][2:10] for i in range(3))
        z0, m0, k = z_ref[x], m_ref[x], k_ref[x]
        w2, t = turned(w0, n0, l, *alphas[0])
        z2, q = turned(z0, m0, k, *alphas[0])
        p, s = (z0 - alpha0 * m0) + beta1 * z0, (w0 - alpha0 * n0) + beta1 * w0
        r2 = (half(low_ref, high_ref, x) - alpha0 * w0) - alpha1 * s
        xo_ref[x] = alpha0 * z0 + alpha1 * p
        ro_ref[x], zo_ref[x] = r2, z2
        put(wolow_ref, wohigh_ref, x, w2)
        mo_ref[x], no_ref[x] = m2, n2
        po_ref[x], so_ref[x], qo_ref[x], to_ref[x] = p, s, q, t
        sums = [a + b for a, b in zip(sums, products((r2, w2, s, n2, t), (z2, m2, q)))]
    dots_ref[...] = dots_of(sums)


def spread_dots_body(dots_ref, send_ref):
    tile = jnp.concatenate([dots_ref[...], jnp.zeros((7, 128), F32)], axis=0)
    for j in range(send_ref.shape[0]):
        send_ref[j] = tile


def sum_dots_body(got_ref, send_ref):
    total, rest = total_of(got_ref, 0, None)
    tile = jnp.concatenate([total, rest, jnp.zeros((6, 128), F32)], axis=0)
    for j in range(send_ref.shape[0]):
        send_ref[j] = tile


def finish_body(got_ref, z_ref, wlow_ref, whigh_ref, m_ref, n_ref, x_ref, r_ref, p_ref, s_ref, q_ref, t_ref, keep_ref,
                xo_ref, ro_ref, xs_ref, rs_ref):
    sums = pairs_of(*two_sum(*total_of(got_ref, 0, 1)), 15)
    table = [sums[3 * k : 3 * k + 3] for k in range(5)]
    keep = keep_ref[...]
    gamma1 = jnp.broadcast_to(keep[:, 0:1], (1, 128))
    alpha1 = jnp.broadcast_to(keep[:, 1:2], (1, 128))
    gamma2 = table[0][0][0]
    beta2 = gamma2 / gamma1
    alpha2 = gamma2 / (table[1][0][0] - beta2 * gamma2 / alpha1)
    weights = (None, (-alpha2, jnp.zeros_like(alpha2)), two_product(-alpha2, beta2))
    gamma3 = form(table, (0, 1, 2), weights)
    delta3 = form(table, (1, 3, 4), weights)
    beta3 = gamma3 / gamma2
    alpha3 = gamma3 / (delta3 - beta3 * gamma3 / alpha2)
    alpha2, beta2, alpha3, beta3 = tiled(alpha2), tiled(beta2), tiled(alpha3), tiled(beta3)
    for x in range(4):
        z, w, q1, t1 = z_ref[x], half(wlow_ref, whigh_ref, x), q_ref[x], t_ref[x]
        p2, s2 = z + beta2 * p_ref[x], w + beta2 * s_ref[x]
        q2, t2 = m_ref[x] + beta2 * q1, n_ref[x] + beta2 * t1
        p3 = (z - alpha2 * q2) + beta3 * p2
        s3 = (w - alpha2 * t2) + beta3 * s2
        xs_ref[pl.ds(64 * x, 64), :] = ((x_ref[x] + alpha2 * p2) + alpha3 * p3).reshape(64, 128)
        rs_ref[pl.ds(64 * x, 64), :] = ((r_ref[x] - alpha2 * s2) - alpha3 * s3).reshape(64, 128)
    for x in range(4):
        for s in range(8):
            part = slice(s * 128, (s + 1) * 128)
            xo_ref[x, :, part] = xs_ref[pl.ds(64 * x + s, 8, stride=8), :]
            ro_ref[x, :, part] = rs_ref[pl.ds(64 * x + s, 8, stride=8), :]


def local(right_side, diagonal, aggregate_id, coarse_diag, coarse_link):
    count_x, count_y = lax.axis_size("px"), lax.axis_size("py")
    me = jnp.stack([lax.axis_index("px"), lax.axis_index("py"), count_x - 1, count_y - 1]).astype(jnp.int32)

    def both_ways(low, high, axis, far=1):
        count = lax.axis_size(axis)
        up = [(i, (i + far) % count) for i in range(count)]
        down = [(b, a) for a, b in up]
        return lax.ppermute(high, axis, up), lax.ppermute(low, axis, down)

    def gather(value, axis):
        return lax.all_to_all(value, axis, 0, 0)

    two, field = (2, 8, 8, 128), (4, 8, 8, 128)
    low, high = call(enter_body, [(256, 128)] * 2, right_side, diagonal, scalars=0)
    low, high = low.reshape(4, 8, 8, 128), high.reshape(4, 8, 8, 128)
    xlow, xhigh = both_ways(low, high, "px")
    olow, ohigh, coarse = call(
        enter_more_body, [(192, 128)] * 2 + [(16, 128)], aggregate_id, coarse_diag, coarse_link, low, scalars=0
    )
    olow, ohigh = olow.reshape(3, 8, 8, 128), ohigh.reshape(3, 8, 8, 128)
    first, last = call(pack_first_body, [(20, 8, 128)] * 2, low, high, xlow, xhigh, scalars=0)
    ylow, yhigh = both_ways(first, last, "py")
    inverse, scale = call(
        setup_body, [(8, 12, 8, 128), (6, 10, 8, 128)], me, low, high, xlow, xhigh, ylow, yhigh
    )
    mid, dots = (6, 10, 8, 128), (1, 128)
    smooth, remain, send, down, up = call(
        restrict_body, [mid, mid, (24, 128)] + [(27, 8, 128)] * 2,
        low, high, xlow, xhigh, ylow, yhigh, inverse, olow, ohigh, coarse, scalars=0,
    )
    below, above = both_ways(down, up, "px")
    below2, above2 = both_ways(send, send, "px", 2)
    first, last, send = call(
        window_first_body, [(32, 8, 128)] * 2 + [(112, 128)],
        below2, below, send, above, above2, olow, ohigh, scalars=0,
    )
    left, right = both_ways(first, last, "py")
    left2, right2 = both_ways(send, send, "py", 2)
    coef, sums, offset = call(
        coarse_setup_body, [(7, 8, 16, 128), (8, 16, 128), (10, 14, 8, 128)],
        me, left2, left, send, right, right2, olow, ohigh, below, above,
    )
    fixed = (inverse, scale, offset)
    z, wlow, whigh = call(begin_body, [field, two, two], sums, coef, smooth, remain, *fixed, scalars=0)

    packed = [(18, 8, 128)] * 2 + [(32, 128)] * 2

    def beside_y(low, high, below, above, first, last, early, late):
        left, right = both_ways(first, last, "py")
        left2, right2 = both_ways(early, late, "py", 2)
        return left2, early, late, right2, low, high, below, above, left, right

    def exchanged(low, high):
        share, down, up = call(
            contribute_body, [(16, 128), (18, 8, 128), (18, 8, 128)], low, high, inverse, offset, scalars=0
        )
        below, above = both_ways(down, up, "px")
        below2, above2 = both_ways(share, share, "px", 2)
        below3, above3 = both_ways(share, share, "px", 3)
        outs = call(
            pack_body, packed, low, high, below3, below2, below, share, above, above2, above3, scalars=0
        )
        return beside_y(low, high, below, above, *outs)

    def exchanged_and_summed(low, high, sums):
        send, = call(
            contribute_and_sum_body, [(count_x, 24, 128)], low, high, inverse, offset, sums, scalars=0
        )
        below, above = both_ways(low, high, "px")
        below, above = below.reshape(16, 8, 128), above.reshape(16, 8, 128)
        outs = call(
            pack_and_sum_body, [(19, 8, 128)] * 2 + [(40, 128)] * 2, me, low, high, below, above, gather(send, "px")
        )
        return beside_y(low, high, below, above, *outs)

    def summed(sums):
        send, = call(spread_dots_body, [(count_x, 8, 128)], sums, scalars=0)
        send, = call(sum_dots_body, [(count_y, 8, 128)], gather(send, "px"), scalars=0)
        return gather(send, "py")

    fixed = (coef, *fixed)
    first = exchanged(wlow, whigh)
    m, nlow, nhigh, sums = call(
        second_body, [field, two, two, dots], *first, *fixed, low, high, z, scalars=0
    )
    second = exchanged_and_summed(nlow, nhigh, sums)
    k, llow, lhigh, part = call(third_body, [field, two, two, (8, 128)], *second, *fixed, scalars=0)
    parts = (part, *both_ways(part, part, "py", 4), both_ways(part, part, "py", 8)[0])
    third = exchanged(llow, lhigh)
    z, wlow, whigh, m, n, x, r, p, s, q, t, keep, sums = call(
        fourth_body, [field, two, two] + [field] * 8 + [dots] * 2,
        *first, *second, *third, *fixed, *parts, low, high, z, m, k, scalars=0,
    )
    return tuple(call(
        finish_body, [right_side.shape] * 2,
        summed(sums), z, wlow, whigh, m, n, x, r, p, s, q, t, keep,
        scalars=0, scratch=[pltpu.VMEM((256, 128), F32)] * 2,
    ))


def solution(mesh):
    cells = P("px", "py", None)
    in_specs = (cells, cells, cells, cells, P(None, "px", "py", None))
    return jax.shard_map(local, mesh=mesh, in_specs=in_specs, out_specs=(cells, cells), check_vma=False)
```

```python
import jax
import jax.numpy as jnp
from jax import lax
from jax.experimental import pallas as pl
from jax.experimental.pallas import tpu as pltpu
from jax.sharding import PartitionSpec as P

OMEGA = 2.0 / 3.0
REST = 1.0 - OMEGA
FACES = (32.0, 16.0, 8.0)
F32 = jnp.float32


def call(body, outs, *args, scalars=1, scratch=(), flops=2_000_000):
    smem = pl.BlockSpec(memory_space=pltpu.SMEM)
    vmem = pl.BlockSpec(memory_space=pltpu.VMEM)
    specs = [smem] * scalars + [vmem] * (len(args) - scalars)
    return pl.pallas_call(
        body,
        out_shape=[jax.ShapeDtypeStruct(shape, F32) for shape in outs],
        in_specs=specs,
        out_specs=[vmem] * len(outs),
        scratch_shapes=list(scratch),
        compiler_params=pltpu.CompilerParams(vmem_limit_bytes=20 * 1024 * 1024),
        cost_estimate=pl.CostEstimate(flops=flops, bytes_accessed=1_000_000, transcendentals=0),
    )(*args)


def along_z(value):
    lane = lax.broadcasted_iota(jnp.int32, value.shape, value.ndim - 1)
    sub = lax.broadcasted_iota(jnp.int32, value.shape, value.ndim - 2)
    after = pltpu.roll(value, 127, value.ndim - 1)
    before = pltpu.roll(value, 1, value.ndim - 1)
    after_row = jnp.where(sub == 7, 0.0, pltpu.roll(after, 7, value.ndim - 2))
    before_row = jnp.where(sub == 0, 0.0, pltpu.roll(before, 1, value.ndim - 2))
    return jnp.where(lane == 127, after_row, after) + jnp.where(lane == 0, before_row, before)


def by_eight(value, ahead):
    lane = lax.broadcasted_iota(jnp.int32, value.shape, value.ndim - 1)
    if ahead:
        moved = pltpu.roll(value, 120, value.ndim - 1)
        return jnp.where(lane >= 120, pltpu.roll(moved, 7, value.ndim - 2), moved)
    moved = pltpu.roll(value, 8, value.ndim - 1)
    return jnp.where(lane < 8, pltpu.roll(moved, 1, value.ndim - 2), moved)


def beside(below, here, above):
    count = here.shape[0]
    inner = here[1 : count - 1]
    return below + above + here[0 : count - 2] + here[2:count] + along_z(inner)


def enter_body(b_ref, d_ref, low_ref, high_ref):
    for x in range(4):
        for s in range(8):
            part = slice(s * 128, (s + 1) * 128)
            ref = low_ref if x < 2 else high_ref
            at = (x % 2) * 64 + s
            ref[pl.ds(at, 8, stride=8), :] = b_ref[x, :, part]
            ref[pl.ds(128 + at, 8, stride=8), :] = d_ref[x, :, part]


def enter_more_body(a_ref, cdiag_ref, link_ref, after_ref, olow_ref, ohigh_ref, coarse_ref):
    lane = lax.broadcasted_iota(jnp.int32, (8, 128), 1)
    for x in range(4):
        for s in range(8):
            home = (lane + s * 128) // 8
            o = ((a_ref[x, :, s * 128 : (s + 1) * 128] & 127) - home).astype(F32)
            if x < 3:
                olow_ref[pl.ds(x * 64 + s, 8, stride=8), :] = o
            if x > 0:
                ohigh_ref[pl.ds((x - 1) * 64 + s, 8, stride=8), :] = o
    rows = []
    for ref in (cdiag_ref, link_ref.at[0], link_ref.at[1], link_ref.at[2]):
        rows = rows + [ref[c // 2, c % 2 : c % 2 + 1, :] for c in range(4)]
    coarse_ref[...] = jnp.concatenate(rows, axis=0)


def field_rows(low, high, xlow, xhigh, base):
    return [ref.at[base + k] for ref in (xlow, low, high, xhigh) for k in range(2)]


def offset_rows(olow, ohigh, below, above):
    rows = [below[8 * k : 8 * k + 8] for k in range(3)] + [olow[k] for k in range(3)] + [ohigh[2]]
    return rows + [above[8 * k : 8 * k + 8] for k in range(3)]


SIDE = {2: (0, 2), 3: (2, 2), 4: (4, 2), 5: (6, 2), 1: (8, 1), 6: (9, 1)}
WIDE = {3: (0, 3), 4: (3, 3), 5: (6, 3), 6: (9, 3), 2: (12, 2), 7: (14, 2), 1: (16, 1), 8: (17, 1)}


def send_sides(spots, rows, base, first_ref, last_ref):
    for x, (at, count) in spots.items():
        first_ref[base + at : base + at + count] = rows[x][0:count]
        last_ref[base + at : base + at + count] = rows[x][8 - count : 8]


def side(ref, spots, x, base, width, left):
    at, count = spots.get(x, (0, 0))
    zero = jnp.zeros((width - count, 8, 128), F32)
    if count == 0:
        return zero
    value = ref[base + at : base + at + count]
    if count == width:
        return value
    return jnp.concatenate([zero, value] if left else [value, zero], axis=0)


def pack_first_body(low_ref, high_ref, xlow_ref, xhigh_ref, first_ref, last_ref):
    four = (low_ref, high_ref, xlow_ref, xhigh_ref)
    for f in range(2):
        send_sides(SIDE, [ref[...] for ref in field_rows(*four, 2 * f)], 10 * f, first_ref, last_ref)


def setup_body(me_ref, low_ref, high_ref, xlow_ref, xhigh_ref, ylow_ref, yhigh_ref, inverse_ref):
    px, py, last_x, last_y = me_ref[0], me_ref[1], me_ref[2], me_ref[3]
    below = jnp.where(px > 0, 1.0, 0.0).astype(F32)
    above = jnp.where(px < last_x, 1.0, 0.0).astype(F32)
    left = jnp.where(py > 0, 1.0, 0.0).astype(F32)
    right = jnp.where(py < last_y, 1.0, 0.0).astype(F32)
    four = (low_ref, high_ref, xlow_ref, xhigh_ref)
    for x, ref in enumerate(field_rows(*four, 2)):
        s_mid = 6.0 + ref[...]
        s_left = 6.0 + side(ylow_ref, SIDE, x, 10, 2, True)
        s_right = 6.0 + side(yhigh_ref, SIDE, x, 10, 2, False)
        i_mid, i_left, i_right = 1.0 / s_mid, left / s_left, right / s_right
        if x < 2 or x > 5:
            seen = below if x < 2 else above
            i_mid, i_left, i_right = i_mid * seen, i_left * seen, i_right * seen
        inverse_ref[x, 0:2] = i_left
        inverse_ref[x, 2:10] = i_mid
        inverse_ref[x, 10:12] = i_right

def scale_body(low_ref, high_ref, xlow_ref, xhigh_ref, ylow_ref, yhigh_ref, scale_ref):
    rows = field_rows(low_ref, high_ref, xlow_ref, xhigh_ref, 2)
    for x in range(1, 7):
        scale_ref[x - 1, 0:1] = 6.0 + side(ylow_ref, SIDE, x, 10, 2, True)[1:2]
        scale_ref[x - 1, 1:9] = 6.0 + rows[x][...]
        scale_ref[x - 1, 9:10] = 6.0 + side(yhigh_ref, SIDE, x, 10, 2, False)[0:1]


def padded(value, width):
    zero = jnp.zeros((width, 8, 128), F32)
    return jnp.concatenate([zero, value, zero], axis=0)


def contribute_body(low_ref, high_ref, inverse_ref, offset_ref, share_ref, down_ref, up_ref):
    share = shares(low_ref, high_ref, inverse_ref, offset_ref)
    share_ref[...] = share
    for ref, cells in ((down_ref, low_ref), (up_ref, high_ref)):
        for k in range(2):
            ref[8 * k : 8 * k + 8] = cells[k]
            ref[16 + k] = share[8 * k : 8 * k + 8]


def contribute_and_sum_body(low_ref, high_ref, inverse_ref, offset_ref, dots_ref, send_ref):
    share = shares(low_ref, high_ref, inverse_ref, offset_ref)
    more = jnp.concatenate([dots_ref[...], jnp.zeros((7, 128), F32)], axis=0)
    for j in range(send_ref.shape[0]):
        send_ref[j, 0:16] = share
        send_ref[j, 16:24] = more


def shares(low_ref, high_ref, inverse_ref, offset_ref):
    vector = [half(low_ref, high_ref, x) for x in range(4)]
    smooth = [OMEGA * vector[x] * inverse_ref[x + 2, 2:10] for x in range(4)]
    remains = [padded(smooth[0], 1)]
    for x in range(4):
        around = padded(smooth[x], 1)
        center = REST * vector[x] + (around[0:8] + around[2:10] + along_z(smooth[x]))
        for other in (x - 1, x + 1):
            if 0 <= other < 4:
                center = center + smooth[other]
        remains.append(jnp.concatenate([smooth[x][0:1], center, smooth[x][7:8]], axis=0))
    remains.append(padded(smooth[3], 1))
    shrunk = [remains[x] * inverse_ref[x + 1, 1:11] for x in range(6)]
    cells = []
    for x in range(8):
        near = None
        for other in (x - 2, x):
            if 0 <= other < 6:
                near = shrunk[other] if near is None else near + shrunk[other]
        if 1 <= x <= 6:
            near = padded(near + along_z(shrunk[x - 1]), 1)
            wide = padded(shrunk[x - 1], 2)
            value = REST * padded(remains[x - 1], 1) + OMEGA * (near + (wide[0:12] + wide[2:14]))
        else:
            value = padded(OMEGA * near, 1)
        value = jnp.where(inverse_ref[x] > 0.0, value, 0.0)
        offset = offset_ref[x + 1, 1:13]
        cells.append((
            jnp.where(jnp.abs(offset) < 0.5, value, 0.0),
            jnp.where(offset > 0.5, value, 0.0),
            jnp.where(offset < -0.5, value, 0.0),
        ))
    sums = []
    for start, stop in ((0, 2), (2, 6), (6, 10), (10, 12)):
        for i in range(4):
            here, up, down = (
                jnp.sum(cells[2 * i][k][start:stop], axis=0) + jnp.sum(cells[2 * i + 1][k][start:stop], axis=0)
                for k in range(3)
            )
            sums.append(here + by_eight(up, False) + by_eight(down, True))
    return jnp.concatenate(grouped_rows(sums), axis=0)


def grouped_rows(sums):
    stacked = jnp.concatenate(sums, axis=0)
    row = lax.broadcasted_iota(jnp.int32, (128, 128), 0)
    col = lax.broadcasted_iota(jnp.int32, (128, 128), 1)
    group = jnp.where(row // 8 == col % 16, 1.0, 0.0).astype(F32)
    grouped = jnp.dot(stacked, group, preferred_element_type=F32, precision=lax.Precision.HIGHEST)
    sub = lax.broadcasted_iota(jnp.int32, (8, 128), 0)
    lane = lax.broadcasted_iota(jnp.int32, (8, 128), 1)
    return [
        jnp.sum(jnp.where(lane // 16 == sub, grouped[8 * c : 8 * c + 8], 0.0), axis=0, keepdims=True)
        for c in range(len(sums))
    ]


def pack_rows(mids, row, first_ref, last_ref, early_ref, late_ref):
    send_sides(SIDE, [mid() for mid in mids], 0, first_ref, last_ref)
    zero = jnp.zeros((6, 128), F32)
    for j in range(4):
        rows = []
        for d in range(-2, 3):
            rows.append(row(d, 4 * j + 1) + row(d - 1, 4 * j + 3))
            rows.append(row(d, 4 * j + 2) + row(d + 1, 4 * j))
        tile = jnp.concatenate(rows + [zero], axis=0)
        ref = early_ref if j < 2 else late_ref
        ref[16 * (j % 2) : 16 * (j % 2) + 16] = tile
        for k in range(2):
            first_ref[10 + 2 * j + k] = tile[8 * k : 8 * k + 8]
            last_ref[10 + 2 * j + k] = tile[8 * k : 8 * k + 8]


def pack_body(low_ref, high_ref, below3_ref, below2_ref, below_ref, share_ref, above_ref, above2_ref, above3_ref, *outs):
    flat = {-3: below3_ref, -2: below2_ref, 0: share_ref, 2: above2_ref, 3: above3_ref}
    joined = {-1: below_ref, 1: above_ref}

    def row(d, at):
        if d in flat:
            return flat[d][at : at + 1, :]
        return joined[d][16 + at // 8, at % 8 : at % 8 + 1, :]

    pack_rows(row_blocks(low_ref, high_ref, below_ref, above_ref), row, *outs)


def pack_and_sum_body(me_ref, low_ref, high_ref, below_ref, above_ref, got_ref, *outs):
    count = got_ref.shape[0]
    spots = {d: lax.rem(me_ref[0] + (d + count), count) for d in range(-3, 4)}

    def row(d, at):
        return got_ref[spots[d], at : at + 1, :]

    pack_rows(row_blocks(low_ref, high_ref, below_ref, above_ref), row, *outs)
    total, rest = total_of(got_ref, 16, None)
    tile = jnp.concatenate([total, rest, jnp.zeros((6, 128), F32)], axis=0)
    for ref in outs[:2]:
        ref[18] = tile
    for ref in outs[2:]:
        ref[32:40] = tile


def row_blocks(low_ref, high_ref, below_ref, above_ref):
    def sent(ref, k):
        return lambda: ref[8 * k : 8 * k + 8]

    def own(ref, k):
        return lambda: ref[k]

    blocks = [sent(below_ref, k) for k in range(2)] + [own(low_ref, k) for k in range(2)]
    return blocks + [own(high_ref, k) for k in range(2)] + [sent(above_ref, k) for k in range(2)]


def smoothed_rows(vector, inverse_ref):
    smooth = [OMEGA * vector(x) * inverse_ref[x] for x in range(8)]
    remains = [
        REST * vector(x)[1:11] + beside(smooth[x - 1][1:11], smooth[x], smooth[x + 1][1:11]) for x in range(1, 7)
    ]
    return [smooth[x][1:11] for x in range(1, 7)], remains


def widened(low, high, below, above, left, right):
    mids = row_blocks(low, high, below, above)

    def vector(x):
        return jnp.concatenate([side(left, SIDE, x, 0, 2, True), mids[x](), side(right, SIDE, x, 0, 2, False)], axis=0)

    return [vector(x) for x in range(8)]


def restrict_body(low, high, xlow, xhigh, ylow, yhigh, inverse_ref, olow, ohigh, coarse_ref,
                  smooth_ref, remain_ref, send_ref, down_ref, up_ref):
    mids = [ref.at[k] for ref in (xlow, low, high, xhigh) for k in range(2)]

    def vector(x):
        return jnp.concatenate(
            [side(ylow, SIDE, x, 0, 2, True), mids[x][...], side(yhigh, SIDE, x, 0, 2, False)], axis=0
        )

    smooth, full = smoothed_rows(vector, inverse_ref)
    shrunk, remains = [], []
    for x in range(6):
        smooth_ref[x] = smooth[x]
        remain_ref[x] = full[x]
        remains.append(full[x][1:9])
        shrunk.append(full[x] * inverse_ref[x + 1, 1:11])
    sums = []
    for big_x in range(2):
        parts = []
        for x in (2 * big_x, 2 * big_x + 1):
            near = beside(shrunk[x][1:9], shrunk[x + 1], shrunk[x + 2][1:9])
            reduced = REST * remains[x + 1] + OMEGA * near
            offset = olow[x] if x < 3 else ohigh[2]
            parts.append((
                jnp.where(jnp.abs(offset) < 0.5, reduced, 0.0),
                jnp.where(offset > 0.5, reduced, 0.0),
                jnp.where(offset < -0.5, reduced, 0.0),
            ))
        for big_y in range(2):
            cols = slice(4 * big_y, 4 * big_y + 4)
            here, up, down = (
                jnp.sum(parts[0][k][cols], axis=0) + jnp.sum(parts[1][k][cols], axis=0) for k in range(3)
            )
            sums.append(here + by_eight(up, False) + by_eight(down, True))
    send_ref[0:8] = jnp.concatenate(grouped_rows(sums) + [jnp.zeros((4, 128), F32)], axis=0)
    send_ref[8:24] = coarse_ref[...]
    for ref, cells in ((down_ref, olow), (up_ref, ohigh)):
        for k in range(3):
            ref[8 * k : 8 * k + 8] = cells[k]
            ref[24 + k] = send_ref[8 * k : 8 * k + 8]


def window_rows(row, start):
    return [[row(d, start + 2 * big_x + big_y) for d in range(-2, 3) for big_x in range(2)] for big_y in range(2)]


def window_first_body(below2_ref, below_ref, own_ref, above_ref, above2_ref, olow, ohigh, first_ref, last_ref, send_ref):
    flat, joined = {-2: below2_ref, 0: own_ref, 2: above2_ref}, {-1: below_ref, 1: above_ref}

    def row(d, at):
        if d in flat:
            return flat[d][at : at + 1, :]
        return joined[d][24 + at // 8, at % 8 : at % 8 + 1, :]

    zero = jnp.zeros((6, 128), F32)
    early, late = window_rows(row, 0)
    rows = early + [zero] + late + [zero]
    for f in range(4):
        early, late = window_rows(row, 8 + 4 * f)
        rows = rows + early + late
    send_ref[...] = jnp.concatenate(rows, axis=0)
    send_sides(WIDE, offset_rows(olow, ohigh, below_ref, above_ref), 0, first_ref, last_ref)
    for k in range(14):
        first_ref[18 + k] = send_ref[8 * k : 8 * k + 8]
        last_ref[18 + k] = send_ref[8 * k : 8 * k + 8]


SPOTS = ((-2, 1), (-1, 0), (-1, 1), (0, 0), (0, 1), (1, 0), (1, 1), (2, 0))


def shift_x(value, ahead):
    return pltpu.roll(value, 15 if ahead else 1, 0)


def shift_k(value, ahead):
    return pltpu.roll(value, 127 if ahead else 1, 1)


def coarse_setup_body(me_ref, left2_ref, left_ref, own_ref, right_ref, right2_ref, olow, ohigh, below_ref, above_ref,
                      coef_ref, sums_ref, offset_ref):
    pieces = [left2_ref[...], left_ref[18:32].reshape(112, 128), own_ref[...],
              right_ref[18:32].reshape(112, 128), right2_ref[...]]
    for x, cells in enumerate(offset_rows(olow, ohigh, below_ref, above_ref)):
        offset_ref[x, 0:3] = side(left_ref, WIDE, x, 0, 3, True)
        offset_ref[x, 3:11] = cells
        offset_ref[x, 11:14] = side(right_ref, WIDE, x, 0, 3, False)
    for y, (d, big_y) in enumerate(SPOTS):
        sums_ref[y] = pieces[d + 2][16 * big_y : 16 * big_y + 16]
    px, py, last_x, last_y = me_ref[0], me_ref[1], me_ref[2], me_ref[3]
    row = lax.broadcasted_iota(jnp.int32, (16, 128), 0)
    lane = lax.broadcasted_iota(jnp.int32, (16, 128), 1)
    pad = jnp.zeros((6, 128), F32)
    where_x = 2 * px - 4 + row
    inside_x = (where_x >= 0) & (where_x < 2 * (last_x + 1)) & (row < 10)

    def take(y, f):
        d, big_y = SPOTS[y]
        start = 32 + 20 * f + 10 * big_y
        return jnp.concatenate([pieces[d + 2][start : start + 10], pad], axis=0)

    links = [[FACES[f - 1] * take(y, f) for y in range(8)] for f in range(1, 4)]
    for y in range(8):
        where_y = 2 * py - 3 + y
        seen = jnp.where((where_y >= 0) & (where_y < 2 * (last_y + 1)), 1.0, 0.0).astype(F32)
        diag = jnp.where(inside_x, take(y, 0), 1.0)
        inverse = jnp.where(inside_x, seen / diag, 0.0)
        coef_ref[0, y] = inverse
        if 1 <= y <= 6:
            coef_ref[1, y] = links[0][y] * inverse
            coef_ref[2, y] = shift_x(links[0][y], False) * inverse
            coef_ref[3, y] = links[1][y] * inverse
            coef_ref[4, y] = links[1][y - 1] * inverse
            coef_ref[5, y] = jnp.where(lane < 127, links[2][y] * inverse, 0.0)
            coef_ref[6, y] = jnp.where(lane > 0, shift_k(links[2][y], False) * inverse, 0.0)
        else:
            for f in range(1, 7):
                coef_ref[f, y] = jnp.zeros((16, 128), F32)


def dots_of(pairs):
    lane = lax.broadcasted_iota(jnp.int32, (1, 128), 1)
    out = jnp.zeros((1, 128), F32)
    for k, value in enumerate(pairs):
        out = jnp.where(lane == k, jnp.sum(value), out)
    return out


def shared_sums(left2_ref, left_ref, early_ref, late_ref, right_ref, right2_ref):
    def share(d, j):
        if d in (-1, 1):
            ref = left_ref if d < 0 else right_ref
            return ref[10 + 2 * j : 12 + 2 * j].reshape(16, 128)
        ref = {-2: left2_ref, 0: early_ref if j < 2 else late_ref, 2: right2_ref}[d]
        return ref[16 * (j % 2) : 16 * (j % 2) + 16, :]

    return [share(d, big_y + 1) + (share(d - 1, 3) if big_y == 0 else share(d + 1, 0)) for d, big_y in SPOTS]


def correct_rows(sums, coef_ref, smooth, remain, inverse_ref, scale_ref, offset_ref):
    start = [sums[y] * coef_ref[0, y] for y in range(8)]

    def sweep(now, y):
        here = now[y]
        total = start[y] + coef_ref[1, y] * shift_x(here, True) + coef_ref[2, y] * shift_x(here, False)
        total = total + coef_ref[3, y] * now[y + 1] + coef_ref[4, y] * now[y - 1]
        return total + coef_ref[5, y] * shift_k(here, True) + coef_ref[6, y] * shift_k(here, False)

    second = [None] + [sweep(start, y) for y in range(1, 7)] + [None]
    third = [None, None] + [sweep(second, y) for y in range(2, 6)]
    sub = lax.broadcasted_iota(jnp.int32, (8, 128), 0)
    lane = lax.broadcasted_iota(jnp.int32, (8, 128), 1)
    index = sub * 16 + lane // 8

    def spread_out(tile, x):
        wide = jnp.broadcast_to(tile[x + 4 : x + 5, :], (8, 128))
        return jnp.take_along_axis(wide, index, axis=1)

    tables = [[], [], []]
    for y in range(2, 6):
        for k, tile in enumerate((third[y], shift_k(third[y], True), shift_k(third[y], False))):
            tables[k].append([spread_out(tile, x) for x in range(-2, 4)])
    counts = (3, 4, 4, 3)

    def lifted(x):
        big_x = x // 2
        here, up, down = (
            jnp.concatenate(
                [jnp.broadcast_to(tables[k][y][big_x + 2][None], (counts[y], 8, 128)) for y in range(4)], axis=0
            )
            for k in range(3)
        )
        offset = offset_ref[x + 3]
        return jnp.where(offset > 0.5, up, jnp.where(offset < -0.5, down, here))

    lifts = [lifted(x) for x in range(-3, 7)]
    spreads = []
    for x in range(8):
        near = beside(lifts[x][1:13], lifts[x + 1], lifts[x + 2][1:13])
        spreads.append(REST * lifts[x + 1][1:13] + OMEGA * (inverse_ref[x] * near))
    shaped = []
    for x in range(6):
        near = beside(spreads[x][1:11], spreads[x + 1], spreads[x + 2][1:11])
        spread = spreads[x + 1][1:11]
        left = remain[x] - (scale_ref[x] * spread - near)
        shaped.append(smooth[x] + spread + OMEGA * (inverse_ref[x + 1, 1:11] * left))
    for x in range(4):
        near = beside(shaped[x][1:9], shaped[x + 1], shaped[x + 2][1:9])
        own = shaped[x + 1][1:9]
        yield x, own, scale_ref[x + 1, 1:9] * own - near


def put(low_ref, high_ref, x, value):
    (low_ref if x < 2 else high_ref)[x % 2] = value


def half(low_ref, high_ref, x):
    return (low_ref if x < 2 else high_ref)[x % 2]


def products(left, right):
    return [jnp.sum(a * b, axis=0) for a in left for b in right]


def begin_body(*refs):
    sums, fixed, (z_ref, wlow_ref, whigh_ref) = refs[0], refs[1:7], refs[7:]
    for x, z, w in correct_rows([sums[y] for y in range(8)], *fixed):
        z_ref[x] = z
        put(wlow_ref, whigh_ref, x, w)


EXCHANGED = 10


def received(refs):
    left2, early, late, right2, low, high, below, above, left, right = refs
    return widened(low, high, below, above, left, right), shared_sums(left2, left, early, late, right, right2)


def corrected(vectors, sums, refs):
    coef, fixed = refs[0], refs[1:4]
    smooth, remain = smoothed_rows(lambda x: vectors[x], fixed[0])
    return correct_rows(sums, coef, smooth, remain, *fixed)


def second_body(*refs):
    low_ref, high_ref, z_ref, m_ref, nlow_ref, nhigh_ref, dots_ref = refs[14:]
    wlow_ref, whigh_ref = refs[4:6]
    sums = [jnp.zeros((8, 128), F32)] * 6
    for x, m, n in corrected(*received(refs[:10]), refs[10:14]):
        m_ref[x] = m
        put(nlow_ref, nhigh_ref, x, n)
        here = products((half(low_ref, high_ref, x), half(wlow_ref, whigh_ref, x), n), (z_ref[x], m))
        sums = [a + b for a, b in zip(sums, here)]
    dots_ref[...] = dots_of(sums)


def two_sum(a, b):
    total = a + b
    part = total - a
    return total, (a - (total - part)) + (b - part)


def split(a):
    wide = a * 4097.0
    high = wide - (wide - a)
    return high, a - high


def two_product(a, b):
    product = a * b
    a_high, a_low = split(a)
    b_high, b_low = split(b)
    return product, a_low * b_low - (((product - a_high * b_high) - a_low * b_high) - a_high * b_low)


def pair_add(a, b):
    total, rest = two_sum(a[0], b[0])
    return two_sum(total, rest + (a[1] + b[1]))


def pair_scale(a, factor):
    product, rest = two_product(a[0], factor)
    return two_sum(product, rest + a[1] * factor)


def pair_times(a, b):
    product, rest = two_product(a[0], b[0])
    return two_sum(product, rest + (a[0] * b[1] + a[1] * b[0]))


def total_of(got_ref, row, rest_row):
    total = got_ref[0, row : row + 1, :]
    rest = jnp.zeros((1, 128), F32) if rest_row is None else got_ref[0, rest_row : rest_row + 1, :]
    for j in range(1, got_ref.shape[0]):
        total, lost = two_sum(total, got_ref[j, row : row + 1, :])
        rest = rest + lost
        if rest_row is not None:
            rest = rest + got_ref[j, rest_row : rest_row + 1, :]
    return total, rest


def gathered(tiles):
    total, rest = tiles[0][0:1], tiles[0][1:2]
    for tile in tiles[1:]:
        total, lost = two_sum(total, tile[0:1])
        rest = rest + (lost + tile[1:2])
    return two_sum(total, rest)


def pairs_of(total, rest, count):
    return [
        (jnp.broadcast_to(total[:, k : k + 1], (1, 128)), jnp.broadcast_to(rest[:, k : k + 1], (1, 128)))
        for k in range(count)
    ]


def form(table, left, weights):
    out = None
    for i, row in enumerate(left):
        for j, entry in enumerate(table[row]):
            factor = None
            for w in (weights[i], weights[j]):
                if w is not None:
                    factor = w if factor is None else pair_times(factor, w)
            term = entry if factor is None else pair_times(entry, factor)
            out = term if out is None else pair_add(out, term)
    return out[0] + out[1]


def tiled(row):
    return jnp.broadcast_to(row, (8, 128))[None]


def negated(pair):
    return -pair[0], -pair[1]


def third_body(*refs):
    k_ref, llow_ref, lhigh_ref, part_ref = refs[14:]
    early, right2, left, right = refs[1], refs[3], refs[8], refs[9]
    total, rest = gathered([early[32:40, :], left[18], right[18], right2[32:40, :]])
    part_ref[...] = jnp.concatenate([total, rest, jnp.zeros((6, 128), F32)], axis=0)
    for x, k, l in corrected(*received(refs[:10]), refs[10:14]):
        k_ref[x] = k
        put(llow_ref, lhigh_ref, x, l)


def fourth_body(*refs):
    rows, window = zip(*(received(refs[10 * i : 10 * i + 10]) for i in range(3)))
    rest = refs[30:34]
    parts, refs = refs[34:38], refs[38:]
    low_ref, high_ref, z_ref, m_ref, k_ref = refs[:5]
    zo_ref, wolow_ref, wohigh_ref, mo_ref, no_ref, xo_ref, ro_ref, po_ref, so_ref, qo_ref, to_ref = refs[5:16]
    keep_ref, dots_ref = refs[16:]
    sums = pairs_of(*gathered([part[...] for part in parts]), 6)
    table = [sums[0:2], sums[2:4], sums[4:6]]
    gamma0 = table[0][0][0]
    alpha0 = gamma0 / table[1][0][0]
    weights = (None, negated((alpha0, jnp.zeros_like(alpha0))))
    gamma1 = form(table, (0, 1), weights)
    delta1 = form(table, (1, 2), weights)
    beta1 = gamma1 / gamma0
    alpha1 = gamma1 / (delta1 - beta1 * gamma1 / alpha0)
    lane = lax.broadcasted_iota(jnp.int32, (1, 128), 1)
    keep_ref[...] = jnp.where(lane == 0, gamma1, jnp.where(lane == 1, alpha1, 0.0))
    alphas = [(tiled(alpha0), tiled(alpha1), tiled(beta1)), (alpha0, alpha1, beta1)]

    def turned(w, n, l, alpha0, alpha1, beta1):
        t = (n - alpha0 * l) + beta1 * n
        return (w - alpha0 * n) - alpha1 * t, t

    vectors = [turned(*(rows[i][x] for i in range(3)), *alphas[0])[0] for x in range(8)]
    window = [turned(*(window[i][y] for i in range(3)), *alphas[1])[0] for y in range(8)]
    alpha0, alpha1, beta1 = alphas[0]
    sums = [jnp.zeros((8, 128), F32)] * 15
    for x, m2, n2 in corrected(vectors, window, rest):
        w0, n0, l = (rows[i][x + 2][2:10] for i in range(3))
        z0, m0, k = z_ref[x], m_ref[x], k_ref[x]
        w2, t = turned(w0, n0, l, *alphas[0])
        z2, q = turned(z0, m0, k, *alphas[0])
        p, s = (z0 - alpha0 * m0) + beta1 * z0, (w0 - alpha0 * n0) + beta1 * w0
        r2 = (half(low_ref, high_ref, x) - alpha0 * w0) - alpha1 * s
        xo_ref[x] = alpha0 * z0 + alpha1 * p
        ro_ref[x], zo_ref[x] = r2, z2
        put(wolow_ref, wohigh_ref, x, w2)
        mo_ref[x], no_ref[x] = m2, n2
        po_ref[x], so_ref[x], qo_ref[x], to_ref[x] = p, s, q, t
        sums = [a + b for a, b in zip(sums, products((r2, w2, s, n2, t), (z2, m2, q)))]
    dots_ref[...] = dots_of(sums)


def spread_dots_body(dots_ref, send_ref):
    tile = jnp.concatenate([dots_ref[...], jnp.zeros((7, 128), F32)], axis=0)
    for j in range(send_ref.shape[0]):
        send_ref[j] = tile


def sum_dots_body(got_ref, send_ref):
    total, rest = total_of(got_ref, 0, None)
    tile = jnp.concatenate([total, rest, jnp.zeros((6, 128), F32)], axis=0)
    for j in range(send_ref.shape[0]):
        send_ref[j] = tile


def finish_body(got_ref, z_ref, wlow_ref, whigh_ref, m_ref, n_ref, x_ref, r_ref, p_ref, s_ref, q_ref, t_ref, keep_ref,
                xo_ref, ro_ref, xs_ref, rs_ref):
    sums = pairs_of(*two_sum(*total_of(got_ref, 0, 1)), 15)
    table = [sums[3 * k : 3 * k + 3] for k in range(5)]
    keep = keep_ref[...]
    gamma1 = jnp.broadcast_to(keep[:, 0:1], (1, 128))
    alpha1 = jnp.broadcast_to(keep[:, 1:2], (1, 128))
    gamma2 = table[0][0][0]
    beta2 = gamma2 / gamma1
    alpha2 = gamma2 / (table[1][0][0] - beta2 * gamma2 / alpha1)
    weights = (None, (-alpha2, jnp.zeros_like(alpha2)), two_product(-alpha2, beta2))
    gamma3 = form(table, (0, 1, 2), weights)
    delta3 = form(table, (1, 3, 4), weights)
    beta3 = gamma3 / gamma2
    alpha3 = gamma3 / (delta3 - beta3 * gamma3 / alpha2)
    alpha2, beta2, alpha3, beta3 = tiled(alpha2), tiled(beta2), tiled(alpha3), tiled(beta3)
    for x in range(4):
        z, w, q1, t1 = z_ref[x], half(wlow_ref, whigh_ref, x), q_ref[x], t_ref[x]
        p2, s2 = z + beta2 * p_ref[x], w + beta2 * s_ref[x]
        q2, t2 = m_ref[x] + beta2 * q1, n_ref[x] + beta2 * t1
        p3 = (z - alpha2 * q2) + beta3 * p2
        s3 = (w - alpha2 * t2) + beta3 * s2
        xs_ref[pl.ds(64 * x, 64), :] = ((x_ref[x] + alpha2 * p2) + alpha3 * p3).reshape(64, 128)
        rs_ref[pl.ds(64 * x, 64), :] = ((r_ref[x] - alpha2 * s2) - alpha3 * s3).reshape(64, 128)
    for x in range(4):
        for s in range(8):
            part = slice(s * 128, (s + 1) * 128)
            xo_ref[x, :, part] = xs_ref[pl.ds(64 * x + s, 8, stride=8), :]
            ro_ref[x, :, part] = rs_ref[pl.ds(64 * x + s, 8, stride=8), :]


def local(right_side, diagonal, aggregate_id, coarse_diag, coarse_link):
    count_x, count_y = lax.axis_size("px"), lax.axis_size("py")
    me = jnp.stack([lax.axis_index("px"), lax.axis_index("py"), count_x - 1, count_y - 1]).astype(jnp.int32)

    def both_ways(low, high, axis, far=1):
        count = lax.axis_size(axis)
        up = [(i, (i + far) % count) for i in range(count)]
        down = [(b, a) for a, b in up]
        return lax.ppermute(high, axis, up), lax.ppermute(low, axis, down)

    def gather(value, axis):
        return lax.all_to_all(value, axis, 0, 0)

    two, field = (2, 8, 8, 128), (4, 8, 8, 128)
    low, high = call(enter_body, [(256, 128)] * 2, right_side, diagonal, scalars=0)
    low, high = low.reshape(4, 8, 8, 128), high.reshape(4, 8, 8, 128)
    xlow, xhigh = both_ways(low, high, "px")
    olow, ohigh, coarse = call(
        enter_more_body, [(192, 128)] * 2 + [(16, 128)], aggregate_id, coarse_diag, coarse_link, low, scalars=0
    )
    olow, ohigh = olow.reshape(3, 8, 8, 128), ohigh.reshape(3, 8, 8, 128)
    first, last = call(pack_first_body, [(20, 8, 128)] * 2, low, high, xlow, xhigh, scalars=0)
    ylow, yhigh = both_ways(first, last, "py")
    inverse, = call(
        setup_body, [(8, 12, 8, 128)], me, low, high, xlow, xhigh, ylow, yhigh
    )
    mid, dots = (6, 10, 8, 128), (1, 128)
    smooth, remain, send, down, up = call(
        restrict_body, [mid, mid, (24, 128)] + [(27, 8, 128)] * 2,
        low, high, xlow, xhigh, ylow, yhigh, inverse, olow, ohigh, coarse, scalars=0,
    )
    below, above = both_ways(down, up, "px")
    below2, above2 = both_ways(send, send, "px", 2)
    scale, = call(scale_body, [(6, 10, 8, 128)], low, high, xlow, xhigh, ylow, yhigh, scalars=0)
    first, last, send = call(
        window_first_body, [(32, 8, 128)] * 2 + [(112, 128)],
        below2, below, send, above, above2, olow, ohigh, scalars=0,
    )
    left, right = both_ways(first, last, "py")
    left2, right2 = both_ways(send, send, "py", 2)
    coef, sums, offset = call(
        coarse_setup_body, [(7, 8, 16, 128), (8, 16, 128), (10, 14, 8, 128)],
        me, left2, left, send, right, right2, olow, ohigh, below, above,
    )
    fixed = (inverse, scale, offset)
    z, wlow, whigh = call(begin_body, [field, two, two], sums, coef, smooth, remain, *fixed, scalars=0)

    packed = [(18, 8, 128)] * 2 + [(32, 128)] * 2

    def beside_y(low, high, below, above, first, last, early, late):
        left, right = both_ways(first, last, "py")
        left2, right2 = both_ways(early, late, "py", 2)
        return left2, early, late, right2, low, high, below, above, left, right

    def exchanged(low, high):
        share, down, up = call(
            contribute_body, [(16, 128), (18, 8, 128), (18, 8, 128)], low, high, inverse, offset, scalars=0
        )
        below, above = both_ways(down, up, "px")
        below2, above2 = both_ways(share, share, "px", 2)
        below3, above3 = both_ways(share, share, "px", 3)
        outs = call(
            pack_body, packed, low, high, below3, below2, below, share, above, above2, above3, scalars=0
        )
        return beside_y(low, high, below, above, *outs)

    def exchanged_and_summed(low, high, sums):
        send, = call(
            contribute_and_sum_body, [(count_x, 24, 128)], low, high, inverse, offset, sums, scalars=0
        )
        below, above = (a.reshape(16, 8, 128) for a in both_ways(low, high, "px"))
        outs = call(
            pack_and_sum_body, [(19, 8, 128)] * 2 + [(40, 128)] * 2, me, low, high, below, above, gather(send, "px")
        )
        return beside_y(low, high, below, above, *outs)

    def summed(sums):
        send, = call(spread_dots_body, [(count_x, 8, 128)], sums, scalars=0)
        send, = call(sum_dots_body, [(count_y, 8, 128)], gather(send, "px"), scalars=0)
        return gather(send, "py")

    fixed = (coef, *fixed)
    first = exchanged(wlow, whigh)
    m, nlow, nhigh, sums = call(
        second_body, [field, two, two, dots], *first, *fixed, low, high, z, scalars=0
    )
    second = exchanged_and_summed(nlow, nhigh, sums)
    k, llow, lhigh, part = call(third_body, [field, two, two, (8, 128)], *second, *fixed, scalars=0)
    parts = (part, *both_ways(part, part, "py", 4), both_ways(part, part, "py", 8)[0])
    third = exchanged(llow, lhigh)
    z, wlow, whigh, m, n, x, r, p, s, q, t, keep, sums = call(
        fourth_body, [field, two, two] + [field] * 8 + [dots] * 2,
        *first, *second, *third, *fixed, *parts, low, high, z, m, k, scalars=0,
    )
    return tuple(call(
        finish_body, [right_side.shape] * 2,
        summed(sums), z, wlow, whigh, m, n, x, r, p, s, q, t, keep,
        scalars=0, scratch=[pltpu.VMEM((256, 128), F32)] * 2,
    ))


def solution(mesh):
    cells = P("px", "py", None)
    in_specs = (cells, cells, cells, cells, P(None, "px", "py", None))
    return jax.shard_map(local, mesh=mesh, in_specs=in_specs, out_specs=(cells, cells), check_vma=False)
```
